32 devices in a mesh: gx: 8 (over z, x), gy: 4 (over y, core).
Axes of the slice: x: 2, y: 2, z: 4, core: 2. Of those that a mesh axis runs over, the one named last changes fastest.
Arguments:
- state: float32 [9, 56, 8192], P(None, None, ('gx', 'gy')), may hold values from -6 to 6
- star: float32 [3, 9, 9, 8192], P(None, None, None, ('gx', 'gy')), may hold values from -1.5 to 1.5
- deriv: float32 [3, 56, 56], replicated, may hold values from -0.75 to 0.75
- trace_ops: float32 [4, 56, 21], replicated, may hold values from -0.75 to 0.75
- lift: float32 [4, 21, 56], replicated, may hold values from -1.25 to 1.25
- face_flux: float32 [4, 9, 9, 8192], P(None, None, None, ('gx', 'gy')), may hold values from -0.3 to 0.3
- orient: int32 [4, 8192], P(None, ('gx', 'gy')), may hold values from 0 to 2
- neighbours: int32 [4, 8192], P(None, ('gx', 'gy')), may hold values from 0 to 1536, as said below
- send_faces: int32 [8, 4, 4, 128], P('gx', 'gy'), may hold values from 0 to 1023, as said below
- sea_faces: int32 [4096], P(('gx', 'gy')), may hold values from 0 to 1023
- sea_owner: int32 [4096, 1], P(('gx', 'gy')), may hold values from 0 to 31; in each aligned block of 128 rows (0 to 127, 128 to 255, ...) at most 4 rows name the same one
- sea_blocks: int32 [4096], P(('gx', 'gy')), may hold values from 0 to 255
- sea_weights: float32 [21, 4096, 256], P(None, ('gx', 'gy')), may hold values from -0.6 to 0.6
- depth: float32 [2048, 1024], P('gx', 'gy'), may hold values from 1 to 3
- wet: int32 [2048, 1024], P('gx', 'gy'), may hold values 0 or 1
- sea_state: float32 [3, 2048, 1024], P(None, 'gx', 'gy'), may hold values from -0.6 to 0.6
Outputs:
- elastic: float32 [9, 56, 8192], P(None, None, ('gx', 'gy'))
- ocean: float32 [3, 2048, 1024], P(None, 'gx', 'gy')
The draws below stay inside these ranges and needn't reach their ends.
Inputs may be any that keep to these rules, and one draw needn't show every extreme that they name: `neighbours`: A code below 1024 names a face of the same device, paired both ways; 1024 + k * 128 + s names the face in slot s of the back-pointing list of the grid neighbour in direction k, which lists this face in its slot s; 1536 marks a face at the edge of the device grid. `send_faces`: local face codes; each face of a device stands in at most one of its lists, once. `sea_faces`: local face codes. `sea_owner`: the flat index of a device, gx index times the gy axis's length plus gy index; among the 128 rows of one device at most 4 name the same owner, and some owner is named 4 times.
All inputs are finite; a program needn't handle non-finite values. No bound on the sum of `wet` on one device may be relied on, other than what follows from the above.
Results may differ from the reference program's by a relative error of at most 0.0001.
Values sent between devices are 32-bit elements; how exact they have to be, the bound alone decides.
No kernel may reach another device: no remote copies, remote signals or barrier semaphores. Data moves between devices by JAX's collectives and lax.ppermute only.
A program may use at most 128 MiB of HBM per device.

```python
import math
import jax
import jax.numpy as jnp
import numpy as np
from jax import lax

VARS = 9
ORDER = 6
BASIS = 56
FACE_NODES = 21
EL_DEV = 256
SLOTS = 128
STEPS = 2
SEA_DEV = 128
CAP = 4
BS = 16
TX = 256
TY = 256
TAPS = 65
HALF = 32
CELLS = 256
BLOCKS = 256
ELEMENTS = 8192
SEA_ALL = 4096
RX = 2048
RY = 1024
N_GX = 8
N_GY = 4
DEVICES = 32


def link_table(key):
    base = jax.random.fold_in(key, 11)
    keys = jax.random.split(base, N_GX * N_GY)
    return jax.vmap(lambda single: jax.random.permutation(single, 4 * EL_DEV))(keys).astype(jnp.int32)


def draw_send_faces(key, part):
    perms = link_table(key)
    return perms[:, :4 * SLOTS].reshape(N_GX, N_GY, 4, SLOTS).astype(jnp.int32)


def draw_neighbours(key, part):
    perms = link_table(key)
    devs = N_GX * N_GY
    places = jnp.arange(4 * EL_DEV, dtype=jnp.int32)
    device_ids = jnp.arange(devs, dtype=jnp.int32)
    row_x = device_ids // N_GY
    row_y = device_ids % N_GY
    exists = jnp.stack([row_x > 0, row_x < N_GX - 1, row_y > 0, row_y < N_GY - 1], axis=1)
    direction = jnp.minimum(places // SLOTS, 3)
    present = exists[:, direction]
    cross_code = jnp.where(present, 4 * EL_DEV + places[None, :], 4 * EL_DEV + 4 * SLOTS)
    rest = jnp.maximum(places - 4 * SLOTS, 0)
    mate = jnp.minimum(4 * SLOTS + jnp.bitwise_xor(rest, 1), 4 * EL_DEV - 1)
    local_code = perms[:, mate]
    values = jnp.where((places < 4 * SLOTS)[None, :], cross_code, local_code).astype(jnp.int32)
    table = jnp.zeros((devs, 4 * EL_DEV), jnp.int32)
    table = table.at[device_ids[:, None], perms].set(values)
    return table.reshape(devs, 4, EL_DEV).transpose(1, 0, 2).reshape(4, devs * EL_DEV)


def touch_ends(values, key, least, largest):
    index_at = [jax.random.randint(jax.random.fold_in(key, axis), (), 0, length) for axis, length in enumerate(values.shape)]
    main_axis = values.shape.index(max(values.shape))
    next_to = index_at[:main_axis] + [(index_at[main_axis] + 1) % values.shape[main_axis]] + index_at[main_axis + 1:]
    return values.at[tuple(index_at)].set(least).at[tuple(next_to)].set(largest)


def block_scale(rng, extent, shards, least, top_value):
    def one(dim, shards_of):
        heights = jax.random.uniform(jax.random.fold_in(jax.random.fold_in(rng, 6), dim), (shards_of,), jnp.float32, least / len(shards), top_value / len(shards))
        return jnp.repeat(jnp.exp(heights), extent[dim] // shards_of).reshape((-1,) + (1,) * (len(extent) - dim - 1))

    gain = one(*shards[0])
    for cut in shards[1:]:
        gain = gain * one(*cut)
    return gain


def assign_block(own_key, own, number, rows, count, top, most, slope):
    sequence = jax.random.permutation(own_key, count)
    packed, usual = portions_of(count, rows * top, most, slope, True), portions_of(count, rows * top, most, slope, False)
    places = jnp.arange(count)

    def named(sizes, turn):
        used = int((sizes > 0).sum())
        fixed = max(1, used // 4)
        passed = fixed + (places - fixed + turn * (used - fixed)) % max(1, count - fixed)
        return jnp.zeros((count,), jnp.int32).at[sequence[jnp.where(places < fixed, places, passed)]].set(jnp.asarray(sizes, jnp.int32))

    sizes = jnp.where(number % 4 == 0, named(packed, number // 4), named(usual, number - number // 4 - 1))
    mixed = jax.random.permutation(jax.random.fold_in(own, 3), count)
    source_of, sink = mixed[0:count // 2 * 2:2], mixed[1:count // 2 * 2:2]
    margin = jnp.minimum(sizes[source_of] - 1, most - sizes[sink]) // 2
    margin = jnp.where((source_of == sequence[0]) | (sink == sequence[0]) | (sizes[sink] == 0), 0, jnp.maximum(margin, 0))
    passed = jax.random.randint(jax.random.fold_in(own, 4), (count // 2,), 0, 1 << 20) % (margin + 1)
    sizes = sizes.at[source_of].add(-passed).at[sink].add(passed)
    members = jnp.searchsorted(jnp.cumsum(sizes), jnp.arange(rows * top), side="right").astype(jnp.int32)
    table = members.reshape(top, rows).T
    table = table[jax.random.permutation(jax.random.fold_in(own, 1), rows)]
    turn = jax.random.randint(jax.random.fold_in(own, 2), (rows, 1), 0, top)
    return jnp.take_along_axis(table, (jnp.arange(top)[None, :] + turn) % top, axis=1)


def portions_of(count, total, most, lean, full):
    portions = [(1 << 20) // math.isqrt(rank ** lean) + 1 for rank in range(1, count + 1)]
    largest = most if full else min(most, max(-(-total // count), total * portions[0] // sum(portions)))
    least = 1 if total - largest >= count - 1 else 0
    counts, spare = [largest] + [least] * (count - 1), total - largest - least * (count - 1)
    while spare > 0:
        free = [i for i in range(1, count) if counts[i] < largest] or [i for i in range(1, count) if counts[i] < most]
        whole, left = sum([portions[i] for i in free]), spare
        for i in free:
            addition = min(most - counts[i], max(1, left * portions[i] // whole), spare)
            counts[i] = counts[i] + addition
            spare = spare - addition
    return np.array(counts)


def centred(rng, extent, scale, most, cuts=(), kind=jnp.bfloat16):
    values = jax.random.normal(rng, extent, jnp.float32) * scale
    if len(cuts) > 0:
        values = block_scale(rng, extent, cuts, -0.22, 0.18) * values
    return jnp.clip(values, min=-most, max=most).astype(kind)


def setup_inputs(seed: int = 0) -> dict:
    seeds = jax.random.split(jax.random.key(seed), 17)
    state = centred(seeds[0], (VARS, BASIS, ELEMENTS), 1.0, 6.0, ((2, 32),), jnp.float32)
    star = centred(seeds[1], (3, VARS, VARS, ELEMENTS), 0.25, 1.5, ((3, 32),), jnp.float32)
    deriv = centred(seeds[2], (3, BASIS, BASIS), BASIS ** -0.5, 0.75, (), jnp.float32)
    trace_ops = centred(seeds[3], (4, BASIS, FACE_NODES), BASIS ** -0.5, 0.75, (), jnp.float32)
    lift = centred(seeds[4], (4, FACE_NODES, BASIS), FACE_NODES ** -0.5, 1.25, (), jnp.float32)
    face_flux = centred(seeds[5], (4, VARS, VARS, ELEMENTS), 0.05, 0.3, ((3, 32),), jnp.float32)
    orient = touch_ends(jax.random.randint(seeds[6], (4, ELEMENTS), 0, 3), jax.random.fold_in(seeds[6], 1), 0, 2).astype(jnp.int32)
    neighbours = draw_neighbours(jax.random.fold_in(seeds[16], 71), 0)
    send_faces = draw_send_faces(jax.random.fold_in(seeds[16], 71), 0)
    sea_faces = touch_ends(jax.random.randint(seeds[9], (SEA_ALL,), 0, 4 * EL_DEV), jax.random.fold_in(seeds[9], 1), 0, (4 * EL_DEV) - 1).astype(jnp.int32)
    sea_owner_keys = jax.random.split(jax.random.fold_in(seeds[10], 1), SEA_ALL // SEA_DEV)
    sea_owner_turns = jax.random.permutation(jax.random.fold_in(seeds[10], 3), SEA_ALL // SEA_DEV)
    sea_owner = jax.vmap(lambda own, number: assign_block(jax.random.fold_in(seeds[10], 2), own, number, SEA_DEV, DEVICES, 1, CAP, 2))(sea_owner_keys, sea_owner_turns).reshape((SEA_ALL, 1))
    sea_blocks = touch_ends(jax.random.randint(seeds[11], (SEA_ALL,), 0, BLOCKS), jax.random.fold_in(seeds[11], 1), 0, BLOCKS - 1).astype(jnp.int32)
    sea_weights = centred(seeds[12], (FACE_NODES, SEA_ALL, CELLS), 0.1, 0.6, ((1, 32),), jnp.float32)
    depth = jnp.clip(1.0 + 2.0 * jax.random.uniform(seeds[13], (RX, RY), jnp.float32) ** block_scale(seeds[13], (RX, RY), ((0, 8), (1, 4)), -0.2, 0.2), 1.0, 3.0)
    wet = touch_ends((jax.random.randint(seeds[14], (RX, RY), 0, 4) < 3).astype(jnp.int32), jax.random.fold_in(seeds[14], 1), 0, 1)
    sea_state = centred(seeds[15], (3, RX, RY), 0.1, 0.6, ((1, 8), (2, 4)), jnp.float32)
    return dict(state=state, star=star, deriv=deriv, trace_ops=trace_ops, lift=lift, face_flux=face_flux, orient=orient, neighbours=neighbours, send_faces=send_faces, sea_faces=sea_faces, sea_owner=sea_owner, sea_blocks=sea_blocks, sea_weights=sea_weights, depth=depth, wet=wet, sea_state=sea_state)


spread_cells = 8.0
gravity = 1.0
courant = 0.25
best = lax.Precision.HIGHEST


def node_turns():
    upper = ORDER - 1
    nodes = [(i, j) for i in range(upper + 1) for j in range(upper + 1 - i)]
    once = [nodes.index((pair[1], upper - pair[0] - pair[1])) for pair in nodes]
    twice = [once[once[number]] for number in range(len(nodes))]
    return np.array(once), np.array(twice)


def filter_taps():
    offsets = jnp.arange(-HALF, HALF + 1).astype(jnp.float32)
    scaled = math.pi * offsets / (2.0 * spread_cells)
    raw = 2.0 / (jnp.exp(scaled) + jnp.exp(-scaled))
    return raw / jnp.sum(raw)


def derive(field, star, deriv):
    total = jnp.zeros(field.shape, jnp.float32)
    for direction in range(3):
        moved = jnp.einsum("vbe,bc->vce", field, deriv[direction], precision=best)
        total = total + jnp.einsum("uve,vce->uce", star[direction], moved, precision=best)
    return total


def predict(field, star, deriv):
    term = field
    integ = field
    for order_k in range(1, ORDER):
        term = -derive(term, star, deriv)
        integ = integ + term / float(math.factorial(order_k + 1))
    return integ


def turn_nodes(partner, orient):
    once, twice = node_turns()
    turned = jnp.where(orient == 1, partner[:, once], partner)
    return jnp.where(orient == 2, partner[:, twice], turned)


def settle(field, integ, own_faces, partner, orient, face_flux, lift, star, deriv):
    jump = own_faces - turn_nodes(partner, orient)
    flux = jnp.einsum("fuve,vnfe->unfe", face_flux, jump, precision=best)
    surface = jnp.einsum("unfe,fnb->ube", flux, lift, precision=best)
    return field - derive(integ, star, deriv) - surface


def advance(fields, wide, wet_field):
    plus_x = wide[:, 2:, 1:-1]
    minus_x = wide[:, :-2, 1:-1]
    plus_y = wide[:, 1:-1, 2:]
    minus_y = wide[:, 1:-1, :-2]
    mean = 0.25 * (plus_x + minus_x + plus_y + minus_y)
    east_speed = fields[1]
    north_speed = fields[2]
    factor = 0.5 * courant
    eta_new = mean[0] - factor * ((plus_x[3] - minus_x[3]) + (plus_y[4] - minus_y[4]))
    east_new = mean[1] - factor * (east_speed * (plus_x[1] - minus_x[1]) + north_speed * (plus_y[1] - minus_y[1]) + gravity * (plus_x[0] - minus_x[0]))
    north_new = mean[2] - factor * (east_speed * (plus_x[2] - minus_x[2]) + north_speed * (plus_y[2] - minus_y[2]) + gravity * (plus_y[0] - minus_y[0]))
    return eta_new * wet_field, east_new * wet_field, north_new * wet_field


def reference(state, star, deriv, trace_ops, lift, face_flux, orient, neighbours, send_faces, sea_faces, sea_owner, sea_blocks, sea_weights, depth, wet, sea_state):
    devs = N_GX * N_GY
    width = VARS * FACE_NODES
    limit = 4 * EL_DEV + 4 * SLOTS
    lists = send_faces.reshape(devs, 4 * SLOTS)
    codes = neighbours.reshape(4, devs, EL_DEV).transpose(1, 0, 2).reshape(devs, 4 * EL_DEV)
    sea_lists = sea_faces.reshape(devs, SEA_DEV)
    field = state
    vertical = []
    for turn in range(STEPS):
        integ = predict(field, star, deriv)
        own_faces = jnp.einsum("vbe,fbn->vnfe", integ, trace_ops, precision=best)
        local = own_faces.reshape(VARS, FACE_NODES, 4, devs, EL_DEV).transpose(3, 0, 1, 2, 4).reshape(devs, width, 4 * EL_DEV)
        sent = jax.vmap(lambda table, picks: table[:, picks])(local, lists).reshape(N_GX, N_GY, width, 4, SLOTS)
        blank_x = jnp.zeros((1, N_GY, width, SLOTS), jnp.float32)
        blank_y = jnp.zeros((N_GX, 1, width, SLOTS), jnp.float32)
        from_low_x = jnp.concatenate([blank_x, sent[:-1, :, :, 1]], 0)
        from_high_x = jnp.concatenate([sent[1:, :, :, 0], blank_x], 0)
        from_low_y = jnp.concatenate([blank_y, sent[:, :-1, :, 3]], 1)
        from_high_y = jnp.concatenate([sent[:, 1:, :, 2], blank_y], 1)
        arrived = jnp.stack([from_low_x, from_high_x, from_low_y, from_high_y], 3).reshape(devs, width, 4 * SLOTS)
        pool = jnp.concatenate([local, arrived], 2)
        picked = jax.vmap(lambda table, picks: table[:, jnp.minimum(picks, limit - 1)])(pool, codes)
        picked = jnp.where(codes[:, None, :] < limit, picked, 0.0)
        partner = picked.reshape(devs, VARS, FACE_NODES, 4, EL_DEV).transpose(1, 2, 3, 0, 4).reshape(VARS, FACE_NODES, 4, ELEMENTS)
        upward = local[:, 2 * FACE_NODES:3 * FACE_NODES, :]
        vertical.append(jax.vmap(lambda table, picks: table[:, picks])(upward, sea_lists))
        field = settle(field, integ, own_faces, partner, orient, face_flux, lift, star, deriv)
    frames = []
    running = jnp.zeros(vertical[0].shape, jnp.float32)
    for piece in vertical:
        running = running + piece
        frames.append(running)
    disp = jnp.stack(frames)
    weights = sea_weights.reshape(FACE_NODES, devs, SEA_DEV, CELLS)
    rows = jnp.einsum("sdnr,ndrc->drsc", disp, weights, precision=best).reshape(SEA_ALL, STEPS * CELLS)
    segment = sea_owner[:, 0] * BLOCKS + sea_blocks
    summed = jax.ops.segment_sum(rows, segment, num_segments=devs * BLOCKS)
    uplift = summed.reshape(N_GX, N_GY, TX // BS, TY // BS, STEPS, BS, BS).transpose(4, 0, 2, 5, 1, 3, 6).reshape(STEPS, RX, RY)
    taps = filter_taps()
    padded = jnp.pad(uplift, ((0, 0), (HALF, HALF), (0, 0)))
    along_x = jnp.zeros(uplift.shape, jnp.float32)
    for offset in range(TAPS):
        along_x = along_x + taps[offset] * padded[:, offset:offset + RX, :]
    padded = jnp.pad(along_x, ((0, 0), (0, 0), (HALF, HALF)))
    filtered = jnp.zeros(uplift.shape, jnp.float32)
    for offset in range(TAPS):
        filtered = filtered + taps[offset] * padded[:, :, offset:offset + RY]
    wet_field = wet.astype(jnp.float32)
    eta, east_speed, north_speed = sea_state[0], sea_state[1], sea_state[2]
    for turn in range(STEPS):
        force = filtered[0] if turn == 0 else filtered[turn] - filtered[turn - 1]
        eta = eta + wet_field * force
        column = depth + eta
        fields = jnp.stack([eta, east_speed, north_speed, column * east_speed, column * north_speed])
        wide = jnp.pad(fields, ((0, 0), (1, 1), (1, 1)))
        eta, east_speed, north_speed = advance(fields, wide, wet_field)
    return field, jnp.stack([eta, east_speed, north_speed])
```

```python
import math

import jax
import jax.numpy as jnp
import numpy as np
from jax import lax
from jax.experimental import pallas as pl
from jax.experimental.pallas import tpu as pltpu
from jax.sharding import PartitionSpec as P

ORDER = 6
STEPS = 2
BS = 16
HALF = 32
SPREAD = 8.0
COURANT = 0.25
LANES = 128
HALO_X = 40
HALO_Y = 34
EDGE = 8
F32 = jnp.float32
BF16 = jnp.bfloat16


def node_turns():
    upper = ORDER - 1
    nodes = [(i, j) for i in range(upper + 1) for j in range(upper + 1 - i)]
    once = [nodes.index((pair[1], upper - pair[0] - pair[1])) for pair in nodes]
    twice = [once[once[number]] for number in range(len(nodes))]
    return [list(range(len(nodes))), once, twice]


def pad8(n):
    return -(-n // 8) * 8


def band(out_at, in_at):
    k = np.arange(-HALF, HALF + 1)
    raw = 1.0 / np.cosh(math.pi * k / (2.0 * SPREAD))
    raw = raw / raw.sum()
    diff = in_at[None, :] - out_at[:, None]
    w = np.where(np.abs(diff) <= HALF, raw[np.clip(diff + HALF, 0, 2 * HALF)], 0.0)
    w = w.astype(np.float32)
    hi = w.astype(jnp.bfloat16)
    lo = (w - hi.astype(np.float32)).astype(jnp.bfloat16)
    return hi, lo


def split(x):
    hi = x.astype(BF16)
    lo = (x - hi.astype(F32)).astype(BF16)
    return hi, lo


def mm(a, b):
    return lax.dot_general(a, b, (((1,), (0,)), ((), ())), preferred_element_type=F32)


def mm_tn(a, b):
    return lax.dot_general(a, b, (((0,), (0,)), ((), ())), preferred_element_type=F32)


def mm_nt(a, b):
    return lax.dot_general(a, b, (((1,), (1,)), ((), ())), preferred_element_type=F32)


def iota(shape, dim):
    return lax.broadcasted_iota(jnp.int32, shape, dim)


def hot(mask):
    return jnp.where(mask, 1.0, 0.0).astype(BF16)


def call(body, outs, scratch, *args, name):
    flops = 2 * 10**8
    return pl.pallas_call(
        body,
        out_shape=[jax.ShapeDtypeStruct(s, d) for s, d in outs],
        scratch_shapes=[pltpu.VMEM(s, d) for s, d in scratch],
        compiler_params=pltpu.CompilerParams(vmem_limit_bytes=56 * 2**20),
        name=name,
    )(*args)


def slots_of(basis):
    kb = -(-basis // 16) * 16
    row, col = iota((basis, 3 * kb), 0), iota((basis, 3 * kb), 1)
    return hot((col == row) | (col == kb + row)), hot(col == 2 * kb + row)


def prep_deriv(deriv_ref, w_ref):
    basis = deriv_ref.shape[1]
    sel_hi, sel_lo = slots_of(basis)
    parts = []
    for d in range(3):
        hi, lo = split(deriv_ref[d])
        parts.append(mm_tn(hi, sel_hi) + mm_tn(lo, sel_lo))
    w_ref[...] = jnp.concatenate(parts, axis=0).astype(BF16)


def prep_trace(trace_ref, place_ref, wt_ref):
    basis = trace_ref.shape[1]
    sel_hi, sel_lo = slots_of(basis)
    all_hi, all_lo = 0.0, 0.0
    for f in range(4):
        hi, lo = split(trace_ref[f])
        all_hi = all_hi + mm(hi, place_ref[f])
        all_lo = all_lo + mm(lo, place_ref[f])
    both = mm_tn(all_hi.astype(BF16), sel_hi) + mm_tn(all_lo.astype(BF16), sel_lo)
    wt_ref[...] = both.astype(BF16)


def prep_lift(lift_ref, wl_ref):
    nodes = lift_ref.shape[1]
    np_ = pad8(nodes)
    row, col = iota((nodes, 8 * np_), 0), iota((nodes, 8 * np_), 1)
    top, low = 0.0, 0.0
    for f in range(4):
        sel = hot((col == f * np_ + row) | (col == (4 + f) * np_ + row))
        hi, lo = split(lift_ref[f])
        top = top + mm_tn(hi, sel)
        low = low + mm_tn(lo, sel)
    wl_ref[...] = jnp.concatenate([top, low], axis=0).astype(BF16)


def stacked(x):
    rows = x.shape[0]
    pad = -(-rows // 16) * 16 - rows
    if pad:
        x = jnp.concatenate([x, jnp.zeros((pad, x.shape[1]), F32)], axis=0)
    hi, lo = split(x)
    return jnp.concatenate([hi, lo, hi], axis=0)


def derive(src_ref, star_ref, w_ref, moved_ref, emit):
    variables, basis, elems = src_ref.shape
    for v in range(variables):
        moved_ref[v] = mm(w_ref[...], stacked(src_ref[v]))
    group = 3

    def body(g, carry):
        for h in range(elems // LANES):
            at = slice(h * LANES, (h + 1) * LANES)
            acc = [jnp.zeros((basis, LANES), F32) for _ in range(group)]
            for v in range(variables):
                for d in range(3):
                    m = moved_ref[v, d * basis : (d + 1) * basis, at]
                    for i in range(group):
                        acc[i] = acc[i] + star_ref[d, g * group + i, v : v + 1, at] * m
            for i in range(group):
                emit(g * group + i, at, acc[i])
        return carry

    lax.fori_loop(0, variables // group, body, 0)


def predict(field_ref, star_ref, w_ref, moved_ref, term_ref, integ_ref):
    term_ref[...] = field_ref[...]
    integ_ref[...] = field_ref[...]

    def body(k, carry):
        scale = F32(-1.0 / ORDER)
        for o in range(1, ORDER - 1):
            scale = jnp.where(k == o, F32(-1.0 / (o + 1)), scale)

        def emit(u, at, acc):
            value = acc * scale
            term_ref[u, :, at] = value
            integ_ref[u, :, at] = integ_ref[u, :, at] + value

        derive(term_ref, star_ref, w_ref, moved_ref, emit)
        return carry

    lax.fori_loop(1, ORDER, body, 0)


def traces(integ_ref, wt_ref, own_refs):
    variables, basis, elems = integ_ref.shape
    np_ = wt_ref.shape[0] // 12
    for v in range(variables):
        t = mm(wt_ref[...], stacked(integ_ref[v]))
        for r in range(3):
            for f in range(4):
                own_refs[r][v * np_ : (v + 1) * np_, f * elems : (f + 1) * elems] = t[
                    (r * 4 + f) * np_ : (r * 4 + f + 1) * np_
                ]
    rows = own_refs[0].shape[0]
    for r in range(3):
        if rows > variables * np_:
            own_refs[r][variables * np_ :, :] = jnp.zeros(
                (rows - variables * np_, 4 * elems), F32
            )


def send_gather(own_ref, send_ref, left_ref, outs):
    rows, faces = own_ref.shape
    hi, lo = split(own_ref[...])
    left_ref[0:rows] = hi
    left_ref[rows : 2 * rows] = lo
    slots = send_ref.shape[3]
    for k in range(0, 4, 2):
        picks = jnp.concatenate([send_ref[0, 0, k : k + 1], send_ref[0, 0, k + 1 : k + 2]], axis=1)
        res = mm(left_ref[...], hot(iota((faces, 2 * slots), 0) == picks))
        res = res[:rows] + res[rows:]
        outs[k][...] = res[:, :slots]
        outs[k + 1][...] = res[:, slots:]


def row_of(ref):
    return jnp.concatenate([ref[f : f + 1, :] for f in range(ref.shape[0])], axis=1)


def local_jump(own_refs, source_turn, codes, left_ref, jump_ref):
    rows, faces = own_refs[0].shape
    width = faces // 4
    value = jnp.where(
        source_turn == 1.0,
        own_refs[1][...],
        jnp.where(source_turn == 2.0, own_refs[2][...], own_refs[0][...]),
    )
    hi, lo = split(value)
    left_ref[0:rows] = hi
    left_ref[rows : 2 * rows] = lo
    for q in range(4):
        at = slice(q * width, (q + 1) * width)
        res = mm(left_ref[...], hot(iota((faces, width), 0) == codes[:, at]))
        jump_ref[:, at] = own_refs[0][:, at] - (res[:rows] + res[rows:])


def surface(arrived, slot_turn, codes, jump_ref, flux_m_ref, perm_ref, wl_ref, base_ref, scratch, out_ref):
    left_ref, part_ref, flux_ref = scratch
    rows, faces = jump_ref.shape
    variables, basis, elems = base_ref.shape
    value = jnp.concatenate(arrived, axis=1)
    slots = value.shape[1]
    hi, lo = split(value)
    both = jnp.concatenate([hi, lo], axis=1)
    turned = mm(perm_ref[...], both)
    turn = jnp.concatenate([slot_turn, slot_turn], axis=1)
    chosen = jnp.where(
        turn == 1.0, turned[:rows], jnp.where(turn == 2.0, turned[rows:], both.astype(F32))
    ).astype(BF16)
    left_ref[0:rows] = chosen[:, :slots]
    left_ref[rows : 2 * rows] = chosen[:, slots:]
    for q in range(4):
        at = slice(q * elems, (q + 1) * elems)
        res = mm(left_ref[...], hot(iota((slots, elems), 0) + faces == codes[:, at]))
        part_ref[:, at] = jump_ref[:, at] - (res[:rows] + res[rows:])
    np_ = flux_ref.shape[1] // 4

    def body(f, carry):
        for h in range(elems // LANES):
            here = slice(h * LANES, (h + 1) * LANES)
            wide = pl.ds(pl.multiple_of(f * elems + h * LANES, LANES), LANES)
            jumps = [part_ref[v * np_ : (v + 1) * np_, wide] for v in range(variables)]
            for u in range(variables):
                acc = flux_m_ref[f, u, 0:1, here] * jumps[0]
                for v in range(1, variables):
                    acc = acc + flux_m_ref[f, u, v : v + 1, here] * jumps[v]
                flux_ref[u, pl.ds(pl.multiple_of(f * np_, 8), np_), here] = acc
        return carry

    lax.fori_loop(0, 4, body, 0)
    for u in range(variables):
        hi, lo = split(flux_ref[u])
        res = mm(wl_ref[...], jnp.concatenate([hi, lo], axis=0))
        out_ref[u] = base_ref[u] - (res[:basis] + res[basis:])


def first_kernel(
    state_ref, star_ref, deriv_ref, trace_ref, place_ref, send_ref,
    w_ref, wt_ref, integ_ref, own0, own1, own2, o0, o1, o2, o3,
    moved_ref, term_ref, left_ref,
):
    prep_deriv(deriv_ref, w_ref)
    prep_trace(trace_ref, place_ref, wt_ref)
    predict(state_ref, star_ref, w_ref, moved_ref, term_ref, integ_ref)
    traces(integ_ref, wt_ref, (own0, own1, own2))
    send_gather(own0, send_ref, left_ref, (o0, o1, o2, o3))


def local_first_kernel(
    own0, own1, own2, codes_ref, orient_ref, lift_ref, field_ref, integ_ref, star_ref, w_ref,
    sea_ref, depth_ref, wet_ref,
    jump_ref, base_ref, turn_ref, slot_ref, wl_ref, up_ref, down_ref,
    left_ref, moved_ref,
):
    prep_lift(lift_ref, wl_ref)
    codes = row_of(codes_ref)
    faces = codes.shape[1]
    slots = slot_ref.shape[1]
    turns = jnp.broadcast_to(row_of(orient_ref).astype(F32), (16, faces)).astype(BF16)
    width = faces // 4
    for q in range(4):
        at = slice(q * width, (q + 1) * width)
        turn_ref[:, at] = mm(turns, hot(iota((faces, width), 0) == codes[:, at]))[0:8]
    for q in range(slots // LANES):
        at = slice(q * LANES, (q + 1) * LANES)
        wanted = iota((LANES, faces), 0) + (faces + q * LANES)
        slot_ref[:, at] = mm_nt(turns, hot(wanted == codes))[0:8]
    local_jump((own0, own1, own2), turn_ref[0:1, :], codes, left_ref, jump_ref)

    def emit(u, at, acc):
        base_ref[u, :, at] = field_ref[u, :, at] - acc

    derive(integ_ref, star_ref, w_ref, moved_ref, emit)
    rows = depth_ref.shape[0]
    for j in range(5):
        ref = sea_ref.at[j] if j < 3 else (depth_ref if j == 3 else wet_ref)
        up_ref[j * EDGE : (j + 1) * EDGE] = ref[rows - EDGE : rows, :].astype(F32)
        down_ref[j * EDGE : (j + 1) * EDGE] = ref[0:EDGE, :].astype(F32)


def second_kernel(
    a0, a1, a2, a3, slot_ref, codes_ref, jump_ref, flux_m_ref, perm_ref, wl_ref, base_ref,
    star_ref, w_ref, wt_ref, send_ref,
    field_ref, integ_ref, own0, own1, own2, o0, o1, o2, o3,
    arr_left_ref, part_ref, flux_ref, moved_ref, term_ref, left_ref,
):
    surface(
        [a0[...], a1[...], a2[...], a3[...]], slot_ref[0:1, :], row_of(codes_ref), jump_ref,
        flux_m_ref, perm_ref, wl_ref, base_ref, (arr_left_ref, part_ref, flux_ref), field_ref,
    )
    predict(field_ref, star_ref, w_ref, moved_ref, term_ref, integ_ref)
    traces(integ_ref, wt_ref, (own0, own1, own2))
    send_gather(own0, send_ref, left_ref, (o0, o1, o2, o3))


def local_second_kernel(
    own0, own1, own2, codes_ref, turn_ref, field_ref, integ_ref, star_ref, w_ref,
    jump_ref, base_ref, left_ref, moved_ref,
):
    local_jump((own0, own1, own2), turn_ref[0:1, :], row_of(codes_ref), left_ref, jump_ref)

    def emit(u, at, acc):
        base_ref[u, :, at] = field_ref[u, :, at] - acc

    derive(integ_ref, star_ref, w_ref, moved_ref, emit)


def last_kernel(
    x_low, x_high, y_low, y_high, slot_ref, codes_ref, jump_ref, flux_m_ref, perm_ref, wl_ref,
    base_ref, field_ref, arr_left_ref, part_ref, flux_ref,
):
    rows = jump_ref.shape[0]
    half = rows // 2

    def faces_x(ref):
        low = ref.shape[0] - half
        return jnp.concatenate([ref[low:, :LANES], ref[low:, LANES:]], axis=0)

    def faces_y(ref):
        return ref[ref.shape[0] - rows :, :]

    surface(
        [faces_x(x_low), faces_x(x_high), faces_y(y_low), faces_y(y_high)],
        slot_ref[0:1, :], row_of(codes_ref), jump_ref, flux_m_ref, perm_ref, wl_ref, base_ref,
        (arr_left_ref, part_ref, flux_ref), field_ref,
    )


def project_kernel(capacity, nodes, own_a, own_b, faces_ref, owner_ref, blocks_ref, weights_ref, pay_ref, disp_ref, rows_ref):
    np_ = pad8(nodes)
    faces = own_a.shape[1]
    sea_rows, cells = weights_ref.shape[1:]
    at = slice(2 * np_, 3 * np_)
    both = jnp.concatenate([own_a[at, :], own_b[at, :]], axis=0)
    hi, lo = split(both)
    picks = hot(iota((faces, sea_rows), 0) == faces_ref[...])
    disp = mm(jnp.concatenate([hi, lo], axis=0), picks)
    disp = disp[: 2 * np_] + disp[2 * np_ :]
    disp = jnp.concatenate([disp, jnp.zeros((LANES - 2 * np_, sea_rows), F32)], axis=0)
    disp_ref[...] = disp.T
    owner = jnp.broadcast_to(owner_ref[...].astype(F32), (sea_rows, sea_rows))
    across = owner.T
    earlier = iota((sea_rows, sea_rows), 0) < iota((sea_rows, sea_rows), 1)
    rank = jnp.sum(jnp.where((owner == across) & earlier, 1.0, 0.0), axis=0, keepdims=True)
    place = (across[0:1, :] * float(capacity) + rank).astype(jnp.int32)
    total = pay_ref.shape[0]
    put = hot(iota((total, sea_rows), 0) == place)
    chunk = 32

    def body(c, carry):
        here = pl.ds(pl.multiple_of(c * chunk, chunk), chunk)
        cols = disp_ref[here, :]
        for t in range(STEPS):
            acc = cols[:, t * np_ : t * np_ + 1] * weights_ref[0, here, :]
            for n in range(1, nodes):
                acc = acc + cols[:, t * np_ + n : t * np_ + n + 1] * weights_ref[n, here, :]
            rows_ref[t, here, :] = acc
        return carry

    lax.fori_loop(0, sea_rows // chunk, body, 0)
    twice = jnp.concatenate([put, put], axis=1)
    for t in range(STEPS):
        hi, lo = split(rows_ref[t])
        pay_ref[:, t * cells : (t + 1) * cells] = mm(twice, jnp.concatenate([hi, lo], axis=0))
    labels = jnp.broadcast_to(blocks_ref[...].astype(F32), (LANES, sea_rows)).astype(BF16)
    pay_ref[:, STEPS * cells :] = mm_nt(put, labels)


def raster_kernel(got_ref, sx_up, sx_down, o0, o1, uplift_ref, up_ref, down_ref):
    total = got_ref.shape[0]
    tile_x, tile_y = uplift_ref.shape[1:]
    across = tile_y // BS
    cells = BS * BS
    blocks = (tile_x // BS) * across
    labels = got_ref[:, STEPS * cells :].T
    pick = hot(iota((blocks, total), 0) == labels[0:1, :].astype(jnp.int32))
    pick = jnp.concatenate([pick, pick], axis=1)
    by = iota((blocks, cells), 0) % across
    cx = iota((blocks, cells), 1) // BS
    for t in range(STEPS):
        hi, lo = split(got_ref[:, t * cells : (t + 1) * cells])
        x = mm(pick, jnp.concatenate([hi, lo], axis=0))
        step = 1
        while step < BS:
            from_above = pltpu.roll(pltpu.roll(x, blocks - step, 0), BS * step, 1)
            from_below = pltpu.roll(pltpu.roll(x, step, 0), cells - BS * step, 1)
            low_row = (by & step) == 0
            low_col = (cx & step) == 0
            x = jnp.where(low_row == low_col, x, jnp.where(low_row, from_above, from_below))
            step *= 2
        uplift_ref[t] = x
        up_ref[t * HALO_X : (t + 1) * HALO_X] = x[tile_x - HALO_X :, :]
        down_ref[t * HALO_X : (t + 1) * HALO_X] = x[:HALO_X, :]
    low = STEPS * HALO_X
    high = low + 5 * EDGE
    up_ref[low:high] = sx_up[...]
    down_ref[low:high] = sx_down[...]
    half = o0.shape[0] // 2
    for ref, src in ((down_ref, o0), (up_ref, o1)):
        ref[high:, :LANES] = src[:half, :]
        ref[high:, LANES:] = src[half:, :]


def sea_array(j, sea_ref, depth_ref, wet_ref):
    if j < 3:
        return sea_ref[j]
    return depth_ref[...] if j == 3 else wet_ref[...].astype(F32)


def along_x_kernel(
    axes, uplift_ref, low_ref, high_ref, sea_ref, depth_ref, wet_ref, b_hi, b_lo, o2, o3,
    along_ref, ext_ref, right_ref, left_ref,
):
    tile_x, tile_y = uplift_ref.shape[1:]
    at_x = lax.axis_index(axes[0])
    has_low = at_x > 0
    has_high = at_x < lax.axis_size(axes[0]) - 1
    for t in range(STEPS):
        at = slice(t * HALO_X, (t + 1) * HALO_X)
        value = jnp.concatenate(
            [
                uplift_ref[t],
                jnp.where(has_high, high_ref[at, :], 0.0),
                jnp.where(has_low, low_ref[at, :], 0.0),
            ],
            axis=0,
        )
        hi, lo = split(value)
        along_ref[t] = mm(b_hi[...], hi) + mm(b_hi[...], lo) + mm(b_lo[...], hi)
    for j in range(5):
        at = slice(STEPS * HALO_X + j * EDGE, STEPS * HALO_X + (j + 1) * EDGE)
        ext_ref[j] = jnp.concatenate(
            [
                sea_array(j, sea_ref, depth_ref, wet_ref),
                jnp.where(has_high, high_ref[at, :], 0.0),
                jnp.where(has_low, low_ref[at, :], 0.0),
            ],
            axis=0,
        )
    tall = along_ref.shape[1]
    lane = iota((tall, LANES), 1)
    last = slice(tile_y - LANES, tile_y)
    first = slice(0, LANES)
    right = along_ref[0, :, last]
    left = along_ref[0, :, first]
    right = jnp.where(
        lane >= LANES - HALO_Y, right, pltpu.roll(along_ref[1, :, last], LANES - HALO_Y, 1)
    )
    left = jnp.where(lane < HALO_Y, left, pltpu.roll(along_ref[1, :, first], HALO_Y, 1))
    for j in range(5):
        moved = 2 * HALO_Y + 2 * j
        right = jnp.where(
            lane >= LANES - moved, right, pltpu.roll(ext_ref[j, :, last], LANES - moved, 1)
        )
        left = jnp.where(lane < moved, left, pltpu.roll(ext_ref[j, :, first], moved, 1))
    right_ref[0:tall] = right
    left_ref[0:tall] = left
    right_ref[tall:] = o3[...]
    left_ref[tall:] = o2[...]


def ocean_kernel(axes, along_ref, ext_ref, low_ref, high_ref, b_hi, b_lo, out_ref):
    tall, tile_y = along_ref.shape[1:]
    tile_x = out_ref.shape[1]
    at_y = lax.axis_index(axes[1])
    low = jnp.where(at_y > 0, low_ref[0:tall], 0.0)
    high = jnp.where(at_y < lax.axis_size(axes[1]) - 1, high_ref[0:tall], 0.0)
    lane = iota((tall, LANES), 1)
    forces = []
    for t in range(STEPS):
        right = pltpu.roll(high, LANES - HALO_Y, 1) if t else high
        left = pltpu.roll(low, HALO_Y, 1) if t else low
        value = jnp.concatenate([along_ref[t], right, left], axis=1)
        hi, lo = split(value)
        forces.append(mm(hi, b_hi[...]) + mm(lo, b_hi[...]) + mm(hi, b_lo[...]))
    fields = []
    for j in range(5):
        moved = 2 * HALO_Y + 2 * j
        edge = jnp.where(
            lane < LANES // 2, pltpu.roll(high, LANES - moved, 1), pltpu.roll(low, moved, 1)
        )
        fields.append(jnp.concatenate([ext_ref[j], edge], axis=1))
    eta, east, north, depth, wet = fields
    rows, cols = eta.shape

    def px(x):
        return pltpu.roll(x, rows - 1, 0)

    def mx(x):
        return pltpu.roll(x, 1, 0)

    def py(x):
        return pltpu.roll(x, cols - 1, 1)

    def my(x):
        return pltpu.roll(x, 1, 1)

    factor = 0.5 * COURANT
    for t in range(STEPS):
        eta = eta + wet * forces[t]
        column = depth + eta
        qx, qy = column * east, column * north
        near = [(px(a), mx(a), py(a), my(a)) for a in (eta, east, north)]
        mean = [0.25 * (a + b + c + d) for a, b, c, d in near]
        eta_x, eta_y = near[0][0] - near[0][1], near[0][2] - near[0][3]
        east_x, east_y = near[1][0] - near[1][1], near[1][2] - near[1][3]
        north_x, north_y = near[2][0] - near[2][1], near[2][2] - near[2][3]
        eta_new = mean[0] - factor * ((px(qx) - mx(qx)) + (py(qy) - my(qy)))
        east_new = mean[1] - factor * (east * east_x + north * east_y + eta_x)
        north_new = mean[2] - factor * (east * north_x + north * north_y + eta_y)
        eta, east, north = eta_new * wet, east_new * wet, north_new * wet
    out_ref[0] = eta[:tile_x, :tile_y]
    out_ref[1] = east[:tile_x, :tile_y]
    out_ref[2] = north[:tile_x, :tile_y]


def shift(value, axis, step):
    count = lax.axis_size(axis)
    return lax.ppermute(value, axis, [(i, (i + step) % count) for i in range(count)])


def on_device(
    state, star, deriv, trace_ops, lift, face_flux, orient, neighbours, send_faces,
    sea_faces, sea_owner, sea_blocks, sea_weights, depth, wet, sea_state,
):
    variables, basis, elems = state.shape
    nodes = trace_ops.shape[2]
    np_ = pad8(nodes)
    faces = 4 * elems
    slots = send_faces.shape[-1]
    rows = -(-variables * np_ // 16) * 16
    kb = -(-basis // 16) * 16
    turns = node_turns()
    place = np.zeros((4, nodes, 12 * np_), np.float32)
    perm = np.zeros((2 * rows, rows), np.float32)
    for r in range(3):
        for n in range(nodes):
            for f in range(4):
                place[f, turns[r][n], (r * 4 + f) * np_ + n] = 1.0
            for v in range(variables):
                if r:
                    perm[(r - 1) * rows + v * np_ + n, v * np_ + turns[r][n]] = 1.0
    place = jnp.asarray(place, BF16)
    perm = jnp.asarray(perm, BF16)

    wide = (rows, faces)
    out = (rows, slots)
    field_shape = (variables, basis, elems)
    moved = ((variables, 3 * basis, elems), F32)
    left = ((2 * rows, faces), BF16)
    arr_left = ((2 * rows, 4 * slots), BF16)
    flux = ((variables, 4 * np_, elems), F32)

    w, wt, integ, own0, own1, own2, *outgoing = call(
        first_kernel,
        [((3 * basis, 3 * kb), BF16), ((12 * np_, 3 * kb), BF16), (field_shape, F32)]
        + [(wide, F32)] * 3 + [(out, F32)] * 4,
        [moved, (field_shape, F32), left],
        state, star, deriv, trace_ops, place, send_faces, name="first",
    )
    arrived = [
        shift(outgoing[1], "gx", 1), shift(outgoing[0], "gx", -1),
        shift(outgoing[3], "gy", 1), shift(outgoing[2], "gy", -1),
    ]
    jump, base, source_turn, slot_turn, wl, sx_up, sx_down = call(
        local_first_kernel,
        [(wide, F32), (field_shape, F32), ((8, faces), F32), ((8, 4 * slots), F32),
         ((2 * basis, 8 * np_), BF16)] + [((5 * EDGE, depth.shape[1]), F32)] * 2,
        [left, moved],
        own0, own1, own2, neighbours, orient, lift, state, integ, star, w,
        sea_state, depth, wet, name="local_first",
    )
    own_first = own0
    field, integ, own0, own1, own2, *outgoing = call(
        second_kernel,
        [(field_shape, F32), (field_shape, F32)] + [(wide, F32)] * 3 + [(out, F32)] * 4,
        [arr_left, (wide, F32), flux, moved, (field_shape, F32), left],
        *arrived, slot_turn, neighbours, jump, face_flux, perm, wl, base, star, w, wt,
        send_faces, name="second",
    )

    sea_rows, cells = sea_weights.shape[1:]
    devs = lax.axis_size("gx") * lax.axis_size("gy")
    capacity = max(2, (sea_rows + devs - 1) // devs)
    total = devs * capacity
    payload, = call(
        lambda *refs: project_kernel(capacity, nodes, *refs),
        [((total, STEPS * cells + LANES), F32)],
        [((sea_rows, LANES), F32), ((STEPS, sea_rows, cells), F32)],
        own_first, own0, sea_faces.reshape(1, -1), sea_owner, sea_blocks.reshape(1, -1),
        sea_weights, name="project",
    )
    got = lax.all_to_all(payload, ("gx", "gy"), split_axis=0, concat_axis=0, tiled=True)
    jump, base = call(
        local_second_kernel, [(wide, F32), (field_shape, F32)], [left, moved],
        own0, own1, own2, neighbours, source_turn, field, integ, star, w, name="local_second",
    )

    tile_x, tile_y = depth.shape
    message = (STEPS * HALO_X + 5 * EDGE + rows // 2, tile_y)
    uplift, up, down = call(
        raster_kernel, [((STEPS, tile_x, tile_y), F32), (message, F32), (message, F32)], [],
        got, sx_up, sx_down, outgoing[0], outgoing[1], name="raster",
    )
    x_low, x_high = shift(up, "gx", 1), shift(down, "gx", -1)
    tall = tile_x + 2 * EDGE
    cell_x = np.concatenate([np.arange(tile_x + EDGE), np.arange(-EDGE, 0)])
    read_x = np.concatenate([np.arange(tile_x + HALO_X), np.arange(-HALO_X, 0)])
    cell_y = np.concatenate([np.arange(tile_y + LANES // 2), np.arange(-LANES // 2, 0)])
    read_y = np.concatenate([np.arange(tile_y + LANES), np.arange(-LANES, 0)])
    bx = [jnp.asarray(b) for b in band(cell_x, read_x)]
    by = [jnp.asarray(b.T) for b in band(cell_y, read_y)]
    axes = ("gx", "gy")
    along, ext, right, left_going = call(
        lambda *refs: along_x_kernel(axes, *refs),
        [((STEPS, tall, tile_y), F32), ((5, tall, tile_y), F32)]
        + [((tall + rows, LANES), F32)] * 2, [],
        uplift, x_low, x_high, sea_state, depth, wet, *bx, outgoing[2], outgoing[3],
        name="along_x",
    )
    y_low, y_high = shift(right, "gy", 1), shift(left_going, "gy", -1)
    ocean, = call(
        lambda *refs: ocean_kernel(axes, *refs), [((3, tile_x, tile_y), F32)], [],
        along, ext, y_low, y_high, *by, name="ocean",
    )
    elastic, = call(
        last_kernel, [(field_shape, F32)], [arr_left, (wide, F32), flux],
        x_low, x_high, y_low, y_high, slot_turn, neighbours, jump, face_flux, perm, wl, base,
        name="last",
    )
    return elastic, ocean


def solution(mesh):
    both = ("gx", "gy")
    placed = (
        P(None, None, both),
        P(None, None, None, both),
        P(),
        P(),
        P(),
        P(None, None, None, both),
        P(None, both),
        P(None, both),
        P("gx", "gy", None, None),
        P(both),
        P(both, None),
        P(both),
        P(None, both, None),
        P("gx", "gy"),
        P("gx", "gy"),
        P(None, "gx", "gy"),
    )
    return jax.shard_map(
        on_device,
        mesh=mesh,
        in_specs=placed,
        out_specs=(P(None, None, both), P(None, "gx", "gy")),
        check_vma=False,
    )
```

```python
import math

import jax
import jax.numpy as jnp
import numpy as np
from jax import lax
from jax.experimental import pallas as pl
from jax.experimental.pallas import tpu as pltpu
from jax.sharding import PartitionSpec as P


ORDER = 6
STEPS = 2
BS = 16
HALF = 32
SPREAD = 8.0
COURANT = 0.25
LANES = 128
HALO_X = 40
HALO_Y = 34
EDGE = 8
SEA_ROWS = 16
F32 = jnp.float32
BF16 = jnp.bfloat16


def node_turns():
    upper = ORDER - 1
    nodes = [(i, j) for i in range(upper + 1) for j in range(upper + 1 - i)]
    once = [nodes.index((pair[1], upper - pair[0] - pair[1])) for pair in nodes]
    twice = [once[once[number]] for number in range(len(nodes))]
    return [list(range(len(nodes))), once, twice]


def pad8(n):
    return -(-n // 8) * 8


def band(out_at, in_at):
    k = np.arange(-HALF, HALF + 1)
    raw = 1.0 / np.cosh(math.pi * k / (2.0 * SPREAD))
    raw = raw / raw.sum()
    diff = in_at[None, :] - out_at[:, None]
    w = np.where(np.abs(diff) <= HALF, raw[np.clip(diff + HALF, 0, 2 * HALF)], 0.0)
    w = w.astype(np.float32)
    hi = w.astype(jnp.bfloat16)
    lo = (w - hi.astype(np.float32)).astype(jnp.bfloat16)
    return hi, lo


def split(x):
    hi = x.astype(BF16)
    lo = (x - hi.astype(F32)).astype(BF16)
    return hi, lo


def mm(a, b):
    return lax.dot_general(a, b, (((1,), (0,)), ((), ())), preferred_element_type=F32)


def mm_tn(a, b):
    return lax.dot_general(a, b, (((0,), (0,)), ((), ())), preferred_element_type=F32)


def mm_nt(a, b):
    return lax.dot_general(a, b, (((1,), (1,)), ((), ())), preferred_element_type=F32)


def iota(shape, dim):
    return lax.broadcasted_iota(jnp.int32, shape, dim)


def hot(mask):
    return jnp.where(mask, 1.0, 0.0).astype(BF16)


HBM = "hbm"


def call(body, outs, scratch, *args, micros, limit=20, held=()):
    def spec(in_hbm):
        return pl.BlockSpec(memory_space=pltpu.HBM if in_hbm else pltpu.VMEM)

    args = [
        pltpu.with_memory_space_constraint(a, pltpu.HBM) if i in held else a
        for i, a in enumerate(args)
    ]
    return pl.pallas_call(
        body,
        in_specs=[spec(i in held) for i in range(len(args))],
        out_specs=[spec(len(o) == 3) for o in outs],
        out_shape=[(pltpu.HBM if len(o) == 3 else jax.ShapeDtypeStruct)(o[0], o[1]) for o in outs],
        scratch_shapes=[pltpu.VMEM(*x) if isinstance(x, tuple) else x for x in scratch],
        compiler_params=pltpu.CompilerParams(vmem_limit_bytes=limit * 2**20),
        cost_estimate=pl.CostEstimate(
            flops=micros * 10**8, bytes_accessed=micros * 3 * 10**6, transcendentals=0
        ),
    )(*args)


def sems(count):
    return pltpu.SemaphoreType.DMA((count,))


def start(pairs, sem_ref, first=0):
    copies = [
        pltpu.make_async_copy(src, dst, sem_ref.at[first + i])
        for i, (src, dst) in enumerate(pairs)
    ]
    for copy in copies:
        copy.start()
    return copies


def finish(copies):
    for copy in copies:
        copy.wait()


def slots_of(basis):
    kb = -(-basis // 16) * 16
    row, col = iota((basis, 3 * kb), 0), iota((basis, 3 * kb), 1)
    return hot((col == row) | (col == kb + row)), hot(col == 2 * kb + row)


def prep_deriv(deriv_ref, w_ref):
    basis = deriv_ref.shape[1]
    sel_hi, sel_lo = slots_of(basis)
    parts = []
    for d in range(3):
        hi, lo = split(deriv_ref[d])
        parts.append(mm_tn(hi, sel_hi) + mm_tn(lo, sel_lo))
    w_ref[...] = jnp.concatenate(parts, axis=0).astype(BF16)


def staged(ref, stage_ref):
    for n in range(ref.shape[0]):
        stage_ref[n * 4 : (n + 1) * 4, :] = ref[n]
    return split(stage_ref[...])


def prep_trace(trace_ref, place_ref, stage_ref, wt_ref):
    sel_hi, sel_lo = slots_of(trace_ref.shape[2])
    hi, lo = staged(trace_ref, stage_ref)
    hi = mm(place_ref[...], hi).astype(BF16)
    lo = mm(place_ref[...], lo).astype(BF16)
    wt_ref[...] = (mm(hi, sel_hi) + mm(lo, sel_lo)).astype(BF16)


def prep_lift(lift_ref, stage_ref, wl_ref):
    nodes = lift_ref.shape[0]
    np_ = pad8(nodes)
    row, col = iota((4 * nodes, 8 * np_), 0), iota((4 * nodes, 8 * np_), 1)
    at = (row % 4) * np_ + row // 4
    sel = hot((col == at) | (col == 4 * np_ + at))
    hi, lo = staged(lift_ref, stage_ref)
    wl_ref[...] = jnp.concatenate([mm_tn(hi, sel), mm_tn(lo, sel)], axis=0).astype(BF16)


def stacked(x):
    rows = x.shape[0]
    pad = -(-rows // 16) * 16 - rows
    if pad:
        x = jnp.concatenate([x, jnp.zeros((pad, x.shape[1]), F32)], axis=0)
    hi, lo = split(x)
    return jnp.concatenate([hi, lo, hi], axis=0)


def derive(src_ref, star_ref, w_ref, moved_ref, emit):
    variables, basis, elems = src_ref.shape
    for v in range(variables):
        moved_ref[v] = mm(w_ref[...], stacked(src_ref[v]))
    group = 3

    def body(g, carry):
        for h in range(elems // LANES):
            at = slice(h * LANES, (h + 1) * LANES)
            acc = [jnp.zeros((basis, LANES), F32) for _ in range(group)]
            for v in range(variables):
                for d in range(3):
                    m = moved_ref[v, d * basis : (d + 1) * basis, at]
                    for i in range(group):
                        acc[i] = acc[i] + star_ref[g * group + i, v, d : d + 1, at] * m
            for i in range(group):
                emit(g * group + i, at, acc[i])
        return carry

    lax.fori_loop(0, variables // group, body, 0)


def predict(field_ref, star_ref, w_ref, moved_ref, term_ref, integ_ref):
    if field_ref is not term_ref:
        term_ref[...] = field_ref[...]
    integ_ref[...] = term_ref[...]

    def body(k, carry):
        scale = F32(-1.0 / ORDER)
        for o in range(1, ORDER - 1):
            scale = jnp.where(k == o, F32(-1.0 / (o + 1)), scale)

        def emit(u, at, acc):
            value = acc * scale
            term_ref[u, :, at] = value
            integ_ref[u, :, at] = integ_ref[u, :, at] + value

        derive(term_ref, star_ref, w_ref, moved_ref, emit)
        return carry

    lax.fori_loop(1, ORDER, body, 0)


def traces(integ_ref, wt_ref, own_refs):
    variables, _, elems = integ_ref.shape
    np_ = wt_ref.shape[0] // 12
    count = len(own_refs)
    for v in range(variables):
        t = mm(wt_ref[0 : count * 4 * np_, :], stacked(integ_ref[v]))
        for r in range(count):
            for f in range(4):
                own_refs[r][v * np_ : (v + 1) * np_, f * elems : (f + 1) * elems] = t[
                    (r * 4 + f) * np_ : (r * 4 + f + 1) * np_
                ]
    rows = own_refs[0].shape[0]
    for r in range(count):
        if rows > variables * np_:
            own_refs[r][variables * np_ :, :] = jnp.zeros(
                (rows - variables * np_, 4 * elems), F32
            )


def send_gather(own_ref, send_ref, left_ref, outs):
    rows, faces = own_ref.shape
    hi, lo = split(own_ref[...])
    left_ref[0:rows] = hi
    left_ref[rows : 2 * rows] = lo
    slots = send_ref.shape[3]
    for k in range(0, 4, 2):
        picks = jnp.concatenate([send_ref[0, 0, k : k + 1], send_ref[0, 0, k + 1 : k + 2]], axis=1)
        res = mm(left_ref[...], hot(iota((faces, 2 * slots), 0) == picks))
        res = res[:rows] + res[rows:]
        outs[k][0:rows] = res[:, :slots]
        outs[k + 1][0:rows] = res[:, slots:]


def row_of(ref):
    return jnp.concatenate([ref[f : f + 1, :] for f in range(ref.shape[0])], axis=1)


def local_jump(own_refs, source_turn, codes, left_ref, jump_ref):
    rows, faces = own_refs[0].shape
    width = faces // 4
    value = jnp.where(
        source_turn == 1.0,
        own_refs[1][...],
        jnp.where(source_turn == 2.0, own_refs[2][...], own_refs[0][...]),
    )
    hi, lo = split(value)
    left_ref[0:rows] = hi
    left_ref[rows : 2 * rows] = lo
    for q in range(4):
        at = slice(q * width, (q + 1) * width)
        res = mm(left_ref[...], hot(iota((faces, width), 0) == codes[:, at]))
        jump_ref[:, at] = own_refs[0][:, at] - (res[:rows] + res[rows:])


def surface(arrived, slot_turn, codes, jump_ref, flux_m_ref, perm_ref, wl_ref, base_ref, scratch, out_ref):
    left_ref, part_ref, flux_ref = scratch
    rows, faces = jump_ref.shape
    variables, basis, elems = base_ref.shape
    value = jnp.concatenate(arrived, axis=1)
    slots = value.shape[1]
    hi, lo = split(value)
    both = jnp.concatenate([hi, lo], axis=1)
    turned = mm(perm_ref[...], both)
    turn = jnp.concatenate([slot_turn, slot_turn], axis=1)
    chosen = jnp.where(
        turn == 1.0, turned[:rows], jnp.where(turn == 2.0, turned[rows:], both.astype(F32))
    ).astype(BF16)
    left_ref[0:rows] = chosen[:, :slots]
    left_ref[rows : 2 * rows] = chosen[:, slots:]
    for q in range(4):
        at = slice(q * elems, (q + 1) * elems)
        res = mm(left_ref[...], hot(iota((slots, elems), 0) + faces == codes[:, at]))
        part_ref[:, at] = jump_ref[:, at] - (res[:rows] + res[rows:])
    np_ = flux_ref.shape[1] // 4

    group = 3

    def body(g, carry):
        for f in range(4):
            for h in range(elems // LANES):
                here = slice(h * LANES, (h + 1) * LANES)
                wide = slice(f * elems + h * LANES, f * elems + (h + 1) * LANES)
                acc = [jnp.zeros((np_, LANES), F32) for _ in range(group)]
                for v in range(variables):
                    jump = part_ref[v * np_ : (v + 1) * np_, wide]
                    for i in range(group):
                        acc[i] = acc[i] + flux_m_ref[g * group + i, v, f : f + 1, here] * jump
                for i in range(group):
                    flux_ref[g * group + i, f * np_ : (f + 1) * np_, here] = acc[i]
        return carry

    lax.fori_loop(0, variables // group, body, 0)
    for u in range(variables):
        hi, lo = split(flux_ref[u])
        res = mm(wl_ref[...], jnp.concatenate([hi, lo], axis=0))
        out_ref[u] = base_ref[u] - (res[:basis] + res[basis:])


def first_kernel(
    state_hbm, star_hbm, deriv_hbm, trace_hbm, place_hbm, send_hbm, sea_hbm, depth_hbm, wet_hbm,
    w_ref, wt_ref, integ_ref, lifted_ref, o0, o1, o2, o3,
    star_ref, deriv_ref, trace_ref, place_ref, send_ref, own_ref,
    moved_ref, term_ref, left_ref, stage_ref, sea_edge, depth_edge, wet_edge, sem_ref,
):
    urgent = start(
        [(deriv_hbm, deriv_ref), (state_hbm, term_ref), (star_hbm, star_ref)], sem_ref
    )
    later = start(
        [(trace_hbm, trace_ref), (place_hbm, place_ref), (send_hbm, send_ref)], sem_ref, 3
    )
    tall = depth_hbm.shape[0]
    pairs = []
    for side, at in enumerate((pl.ds(0, EDGE), pl.ds(tall - EDGE, EDGE))):
        for j in range(3):
            pairs.append((sea_hbm.at[j, at], sea_edge.at[side, j]))
        pairs.append((depth_hbm.at[at], depth_edge.at[side]))
        pairs.append((wet_hbm.at[at], wet_edge.at[side]))
    later = later + start(pairs, sem_ref, 6)
    finish(urgent[:1])
    prep_deriv(deriv_ref, w_ref)
    finish(urgent[1:])
    predict(term_ref, star_ref, w_ref, moved_ref, term_ref, integ_ref)
    finish(later)
    prep_trace(trace_ref, place_ref, stage_ref, wt_ref)
    traces(integ_ref, wt_ref, (own_ref,))
    send_gather(own_ref, send_ref, left_ref, (o0, o1, o2, o3))
    rows = own_ref.shape[0]
    np_ = lifted_ref.shape[0]
    lifted_ref[...] = own_ref[2 * np_ : 3 * np_, :]
    for side, (out, at) in enumerate(((o0, 0), (o1, EDGE - STEPS))):
        for j in range(5):
            if j < 3:
                edge = sea_edge[side, j]
            else:
                edge = depth_edge[side] if j == 3 else wet_edge[side].astype(F32)
            for h in range(edge.shape[1] // LANES):
                begin = rows + h * SEA_ROWS + j * STEPS
                out[begin : begin + STEPS] = edge[
                    at : at + STEPS, h * LANES : (h + 1) * LANES
                ]


def local_work(
    integ_ref, field_ref, star_ref, w_ref, wt_ref, turn, codes, jump_ref, base_ref,
    own_refs, left_ref, moved_ref,
):
    traces(integ_ref, wt_ref, own_refs)
    local_jump(own_refs, turn, codes, left_ref, jump_ref)

    def emit(u, at, acc):
        base_ref[u, :, at] = field_ref[u, :, at] - acc

    derive(integ_ref, star_ref, w_ref, moved_ref, emit)


def local_first_kernel(
    integ_ref, field_ref, star_ref, w_ref, wt_ref, codes_ref, orient_ref, lift_ref,
    jump_ref, base_ref, slot_ref, wl_ref, turn_out, slot_out, wl_out, w_out, wt_out,
    turn_ref, own0, own1, own2, left_ref, moved_ref, stage_ref, sem_ref,
):
    prep_lift(lift_ref, stage_ref, wl_ref)
    codes = row_of(codes_ref)
    faces = codes.shape[1]
    slots = slot_ref.shape[1]
    turns = jnp.broadcast_to(row_of(orient_ref).astype(F32), (16, faces)).astype(BF16)
    width = faces // 4
    for q in range(4):
        at = slice(q * width, (q + 1) * width)
        turn_ref[:, at] = mm(turns, hot(iota((faces, width), 0) == codes[:, at]))[0:8]
    for q in range(slots // LANES):
        at = slice(q * LANES, (q + 1) * LANES)
        wanted = iota((LANES, faces), 0) + (faces + q * LANES)
        slot_ref[:, at] = mm_nt(turns, hot(wanted == codes))[0:8]
    copies = start(
        [(turn_ref, turn_out), (slot_ref, slot_out), (wl_ref, wl_out), (w_ref, w_out),
         (wt_ref, wt_out)], sem_ref,
    )
    local_work(
        integ_ref, field_ref, star_ref, w_ref, wt_ref, turn_ref[0:1, :], codes, jump_ref, base_ref,
        (own0, own1, own2), left_ref, moved_ref,
    )
    finish(copies)


def second_kernel(
    a0, a1, a2, a3, slot_ref, codes_ref, jump_ref, flux_m_ref, perm_ref, wl_ref, base_ref,
    star_ref, w_ref, wt_ref, send_ref,
    lifted_ref, field_out, integ_out, edge_low, edge_high, s0, s1, s2, s3,
    field_ref, integ_ref, own_ref, o0, o1, o2, o3,
    arr_left_ref, part_ref, flux_ref, moved_ref, term_ref, left_ref, sem_ref,
):
    rows = jump_ref.shape[0]
    tail = pl.ds(rows, a0.shape[0] - rows)
    copies = start([(a0.at[tail], edge_low), (a1.at[tail], edge_high)], sem_ref)
    surface(
        [a[0:rows] for a in (a0, a1, a2, a3)], slot_ref[0:1, :], row_of(codes_ref), jump_ref,
        flux_m_ref, perm_ref, wl_ref, base_ref, (arr_left_ref, part_ref, flux_ref), field_ref,
    )
    copies += start([(field_ref, field_out)], sem_ref, 2)
    predict(field_ref, star_ref, w_ref, moved_ref, term_ref, integ_ref)
    copies += start([(integ_ref, integ_out)], sem_ref, 3)
    traces(integ_ref, wt_ref, (own_ref,))
    np_ = lifted_ref.shape[0]
    lifted_ref[...] = own_ref[2 * np_ : 3 * np_, :]
    send_gather(own_ref, send_ref, left_ref, (o0, o1, o2, o3))
    copies += start([(o0, s0), (o1, s1), (o2, s2), (o3, s3)], sem_ref, 4)
    finish(copies)


def local_second_kernel(
    integ_hbm, field_hbm, star_hbm, w_hbm, wt_hbm, turn_hbm, codes_hbm,
    jump_out, base_out,
    integ_ref, field_ref, star_ref, w_ref, wt_ref, turn_ref, codes_ref, jump_ref, base_ref,
    own0, own1, own2, left_ref, moved_ref, sem_ref,
):
    copies = start(
        [(integ_hbm, integ_ref), (wt_hbm, wt_ref), (turn_hbm, turn_ref), (codes_hbm, codes_ref),
         (star_hbm, star_ref), (w_hbm, w_ref), (field_hbm, field_ref)], sem_ref,
    )
    finish(copies)
    local_work(
        integ_ref, field_ref, star_ref, w_ref, wt_ref, turn_ref[0:1, :], row_of(codes_ref),
        jump_ref, base_ref, (own0, own1, own2), left_ref, moved_ref,
    )
    finish(start([(jump_ref, jump_out), (base_ref, base_out)], sem_ref, 7))


def last_kernel(
    a0, a1, a2, a3, slot_hbm, codes_hbm, jump_hbm, flux_m_hbm, perm_hbm, wl_hbm, base_hbm,
    field_out,
    b0, b1, b2, b3, slot_ref, codes_ref, jump_ref, flux_m_ref, perm_ref, wl_ref, base_ref,
    field_ref, arr_left_ref, part_ref, flux_ref, sem_ref,
):
    copies = start(
        [(a0, b0), (a1, b1), (a2, b2), (a3, b3), (slot_hbm, slot_ref), (perm_hbm, perm_ref),
         (codes_hbm, codes_ref), (jump_hbm, jump_ref), (flux_m_hbm, flux_m_ref),
         (wl_hbm, wl_ref), (base_hbm, base_ref)], sem_ref,
    )
    finish(copies)
    surface(
        [b0[...], b1[...], b2[...], b3[...]], slot_ref[0:1, :], row_of(codes_ref), jump_ref,
        flux_m_ref, perm_ref, wl_ref, base_ref, (arr_left_ref, part_ref, flux_ref), field_ref,
    )
    finish(start([(field_ref, field_out)], sem_ref))


def project_kernel(capacity, nodes, own_a, own_b, faces_ref, owner_ref, blocks_ref, weights_ref, pay_ref, disp_ref, rows_ref):
    np_ = pad8(nodes)
    faces = own_a.shape[1]
    sea_rows, _ = weights_ref.shape[1:]
    both = jnp.concatenate([own_a[...], own_b[...]], axis=0)
    hi, lo = split(both)
    picks = hot(iota((faces, sea_rows), 0) == faces_ref[...])
    disp = mm(jnp.concatenate([hi, lo], axis=0), picks)
    disp = disp[: 2 * np_] + disp[2 * np_ :]
    disp = jnp.concatenate([disp, jnp.zeros((LANES - 2 * np_, sea_rows), F32)], axis=0)
    disp_ref[...] = disp.T
    across = jnp.broadcast_to(owner_ref[...].astype(F32), (sea_rows, sea_rows))
    owner = across.T
    earlier = iota((sea_rows, sea_rows), 0) < iota((sea_rows, sea_rows), 1)
    rank = jnp.sum(jnp.where((owner == across) & earlier, 1.0, 0.0), axis=0, keepdims=True)
    place = (across[0:1, :] * float(capacity) + rank).astype(jnp.int32)
    devs = pay_ref.shape[0]
    total = devs * capacity
    put = hot(iota((total, sea_rows), 0) == place)
    chunk = 32

    def body(c, carry):
        here = pl.ds(pl.multiple_of(c * chunk, chunk), chunk)
        cols = disp_ref[here, :]
        for t in range(STEPS):
            acc = cols[:, t * np_ : t * np_ + 1] * weights_ref[0, here, :]
            for n in range(1, nodes):
                acc = acc + cols[:, t * np_ + n : t * np_ + n + 1] * weights_ref[n, here, :]
            rows_ref[t, here, :] = acc
        return carry

    lax.fori_loop(0, sea_rows // chunk, body, 0)
    twice = jnp.concatenate([put, put], axis=1)
    parts = []
    for t in range(STEPS):
        hi, lo = split(rows_ref[t])
        parts.append(mm(twice, jnp.concatenate([hi, lo], axis=0)))
    labels = jnp.broadcast_to(blocks_ref[...].astype(F32), (LANES, sea_rows)).astype(BF16)
    parts.append(mm_nt(put, labels))
    value = jnp.concatenate(parts, axis=1)
    for d in range(devs):
        pay_ref[d] = value[d * capacity : (d + 1) * capacity]


def raster_kernel(
    pay_hbm, bx_hi_hbm, bx_lo_hbm, by_hi_hbm, by_lo_hbm, ext_hbm, right_hbm, left_hbm,
    uplift_ref, up_ref, down_ref, bx_hi, bx_lo, by_hi, by_lo, ext_ref, right_ref, left_ref,
    pay_ref, got_ref, sem_ref,
):
    urgent = start([(pay_hbm, pay_ref)], sem_ref)
    later = start(
        [(bx_hi_hbm, bx_hi), (bx_lo_hbm, bx_lo), (right_hbm, right_ref), (left_hbm, left_ref),
         (by_hi_hbm, by_hi), (by_lo_hbm, by_lo), (ext_hbm, ext_ref)], sem_ref, 1,
    )
    finish(urgent)
    devs, capacity, _ = pay_ref.shape
    total = devs * capacity
    for d in range(devs):
        got_ref[d * capacity : (d + 1) * capacity] = pay_ref[d]
    tile_x, tile_y = uplift_ref.shape[1:]
    across = tile_y // BS
    cells = BS * BS
    blocks = (tile_x // BS) * across
    labels = got_ref[:, STEPS * cells :].T
    pick = hot(iota((blocks, total), 0) == labels[0:1, :].astype(jnp.int32))
    pick = jnp.concatenate([pick, pick], axis=1)
    by = iota((blocks, cells), 0) % across
    cx = iota((blocks, cells), 1) // BS
    for t in range(STEPS):
        hi, lo = split(got_ref[:, t * cells : (t + 1) * cells])
        x = mm(pick, jnp.concatenate([hi, lo], axis=0))
        step = 1
        while step < BS:
            from_above = pltpu.roll(pltpu.roll(x, blocks - step, 0), BS * step, 1)
            from_below = pltpu.roll(pltpu.roll(x, step, 0), cells - BS * step, 1)
            low_row = (by & step) == 0
            low_col = (cx & step) == 0
            x = jnp.where(low_row == low_col, x, jnp.where(low_row, from_above, from_below))
            step *= 2
        uplift_ref[t] = x
        up_ref[t * HALO_X : (t + 1) * HALO_X] = x[tile_x - HALO_X :, :]
        down_ref[t * HALO_X : (t + 1) * HALO_X] = x[:HALO_X, :]
    finish(later)


def shore_kernel(
    axes, sea_hbm, depth_hbm, wet_hbm, low_hbm, high_hbm,
    ext_out, right_out, left_out,
    ext_ref, wet_ref, low_ref, high_ref, right_ref, left_ref, sem_ref,
):
    tile_x, tile_y = depth_hbm.shape
    body = pl.ds(0, tile_x)
    finish(
        start(
            [(sea_hbm.at[j], ext_ref.at[j, body]) for j in range(3)]
            + [(depth_hbm, ext_ref.at[3, body]), (wet_hbm, wet_ref), (low_hbm, low_ref),
               (high_hbm, high_ref)], sem_ref,
        )
    )
    ext_ref[4, 0:tile_x, :] = wet_ref[...].astype(F32)
    at_x = lax.axis_index(axes[0])
    has_low = at_x > 0
    has_high = at_x < lax.axis_size(axes[0]) - 1

    def edge_of(ref, present, j, before):
        halves = []
        for h in range(tile_y // LANES):
            begin = h * SEA_ROWS + j * STEPS
            halves.append(ref[begin : begin + STEPS, :])
        value = jnp.where(present, jnp.concatenate(halves, axis=1), 0.0)
        blank = jnp.zeros((EDGE - STEPS, tile_y), F32)
        return jnp.concatenate([blank, value] if before else [value, blank], axis=0)

    for j in range(5):
        ext_ref[j, tile_x : tile_x + EDGE, :] = edge_of(high_ref, has_high, j, False)
        ext_ref[j, tile_x + EDGE : tile_x + 2 * EDGE, :] = edge_of(low_ref, has_low, j, True)
    copies = start([(ext_ref, ext_out)], sem_ref)
    lane = iota(right_ref.shape, 1)
    right = jnp.zeros(right_ref.shape, F32)
    left = right
    for j in range(5):
        moved = 2 * HALO_Y + 2 * j
        last = ext_ref[j, :, tile_y - LANES :]
        first = ext_ref[j, :, :LANES]
        right = jnp.where(
            lane >= LANES - moved, right, pltpu.roll(last, LANES - moved, 1)
        )
        left = jnp.where(lane < moved, left, pltpu.roll(first, moved, 1))
    right_ref[...] = right
    left_ref[...] = left
    finish(copies + start([(right_ref, right_out), (left_ref, left_out)], sem_ref, 1))


def along_x_kernel(
    axes, uplift_ref, low_ref, high_ref, b_hi, b_lo, sea_right, sea_left,
    along_ref, right_ref, left_ref,
):
    _, tile_y = uplift_ref.shape[1:]
    at_x = lax.axis_index(axes[0])
    has_low = at_x > 0
    has_high = at_x < lax.axis_size(axes[0]) - 1
    for t in range(STEPS):
        at = slice(t * HALO_X, (t + 1) * HALO_X)
        value = jnp.concatenate(
            [
                uplift_ref[t],
                jnp.where(has_high, high_ref[at, :], 0.0),
                jnp.where(has_low, low_ref[at, :], 0.0),
            ],
            axis=0,
        )
        hi, lo = split(value)
        along_ref[t] = mm(b_hi[...], hi) + mm(b_hi[...], lo) + mm(b_lo[...], hi)
    tall = along_ref.shape[1]
    lane = iota((tall, LANES), 1)
    last = slice(tile_y - LANES, tile_y)
    first = slice(0, LANES)
    right, left = sea_right[...], sea_left[...]
    for t in reversed(range(STEPS)):
        moved = t * HALO_Y
        tail = along_ref[t, :, last]
        head = along_ref[t, :, first]
        if t:
            tail, head = pltpu.roll(tail, LANES - moved, 1), pltpu.roll(head, moved, 1)
        right = jnp.where(lane >= LANES - moved - HALO_Y, tail, right)
        left = jnp.where(lane < moved + HALO_Y, head, left)
    right_ref[...] = right
    left_ref[...] = left


def ocean_kernel(axes, along_ref, ext_ref, low_ref, high_ref, b_hi, b_lo, out_ref):
    tall, tile_y = along_ref.shape[1:]
    tile_x = out_ref.shape[1]
    at_y = lax.axis_index(axes[1])
    low = jnp.where(at_y > 0, low_ref[...], 0.0)
    high = jnp.where(at_y < lax.axis_size(axes[1]) - 1, high_ref[...], 0.0)
    lane = iota((tall, LANES), 1)
    forces = []
    for t in range(STEPS):
        right = pltpu.roll(high, LANES - HALO_Y, 1) if t else high
        left = pltpu.roll(low, HALO_Y, 1) if t else low
        value = jnp.concatenate([along_ref[t], right, left], axis=1)
        hi, lo = split(value)
        forces.append(mm(hi, b_hi[...]) + mm(lo, b_hi[...]) + mm(hi, b_lo[...]))
    fields = []
    for j in range(5):
        moved = 2 * HALO_Y + 2 * j
        edge = jnp.where(
            lane < LANES // 2, pltpu.roll(high, LANES - moved, 1), pltpu.roll(low, moved, 1)
        )
        fields.append(jnp.concatenate([ext_ref[j], edge], axis=1))
    eta, east, north, depth, wet = fields
    rows, cols = eta.shape

    def px(x):
        return pltpu.roll(x, rows - 1, 0)

    def mx(x):
        return pltpu.roll(x, 1, 0)

    def py(x):
        return pltpu.roll(x, cols - 1, 1)

    def my(x):
        return pltpu.roll(x, 1, 1)

    factor = 0.5 * COURANT
    for t in range(STEPS):
        eta = eta + wet * forces[t]
        column = depth + eta
        qx, qy = column * east, column * north
        near = [(px(a), mx(a), py(a), my(a)) for a in (eta, east, north)]
        mean = [0.25 * (a + b + c + d) for a, b, c, d in near]
        eta_x, eta_y = near[0][0] - near[0][1], near[0][2] - near[0][3]
        east_x, east_y = near[1][0] - near[1][1], near[1][2] - near[1][3]
        north_x, north_y = near[2][0] - near[2][1], near[2][2] - near[2][3]
        eta_new = mean[0] - factor * ((px(qx) - mx(qx)) + (py(qy) - my(qy)))
        east_new = mean[1] - factor * (east * east_x + north * east_y + eta_x)
        north_new = mean[2] - factor * (east * north_x + north * north_y + eta_y)
        eta, east, north = eta_new * wet, east_new * wet, north_new * wet
    out_ref[0] = eta[:tile_x, :tile_y]
    out_ref[1] = east[:tile_x, :tile_y]
    out_ref[2] = north[:tile_x, :tile_y]


def shift(value, axis, step):
    count = lax.axis_size(axis)
    return lax.ppermute(value, axis, [(i, (i + step) % count) for i in range(count)])


def on_device(
    state, star, deriv, trace_ops, lift, face_flux, orient, neighbours, send_faces,
    sea_faces, sea_owner, sea_blocks, sea_weights, depth, wet, sea_state,
):
    variables, basis, elems = state.shape
    nodes = trace_ops.shape[2]
    np_ = pad8(nodes)
    faces = 4 * elems
    slots = send_faces.shape[-1]
    rows = -(-variables * np_ // 16) * 16
    kb = -(-basis // 16) * 16
    turns = node_turns()
    place = np.zeros((12 * np_, 4 * nodes), np.float32)
    perm = np.zeros((2 * rows, rows), np.float32)
    for r in range(3):
        for n in range(nodes):
            for f in range(4):
                place[(r * 4 + f) * np_ + n, turns[r][n] * 4 + f] = 1.0
            for v in range(variables):
                if r:
                    perm[(r - 1) * rows + v * np_ + n, v * np_ + turns[r][n]] = 1.0
    place = jnp.asarray(place, BF16)
    perm = jnp.asarray(perm, BF16)
    star = star.transpose(1, 2, 0, 3)
    face_flux = face_flux.transpose(1, 2, 0, 3)
    trace_ops = trace_ops.transpose(2, 0, 1)
    lift = lift.transpose(1, 0, 2)

    wide = (rows, faces)
    out = (rows, slots)
    tile_x, tile_y = depth.shape
    out_x = (rows + (tile_y // LANES) * SEA_ROWS, slots)
    field_shape = (variables, basis, elems)
    moved = ((variables, 3 * basis, elems), F32)
    left = ((2 * rows, faces), BF16)
    arr_left = ((2 * rows, 4 * slots), BF16)
    flux = ((variables, 4 * np_, elems), F32)
    stage = ((4 * nodes, basis), F32)

    def sent(outgoing):
        return [
            shift(outgoing[1], "gx", 1), shift(outgoing[0], "gx", -1),
            shift(outgoing[3], "gy", 1), shift(outgoing[2], "gy", -1),
        ]

    w_of = ((3 * basis, 3 * kb), BF16)
    wt_of = ((12 * np_, 3 * kb), BF16)
    wl_of = ((2 * basis, 8 * np_), BF16)
    turn_of = ((8, faces), F32)
    slot_of = ((8, 4 * slots), F32)
    field_of, wide_of, out_of = (field_shape, F32), (wide, F32), (out, F32)
    star_of, flux_m_of = (star.shape, F32), (face_flux.shape, F32)
    lifted_of = ((np_, faces), F32)
    codes_of = (neighbours.shape, neighbours.dtype)
    perm_of = (perm.shape, BF16)

    def hbm(array):
        return (*array, HBM)

    w, wt, integ, lifted_a, *outgoing = call(
        first_kernel,
        [w_of, wt_of, field_of, lifted_of] + [(out_x, F32)] * 2 + [out_of] * 2,
        [star_of, (deriv.shape, F32), (trace_ops.shape, F32), (place.shape, BF16),
         (send_faces.shape, send_faces.dtype), wide_of, moved, field_of, left, stage,
         ((2, 3, EDGE, tile_y), F32), ((2, EDGE, tile_y), F32), ((2, EDGE, tile_y), wet.dtype),
         sems(16)],
        state, star, deriv, trace_ops, place, send_faces, sea_state, depth, wet,
        micros=10, held=range(9),
    )
    arrived = sent(outgoing)
    jump, base, slot_turn, wl, turn_h, slot_h, wl_h, w_h, wt_h = call(
        local_first_kernel,
        [wide_of, field_of, slot_of, wl_of, hbm(turn_of), hbm(slot_of), hbm(wl_of), hbm(w_of),
         hbm(wt_of)],
        [turn_of, wide_of, wide_of, wide_of, left, moved, stage, sems(5)],
        integ, state, star, w, wt, neighbours, orient, lift,
        micros=4,
    )
    lifted_b, field_h, integ_h, edge_low, edge_high, *outgoing = call(
        second_kernel,
        [lifted_of, hbm(field_of), hbm(field_of)]
        + [((out_x[0] - rows, slots), F32, HBM)] * 2 + [hbm(out_of)] * 4,
        [field_of, field_of, wide_of] + [out_of] * 4
        + [arr_left, wide_of, flux, moved, field_of, left, sems(8)],
        *arrived, slot_turn, neighbours, jump, face_flux, perm, wl, base, star, w, wt,
        send_faces, micros=10,
    )

    sea_rows, cells = sea_weights.shape[1:]
    devs = lax.axis_size("gx") * lax.axis_size("gy")
    capacity = max(2, (sea_rows + devs - 1) // devs)
    message = (devs, capacity, STEPS * cells + LANES)
    payload, = call(
        lambda *refs: project_kernel(capacity, nodes, *refs),
        [(message, F32)],
        [((sea_rows, LANES), F32), ((STEPS, sea_rows, cells), F32)],
        lifted_a, lifted_b, sea_faces.reshape(1, -1), sea_owner.reshape(1, -1),
        sea_blocks.reshape(1, -1), sea_weights, micros=3,
    )
    got = lax.all_to_all(payload, ("gx", "gy"), split_axis=0, concat_axis=0, tiled=True)
    arrived = sent(outgoing)
    tall = tile_x + 2 * EDGE
    axes = ("gx", "gy")
    ext_of = ((5, tall, tile_y), F32)
    strip_of = ((tall, LANES), F32)
    edge_of = (edge_low.shape, F32)
    ext_h, right_h, left_h = call(
        lambda *refs: shore_kernel(axes, *refs),
        [hbm(ext_of), hbm(strip_of), hbm(strip_of)],
        [ext_of, (wet.shape, wet.dtype), edge_of, edge_of, strip_of, strip_of, sems(7)],
        sea_state, depth, wet, edge_low, edge_high, micros=2, held=range(5),
    )
    jump_h, base_h = call(
        local_second_kernel, [hbm(wide_of), hbm(field_of)],
        [field_of, field_of, star_of, w_of, wt_of, turn_of, codes_of, wide_of, field_of,
         wide_of, wide_of, wide_of, left, moved, sems(9)],
        integ_h, field_h, star, w_h, wt_h, turn_h, neighbours,
        micros=5, held=range(7),
    )
    elastic, = call(
        last_kernel, [hbm(field_of)],
        [out_of] * 4 + [slot_of, codes_of, wide_of, flux_m_of, perm_of, wl_of, field_of, field_of,
         arr_left, wide_of, flux, sems(11)],
        *arrived, slot_h, neighbours, jump_h, face_flux, perm, wl_h, base_h,
        micros=4, held=range(11),
    )

    halo = ((STEPS * HALO_X, tile_y), F32)
    cell_x = np.concatenate([np.arange(tile_x + EDGE), np.arange(-EDGE, 0)])
    read_x = np.concatenate([np.arange(tile_x + HALO_X), np.arange(-HALO_X, 0)])
    cell_y = np.concatenate([np.arange(tile_y + LANES // 2), np.arange(-LANES // 2, 0)])
    read_y = np.concatenate([np.arange(tile_y + LANES), np.arange(-LANES, 0)])
    bands = [jnp.asarray(b) for b in band(cell_x, read_x)]
    bands += [jnp.asarray(b.T) for b in band(cell_y, read_y)]
    uplift, up, down, bx_hi, bx_lo, by_hi, by_lo, ext, sea_right, sea_left = call(
        raster_kernel,
        [((STEPS, tile_x, tile_y), F32), halo, halo]
        + [(b.shape, BF16) for b in bands] + [ext_of, strip_of, strip_of],
        [(message, F32), ((devs * capacity, message[2]), F32), sems(8)],
        got, *bands, ext_h, right_h, left_h, micros=3, held=range(8),
    )
    x_low, x_high = shift(up, "gx", 1), shift(down, "gx", -1)
    along, right, left_going = call(
        lambda *refs: along_x_kernel(axes, *refs),
        [((STEPS, tall, tile_y), F32), strip_of, strip_of], [],
        uplift, x_low, x_high, bx_hi, bx_lo, sea_right, sea_left, micros=1,
    )
    y_low, y_high = shift(right, "gy", 1), shift(left_going, "gy", -1)
    ocean, = call(
        lambda *refs: ocean_kernel(axes, *refs), [((3, tile_x, tile_y), F32)], [],
        along, ext, y_low, y_high, by_hi, by_lo, micros=4,
    )
    return elastic, ocean


def solution(mesh):
    both = ("gx", "gy")
    placed = (
        P(None, None, both),
        P(None, None, None, both),
        P(),
        P(),
        P(),
        P(None, None, None, both),
        P(None, both),
        P(None, both),
        P("gx", "gy", None, None),
        P(both),
        P(both, None),
        P(both),
        P(None, both, None),
        P("gx", "gy"),
        P("gx", "gy"),
        P(None, "gx", "gy"),
    )

    return jax.shard_map(
        on_device,
        mesh=mesh,
        in_specs=placed,
        out_specs=(P(None, None, both), P(None, "gx", "gy")),
        check_vma=False,
    )
```

```python
import math

import jax
import jax.numpy as jnp
import numpy as np
from jax import lax
from jax.experimental import pallas as pl
from jax.experimental.pallas import tpu as pltpu
from jax.sharding import PartitionSpec as P


ORDER = 6
STEPS = 2
BS = 16
HALF = 32
SPREAD = 8.0
COURANT = 0.25
LANES = 128
HALO_X = 40
HALO_Y = 34
EDGE = 8
SEA_ROWS = 16
F32 = jnp.float32
BF16 = jnp.bfloat16


def node_turns():
    upper = ORDER - 1
    nodes = [(i, j) for i in range(upper + 1) for j in range(upper + 1 - i)]
    once = [nodes.index((pair[1], upper - pair[0] - pair[1])) for pair in nodes]
    twice = [once[once[number]] for number in range(len(nodes))]
    return [list(range(len(nodes))), once, twice]


def pad8(n):
    return -(-n // 8) * 8


def band(out_at, in_at):
    k = np.arange(-HALF, HALF + 1)
    raw = 1.0 / np.cosh(math.pi * k / (2.0 * SPREAD))
    raw = raw / raw.sum()
    diff = in_at[None, :] - out_at[:, None]
    w = np.where(np.abs(diff) <= HALF, raw[np.clip(diff + HALF, 0, 2 * HALF)], 0.0)
    w = w.astype(np.float32)
    hi = w.astype(jnp.bfloat16)
    lo = (w - hi.astype(np.float32)).astype(jnp.bfloat16)
    return hi, lo


def split(x):
    hi = x.astype(BF16)
    lo = (x - hi.astype(F32)).astype(BF16)
    return hi, lo


def mm(a, b):
    return lax.dot_general(a, b, (((1,), (0,)), ((), ())), preferred_element_type=F32)


def mm_tn(a, b):
    return lax.dot_general(a, b, (((0,), (0,)), ((), ())), preferred_element_type=F32)


def mm_nt(a, b):
    return lax.dot_general(a, b, (((1,), (1,)), ((), ())), preferred_element_type=F32)


def iota(shape, dim):
    return lax.broadcasted_iota(jnp.int32, shape, dim)


def hot(mask):
    return jnp.where(mask, 1.0, 0.0).astype(BF16)


HBM = "hbm"


def call(body, outs, scratch, *args, micros, limit=20, held=()):
    def spec(in_hbm):
        return pl.BlockSpec(memory_space=pltpu.HBM if in_hbm else pltpu.VMEM)

    args = [
        pltpu.with_memory_space_constraint(a, pltpu.HBM) if i in held else a
        for i, a in enumerate(args)
    ]
    return pl.pallas_call(
        body,
        in_specs=[spec(i in held) for i in range(len(args))],
        out_specs=[spec(len(o) == 3) for o in outs],
        out_shape=[(pltpu.HBM if len(o) == 3 else jax.ShapeDtypeStruct)(o[0], o[1]) for o in outs],
        scratch_shapes=[pltpu.VMEM(*x) if isinstance(x, tuple) else x for x in scratch],
        compiler_params=pltpu.CompilerParams(vmem_limit_bytes=limit * 2**20),
        cost_estimate=pl.CostEstimate(
            flops=micros * 10**8, bytes_accessed=micros * 3 * 10**6, transcendentals=0
        ),
    )(*args)


def sems(count):
    return pltpu.SemaphoreType.DMA((count,))


def start(pairs, sem_ref, first=0):
    copies = [
        pltpu.make_async_copy(src, dst, sem_ref.at[first + i])
        for i, (src, dst) in enumerate(pairs)
    ]
    for copy in copies:
        copy.start()
    return copies


def finish(copies):
    for copy in copies:
        copy.wait()


def slots_of(basis):
    kb = -(-basis // 16) * 16
    row, col = iota((basis, 3 * kb), 0), iota((basis, 3 * kb), 1)
    return hot((col == row) | (col == kb + row)), hot(col == 2 * kb + row)


def prep_deriv(deriv_ref, w_ref):
    basis = deriv_ref.shape[1]
    sel_hi, sel_lo = slots_of(basis)
    parts = []
    for d in range(3):
        hi, lo = split(deriv_ref[d])
        parts.append(mm_tn(hi, sel_hi) + mm_tn(lo, sel_lo))
    w_ref[...] = jnp.concatenate(parts, axis=0).astype(BF16)


def staged(ref, stage_ref):
    for n in range(ref.shape[0]):
        stage_ref[n * 4 : (n + 1) * 4, :] = ref[n]
    return split(stage_ref[...])


def prep_trace(trace_ref, place_ref, stage_ref, wt_ref):
    sel_hi, sel_lo = slots_of(trace_ref.shape[2])
    hi, lo = staged(trace_ref, stage_ref)
    hi = mm(place_ref[...], hi).astype(BF16)
    lo = mm(place_ref[...], lo).astype(BF16)
    wt_ref[...] = (mm(hi, sel_hi) + mm(lo, sel_lo)).astype(BF16)


def prep_lift(lift_ref, stage_ref, wl_ref):
    nodes = lift_ref.shape[0]
    np_ = pad8(nodes)
    row, col = iota((4 * nodes, 8 * np_), 0), iota((4 * nodes, 8 * np_), 1)
    at = (row % 4) * np_ + row // 4
    sel = hot((col == at) | (col == 4 * np_ + at))
    hi, lo = staged(lift_ref, stage_ref)
    wl_ref[...] = jnp.concatenate([mm_tn(hi, sel), mm_tn(lo, sel)], axis=0).astype(BF16)


def stacked(x):
    rows = x.shape[0]
    pad = -(-rows // 16) * 16 - rows
    if pad:
        x = jnp.concatenate([x, jnp.zeros((pad, x.shape[1]), F32)], axis=0)
    hi, lo = split(x)
    return jnp.concatenate([hi, lo, hi], axis=0)


GROUP = 3


def mix(src_ref, first, w_ref, moved_ref):
    for v in range(first, first + GROUP):
        moved_ref[v] = mm(w_ref[...], stacked(src_ref[v]))


def combine(first, star_ref, moved_ref, total_ref, emit):
    variables, basis, elems = total_ref.shape
    for u0 in range(0, variables, GROUP):
        for h in range(elems // LANES):
            at = slice(h * LANES, (h + 1) * LANES)
            acc = [total_ref[u0 + i, :, at] if first else None for i in range(GROUP)]
            for v in range(first, first + GROUP):
                for d in range(3):
                    m = moved_ref[v, d * basis : (d + 1) * basis, at]
                    for i in range(GROUP):
                        part = star_ref[u0 + i, v, d : d + 1, at] * m
                        acc[i] = part if acc[i] is None else acc[i] + part
            for i in range(GROUP):
                if first + GROUP < variables:
                    total_ref[u0 + i, :, at] = acc[i]
                else:
                    emit(u0 + i, at, acc[i])


def derive(src_ref, star_ref, w_ref, moved_ref, total_ref, emit):
    variables = src_ref.shape[0]
    for first in range(0, variables, GROUP):
        if first + GROUP < variables:
            mix(src_ref, first + GROUP, w_ref, moved_ref)
        combine(first, star_ref, moved_ref, total_ref, emit)


def predict(star_ref, w_ref, moved_ref, term_ref, integ_ref, total_ref):
    integ_ref[...] = term_ref[...]
    mix(term_ref, 0, w_ref, moved_ref)

    def body(k, carry):
        scale = F32(-1.0 / ORDER)
        for o in range(1, ORDER - 1):
            scale = jnp.where(k == o, F32(-1.0 / (o + 1)), scale)

        def emit(u, at, acc):
            value = acc * scale
            term_ref[u, :, at] = value
            integ_ref[u, :, at] = integ_ref[u, :, at] + value

        derive(term_ref, star_ref, w_ref, moved_ref, total_ref, emit)
        mix(term_ref, 0, w_ref, moved_ref)
        return carry

    lax.fori_loop(1, ORDER, body, 0)


def traces(integ_ref, wt_ref, own_refs):
    variables, _, elems = integ_ref.shape
    np_ = wt_ref.shape[0] // 12
    count = len(own_refs)
    for v in range(variables):
        t = mm(wt_ref[0 : count * 4 * np_, :], stacked(integ_ref[v]))
        for r in range(count):
            for f in range(4):
                own_refs[r][v * np_ : (v + 1) * np_, f * elems : (f + 1) * elems] = t[
                    (r * 4 + f) * np_ : (r * 4 + f + 1) * np_
                ]
    rows = own_refs[0].shape[0]
    for r in range(count):
        if rows > variables * np_:
            own_refs[r][variables * np_ :, :] = jnp.zeros(
                (rows - variables * np_, 4 * elems), F32
            )


def send_gather(own_ref, send_ref, left_ref, outs):
    rows, faces = own_ref.shape
    hi, lo = split(own_ref[...])
    left_ref[0:rows] = hi
    left_ref[rows : 2 * rows] = lo
    slots = send_ref.shape[3]
    for k in range(0, 4, 2):
        picks = jnp.concatenate([send_ref[0, 0, k : k + 1], send_ref[0, 0, k + 1 : k + 2]], axis=1)
        res = mm(left_ref[...], hot(iota((faces, 2 * slots), 0) == picks))
        res = res[:rows] + res[rows:]
        outs[k][0:rows] = res[:, :slots]
        outs[k + 1][0:rows] = res[:, slots:]


def row_of(ref):
    return jnp.concatenate([ref[f : f + 1, :] for f in range(ref.shape[0])], axis=1)


def local_jump(own_refs, source_turn, codes, left_ref, jump_ref):
    rows, faces = own_refs[0].shape
    width = faces // 4
    value = jnp.where(
        source_turn == 1.0,
        own_refs[1][...],
        jnp.where(source_turn == 2.0, own_refs[2][...], own_refs[0][...]),
    )
    hi, lo = split(value)
    left_ref[0:rows] = hi
    left_ref[rows : 2 * rows] = lo
    for q in range(4):
        at = slice(q * width, (q + 1) * width)
        res = mm(left_ref[...], hot(iota((faces, width), 0) == codes[:, at]))
        jump_ref[:, at] = own_refs[0][:, at] - (res[:rows] + res[rows:])


def surface(arrived, slot_turn, codes, jump_ref, flux_m_ref, perm_ref, wl_ref, base_ref, scratch, out_ref):
    left_ref, part_ref, flux_ref = scratch
    rows, faces = jump_ref.shape
    variables, basis, elems = base_ref.shape
    value = jnp.concatenate(arrived, axis=1)
    slots = value.shape[1]
    hi, lo = split(value)
    both = jnp.concatenate([hi, lo], axis=1)
    turned = mm(perm_ref[...], both)
    turn = jnp.concatenate([slot_turn, slot_turn], axis=1)
    chosen = jnp.where(
        turn == 1.0, turned[:rows], jnp.where(turn == 2.0, turned[rows:], both.astype(F32))
    ).astype(BF16)
    left_ref[0:rows] = chosen[:, :slots]
    left_ref[rows : 2 * rows] = chosen[:, slots:]
    for q in range(4):
        at = slice(q * elems, (q + 1) * elems)
        res = mm(left_ref[...], hot(iota((slots, elems), 0) + faces == codes[:, at]))
        part_ref[:, at] = jump_ref[:, at] - (res[:rows] + res[rows:])
    np_ = flux_ref.shape[1] // 4

    group = 3

    def body(g, carry):
        for f in range(4):
            for h in range(elems // LANES):
                here = slice(h * LANES, (h + 1) * LANES)
                wide = slice(f * elems + h * LANES, f * elems + (h + 1) * LANES)
                acc = [jnp.zeros((np_, LANES), F32) for _ in range(group)]
                for v in range(variables):
                    jump = part_ref[v * np_ : (v + 1) * np_, wide]
                    for i in range(group):
                        acc[i] = acc[i] + flux_m_ref[g * group + i, v, f : f + 1, here] * jump
                for i in range(group):
                    flux_ref[g * group + i, f * np_ : (f + 1) * np_, here] = acc[i]
        return carry

    lax.fori_loop(0, variables // group, body, 0)
    for u in range(variables):
        hi, lo = split(flux_ref[u])
        res = mm(wl_ref[...], jnp.concatenate([hi, lo], axis=0))
        out_ref[u] = base_ref[u] - (res[:basis] + res[basis:])


def first_kernel(
    state_hbm, star_hbm, deriv_hbm, trace_hbm, place_hbm, send_hbm, sea_hbm, depth_hbm, wet_hbm,
    w_ref, wt_ref, integ_ref, lifted_ref, o0, o1, o2, o3,
    star_ref, deriv_ref, trace_ref, place_ref, send_ref, own_ref,
    moved_ref, term_ref, total_ref, left_ref, stage_ref, sea_edge, depth_edge, wet_edge, sem_ref,
):
    urgent = start(
        [(deriv_hbm, deriv_ref), (state_hbm, term_ref), (star_hbm, star_ref)], sem_ref
    )
    later = start(
        [(trace_hbm, trace_ref), (place_hbm, place_ref), (send_hbm, send_ref)], sem_ref, 3
    )
    tall = depth_hbm.shape[0]
    pairs = []
    for side, at in enumerate((pl.ds(0, EDGE), pl.ds(tall - EDGE, EDGE))):
        for j in range(3):
            pairs.append((sea_hbm.at[j, at], sea_edge.at[side, j]))
        pairs.append((depth_hbm.at[at], depth_edge.at[side]))
        pairs.append((wet_hbm.at[at], wet_edge.at[side]))
    later = later + start(pairs, sem_ref, 6)
    finish(urgent[:1])
    prep_deriv(deriv_ref, w_ref)
    finish(urgent[1:])
    predict(star_ref, w_ref, moved_ref, term_ref, integ_ref, total_ref)
    finish(later)
    prep_trace(trace_ref, place_ref, stage_ref, wt_ref)
    traces(integ_ref, wt_ref, (own_ref,))
    send_gather(own_ref, send_ref, left_ref, (o0, o1, o2, o3))
    rows = own_ref.shape[0]
    np_ = lifted_ref.shape[0]
    lifted_ref[...] = own_ref[2 * np_ : 3 * np_, :]
    for side, (out, at) in enumerate(((o0, 0), (o1, EDGE - STEPS))):
        for j in range(5):
            if j < 3:
                edge = sea_edge[side, j]
            else:
                edge = depth_edge[side] if j == 3 else wet_edge[side].astype(F32)
            for h in range(edge.shape[1] // LANES):
                begin = rows + h * SEA_ROWS + j * STEPS
                out[begin : begin + STEPS] = edge[
                    at : at + STEPS, h * LANES : (h + 1) * LANES
                ]


def local_work(
    integ_ref, field_ref, star_ref, w_ref, wt_ref, turn, codes, jump_ref, base_ref,
    own_refs, left_ref, moved_ref, total_ref,
):
    traces(integ_ref, wt_ref, own_refs)
    local_jump(own_refs, turn, codes, left_ref, jump_ref)

    def emit(u, at, acc):
        base_ref[u, :, at] = field_ref[u, :, at] - acc

    mix(integ_ref, 0, w_ref, moved_ref)
    derive(integ_ref, star_ref, w_ref, moved_ref, total_ref, emit)


def local_first_kernel(
    integ_ref, field_ref, star_ref, w_ref, wt_ref, codes_ref, orient_ref, lift_ref,
    jump_ref, base_ref, slot_ref, wl_ref, turn_out, slot_out, wl_out, w_out, wt_out,
    turn_ref, own0, own1, own2, left_ref, moved_ref, total_ref, stage_ref, sem_ref,
):
    prep_lift(lift_ref, stage_ref, wl_ref)
    codes = row_of(codes_ref)
    faces = codes.shape[1]
    slots = slot_ref.shape[1]
    turns = jnp.broadcast_to(row_of(orient_ref).astype(F32), (16, faces)).astype(BF16)
    width = faces // 4
    for q in range(4):
        at = slice(q * width, (q + 1) * width)
        turn_ref[:, at] = mm(turns, hot(iota((faces, width), 0) == codes[:, at]))[0:8]
    for q in range(slots // LANES):
        at = slice(q * LANES, (q + 1) * LANES)
        wanted = iota((LANES, faces), 0) + (faces + q * LANES)
        slot_ref[:, at] = mm_nt(turns, hot(wanted == codes))[0:8]
    copies = start(
        [(turn_ref, turn_out), (slot_ref, slot_out), (wl_ref, wl_out), (w_ref, w_out),
         (wt_ref, wt_out)], sem_ref,
    )
    local_work(
        integ_ref, field_ref, star_ref, w_ref, wt_ref, turn_ref[0:1, :], codes, jump_ref, base_ref,
        (own0, own1, own2), left_ref, moved_ref, total_ref,
    )
    finish(copies)


def second_kernel(
    capacity, nodes,
    a0, a1, a2, a3, slot_ref, codes_ref, jump_ref, flux_m_ref, perm_ref, wl_ref, base_ref,
    star_ref, w_ref, wt_ref, send_ref, lifted_ref, faces_ref, owner_ref, blocks_ref, weights_ref,
    pay_ref, field_out, integ_out, edge_low, edge_high, s0, s1, s2, s3,
    field_ref, integ_ref, own_ref, o0, o1, o2, o3,
    arr_left_ref, part_ref, flux_ref, moved_ref, term_ref, total_ref, left_ref,
    disp_ref, rows_ref, sem_ref,
):
    rows = jump_ref.shape[0]
    tail = pl.ds(rows, a0.shape[0] - rows)
    copies = start([(a0.at[tail], edge_low), (a1.at[tail], edge_high)], sem_ref)
    surface(
        [a[0:rows] for a in (a0, a1, a2, a3)], slot_ref[0:1, :], row_of(codes_ref), jump_ref,
        flux_m_ref, perm_ref, wl_ref, base_ref, (arr_left_ref, part_ref, flux_ref), field_ref,
    )
    copies += start([(field_ref, field_out)], sem_ref, 2)
    term_ref[...] = field_ref[...]
    predict(star_ref, w_ref, moved_ref, term_ref, integ_ref, total_ref)
    copies += start([(integ_ref, integ_out)], sem_ref, 3)
    traces(integ_ref, wt_ref, (own_ref,))
    send_gather(own_ref, send_ref, left_ref, (o0, o1, o2, o3))
    copies += start([(o0, s0), (o1, s1), (o2, s2), (o3, s3)], sem_ref, 4)
    np_ = lifted_ref.shape[0]
    project(
        capacity, nodes, lifted_ref[...], own_ref[2 * np_ : 3 * np_, :], faces_ref, owner_ref,
        blocks_ref, weights_ref, pay_ref, disp_ref, rows_ref,
    )
    finish(copies)


def local_second_kernel(
    integ_hbm, field_hbm, star_hbm, w_hbm, wt_hbm, turn_hbm, codes_hbm,
    jump_out, base_out,
    integ_ref, field_ref, star_ref, w_ref, wt_ref, turn_ref, codes_ref, jump_ref, base_ref,
    own0, own1, own2, left_ref, moved_ref, total_ref, sem_ref,
):
    copies = start(
        [(integ_hbm, integ_ref), (wt_hbm, wt_ref), (turn_hbm, turn_ref), (codes_hbm, codes_ref),
         (star_hbm, star_ref), (w_hbm, w_ref), (field_hbm, field_ref)], sem_ref,
    )
    finish(copies)
    local_work(
        integ_ref, field_ref, star_ref, w_ref, wt_ref, turn_ref[0:1, :], row_of(codes_ref),
        jump_ref, base_ref, (own0, own1, own2), left_ref, moved_ref, total_ref,
    )
    finish(start([(jump_ref, jump_out), (base_ref, base_out)], sem_ref, 7))


def last_kernel(
    a0, a1, a2, a3, slot_hbm, codes_hbm, jump_hbm, flux_m_hbm, perm_hbm, wl_hbm, base_hbm,
    field_out,
    b0, b1, b2, b3, slot_ref, codes_ref, jump_ref, flux_m_ref, perm_ref, wl_ref, base_ref,
    field_ref, arr_left_ref, part_ref, flux_ref, sem_ref,
):
    copies = start(
        [(a0, b0), (a1, b1), (a2, b2), (a3, b3), (slot_hbm, slot_ref), (perm_hbm, perm_ref),
         (codes_hbm, codes_ref), (jump_hbm, jump_ref), (flux_m_hbm, flux_m_ref),
         (wl_hbm, wl_ref), (base_hbm, base_ref)], sem_ref,
    )
    finish(copies)
    surface(
        [b0[...], b1[...], b2[...], b3[...]], slot_ref[0:1, :], row_of(codes_ref), jump_ref,
        flux_m_ref, perm_ref, wl_ref, base_ref, (arr_left_ref, part_ref, flux_ref), field_ref,
    )
    finish(start([(field_ref, field_out)], sem_ref))


def project(
    capacity, nodes, own_a, own_b, faces_ref, owner_ref, blocks_ref, weights_ref, pay_ref,
    disp_ref, rows_ref,
):
    np_ = pad8(nodes)
    faces = own_a.shape[1]
    sea_rows, _ = weights_ref.shape[1:]
    both = jnp.concatenate([own_a, own_b], axis=0)
    hi, lo = split(both)
    picks = hot(iota((faces, sea_rows), 0) == faces_ref[...])
    disp = mm(jnp.concatenate([hi, lo], axis=0), picks)
    disp = disp[: 2 * np_] + disp[2 * np_ :]
    disp = jnp.concatenate([disp, jnp.zeros((LANES - 2 * np_, sea_rows), F32)], axis=0)
    disp_ref[...] = disp.T
    across = jnp.broadcast_to(owner_ref[...].astype(F32), (sea_rows, sea_rows))
    owner = across.T
    earlier = iota((sea_rows, sea_rows), 0) < iota((sea_rows, sea_rows), 1)
    rank = jnp.sum(jnp.where((owner == across) & earlier, 1.0, 0.0), axis=0, keepdims=True)
    place = (across[0:1, :] * float(capacity) + rank).astype(jnp.int32)
    devs = pay_ref.shape[0]
    total = devs * capacity
    put = hot(iota((total, sea_rows), 0) == place)
    chunk = 32

    def body(c, carry):
        here = pl.ds(pl.multiple_of(c * chunk, chunk), chunk)
        cols = disp_ref[here, :]
        for t in range(STEPS):
            acc = cols[:, t * np_ : t * np_ + 1] * weights_ref[0, here, :]
            for n in range(1, nodes):
                acc = acc + cols[:, t * np_ + n : t * np_ + n + 1] * weights_ref[n, here, :]
            rows_ref[t, here, :] = acc
        return carry

    lax.fori_loop(0, sea_rows // chunk, body, 0)
    twice = jnp.concatenate([put, put], axis=1)
    parts = []
    for t in range(STEPS):
        hi, lo = split(rows_ref[t])
        parts.append(mm(twice, jnp.concatenate([hi, lo], axis=0)))
    labels = jnp.broadcast_to(blocks_ref[...].astype(F32), (LANES, sea_rows)).astype(BF16)
    parts.append(mm_nt(put, labels))
    value = jnp.concatenate(parts, axis=1)
    for d in range(devs):
        pay_ref[d] = value[d * capacity : (d + 1) * capacity]


def raster_kernel(
    pay_ref, b_hi_hbm, b_lo_hbm, right_hbm, left_hbm,
    uplift_ref, up_ref, down_ref, b_hi, b_lo, right_ref, left_ref, got_ref, sem_ref,
):
    later = start(
        [(b_hi_hbm, b_hi), (b_lo_hbm, b_lo), (right_hbm, right_ref), (left_hbm, left_ref)],
        sem_ref,
    )
    devs, capacity, _ = pay_ref.shape
    total = devs * capacity
    for d in range(devs):
        got_ref[d * capacity : (d + 1) * capacity] = pay_ref[d]
    tile_x, tile_y = uplift_ref.shape[1:]
    across = tile_y // BS
    cells = BS * BS
    blocks = (tile_x // BS) * across
    labels = got_ref[:, STEPS * cells :].T
    pick = hot(iota((blocks, total), 0) == labels[0:1, :].astype(jnp.int32))
    pick = jnp.concatenate([pick, pick], axis=1)
    by = iota((blocks, cells), 0) % across
    cx = iota((blocks, cells), 1) // BS
    for t in range(STEPS):
        hi, lo = split(got_ref[:, t * cells : (t + 1) * cells])
        x = mm(pick, jnp.concatenate([hi, lo], axis=0))
        step = 1
        while step < BS:
            from_above = pltpu.roll(pltpu.roll(x, blocks - step, 0), BS * step, 1)
            from_below = pltpu.roll(pltpu.roll(x, step, 0), cells - BS * step, 1)
            low_row = (by & step) == 0
            low_col = (cx & step) == 0
            x = jnp.where(low_row == low_col, x, jnp.where(low_row, from_above, from_below))
            step *= 2
        uplift_ref[t] = x
        up_ref[t * HALO_X : (t + 1) * HALO_X] = x[tile_x - HALO_X :, :]
        down_ref[t * HALO_X : (t + 1) * HALO_X] = x[:HALO_X, :]
    finish(later)


def shore_kernel(
    axes, sea_hbm, depth_hbm, wet_hbm, low_hbm, high_hbm,
    ext_out, right_out, left_out,
    ext_ref, wet_ref, low_ref, high_ref, right_ref, left_ref, sem_ref,
):
    tile_x, tile_y = depth_hbm.shape
    body = pl.ds(0, tile_x)
    finish(
        start(
            [(sea_hbm.at[j], ext_ref.at[j, body]) for j in range(3)]
            + [(depth_hbm, ext_ref.at[3, body]), (wet_hbm, wet_ref), (low_hbm, low_ref),
               (high_hbm, high_ref)], sem_ref,
        )
    )
    ext_ref[4, 0:tile_x, :] = wet_ref[...].astype(F32)
    at_x = lax.axis_index(axes[0])
    has_low = at_x > 0
    has_high = at_x < lax.axis_size(axes[0]) - 1

    def edge_of(ref, present, j, before):
        halves = []
        for h in range(tile_y // LANES):
            begin = h * SEA_ROWS + j * STEPS
            halves.append(ref[begin : begin + STEPS, :])
        value = jnp.where(present, jnp.concatenate(halves, axis=1), 0.0)
        blank = jnp.zeros((EDGE - STEPS, tile_y), F32)
        return jnp.concatenate([blank, value] if before else [value, blank], axis=0)

    for j in range(5):
        ext_ref[j, tile_x : tile_x + EDGE, :] = edge_of(high_ref, has_high, j, False)
        ext_ref[j, tile_x + EDGE : tile_x + 2 * EDGE, :] = edge_of(low_ref, has_low, j, True)
    copies = start([(ext_ref, ext_out)], sem_ref)
    lane = iota(right_ref.shape, 1)
    right = jnp.zeros(right_ref.shape, F32)
    left = right
    for j in range(5):
        moved = 2 * HALO_Y + 2 * j
        last = ext_ref[j, :, tile_y - LANES :]
        first = ext_ref[j, :, :LANES]
        right = jnp.where(
            lane >= LANES - moved, right, pltpu.roll(last, LANES - moved, 1)
        )
        left = jnp.where(lane < moved, left, pltpu.roll(first, moved, 1))
    right_ref[...] = right
    left_ref[...] = left
    finish(copies + start([(right_ref, right_out), (left_ref, left_out)], sem_ref, 1))


def along_x_kernel(
    axes, uplift_ref, low_ref, high_ref, b_hi, b_lo, sea_right, sea_left,
    along_ref, right_ref, left_ref,
):
    _, tile_y = uplift_ref.shape[1:]
    at_x = lax.axis_index(axes[0])
    has_low = at_x > 0
    has_high = at_x < lax.axis_size(axes[0]) - 1
    for t in range(STEPS):
        at = slice(t * HALO_X, (t + 1) * HALO_X)
        value = jnp.concatenate(
            [
                uplift_ref[t],
                jnp.where(has_high, high_ref[at, :], 0.0),
                jnp.where(has_low, low_ref[at, :], 0.0),
            ],
            axis=0,
        )
        hi, lo = split(value)
        along_ref[t] = mm(b_hi[...], hi) + mm(b_hi[...], lo) + mm(b_lo[...], hi)
    tall = along_ref.shape[1]
    lane = iota((tall, LANES), 1)
    last = slice(tile_y - LANES, tile_y)
    first = slice(0, LANES)
    right, left = sea_right[...], sea_left[...]
    for t in reversed(range(STEPS)):
        moved = t * HALO_Y
        tail = along_ref[t, :, last]
        head = along_ref[t, :, first]
        if t:
            tail, head = pltpu.roll(tail, LANES - moved, 1), pltpu.roll(head, moved, 1)
        right = jnp.where(lane >= LANES - moved - HALO_Y, tail, right)
        left = jnp.where(lane < moved + HALO_Y, head, left)
    right_ref[...] = right
    left_ref[...] = left


def ocean_kernel(axes, along_ref, ext_ref, low_ref, high_ref, b_hi, b_lo, out_ref):
    tall, tile_y = along_ref.shape[1:]
    tile_x = out_ref.shape[1]
    at_y = lax.axis_index(axes[1])
    low = jnp.where(at_y > 0, low_ref[...], 0.0)
    high = jnp.where(at_y < lax.axis_size(axes[1]) - 1, high_ref[...], 0.0)
    lane = iota((tall, LANES), 1)
    forces = []
    for t in range(STEPS):
        right = pltpu.roll(high, LANES - HALO_Y, 1) if t else high
        left = pltpu.roll(low, HALO_Y, 1) if t else low
        value = jnp.concatenate([along_ref[t], right, left], axis=1)
        hi, lo = split(value)
        forces.append(mm(hi, b_hi[...]) + mm(lo, b_hi[...]) + mm(hi, b_lo[...]))
    fields = []
    for j in range(5):
        moved = 2 * HALO_Y + 2 * j
        edge = jnp.where(
            lane < LANES // 2, pltpu.roll(high, LANES - moved, 1), pltpu.roll(low, moved, 1)
        )
        fields.append(jnp.concatenate([ext_ref[j], edge], axis=1))
    eta, east, north, depth, wet = fields
    rows, cols = eta.shape

    def px(x):
        return pltpu.roll(x, rows - 1, 0)

    def mx(x):
        return pltpu.roll(x, 1, 0)

    def py(x):
        return pltpu.roll(x, cols - 1, 1)

    def my(x):
        return pltpu.roll(x, 1, 1)

    factor = 0.5 * COURANT
    for t in range(STEPS):
        eta = eta + wet * forces[t]
        column = depth + eta
        qx, qy = column * east, column * north
        near = [(px(a), mx(a), py(a), my(a)) for a in (eta, east, north)]
        mean = [0.25 * (a + b + c + d) for a, b, c, d in near]
        eta_x, eta_y = near[0][0] - near[0][1], near[0][2] - near[0][3]
        east_x, east_y = near[1][0] - near[1][1], near[1][2] - near[1][3]
        north_x, north_y = near[2][0] - near[2][1], near[2][2] - near[2][3]
        eta_new = mean[0] - factor * ((px(qx) - mx(qx)) + (py(qy) - my(qy)))
        east_new = mean[1] - factor * (east * east_x + north * east_y + eta_x)
        north_new = mean[2] - factor * (east * north_x + north * north_y + eta_y)
        eta, east, north = eta_new * wet, east_new * wet, north_new * wet
    out_ref[0] = eta[:tile_x, :tile_y]
    out_ref[1] = east[:tile_x, :tile_y]
    out_ref[2] = north[:tile_x, :tile_y]


def shift(value, axis, step):
    count = lax.axis_size(axis)
    return lax.ppermute(value, axis, [(i, (i + step) % count) for i in range(count)])


def on_device(
    state, star, deriv, trace_ops, lift, face_flux, orient, neighbours, send_faces,
    sea_faces, sea_owner, sea_blocks, sea_weights, depth, wet, sea_state,
):
    variables, basis, elems = state.shape
    nodes = trace_ops.shape[2]
    np_ = pad8(nodes)
    faces = 4 * elems
    slots = send_faces.shape[-1]
    rows = -(-variables * np_ // 16) * 16
    kb = -(-basis // 16) * 16
    turns = node_turns()
    place = np.zeros((12 * np_, 4 * nodes), np.float32)
    perm = np.zeros((2 * rows, rows), np.float32)
    for r in range(3):
        for n in range(nodes):
            for f in range(4):
                place[(r * 4 + f) * np_ + n, turns[r][n] * 4 + f] = 1.0
            for v in range(variables):
                if r:
                    perm[(r - 1) * rows + v * np_ + n, v * np_ + turns[r][n]] = 1.0
    place = jnp.asarray(place, BF16)
    perm = jnp.asarray(perm, BF16)
    star = star.transpose(1, 2, 0, 3)
    face_flux = face_flux.transpose(1, 2, 0, 3)
    trace_ops = trace_ops.transpose(2, 0, 1)
    lift = lift.transpose(1, 0, 2)

    wide = (rows, faces)
    out = (rows, slots)
    tile_x, tile_y = depth.shape
    out_x = (rows + (tile_y // LANES) * SEA_ROWS, slots)
    field_shape = (variables, basis, elems)
    moved = ((variables, 3 * basis, elems), F32)
    left = ((2 * rows, faces), BF16)
    arr_left = ((2 * rows, 4 * slots), BF16)
    flux = ((variables, 4 * np_, elems), F32)
    stage = ((4 * nodes, basis), F32)

    def sent(outgoing):
        return [
            shift(outgoing[1], "gx", 1), shift(outgoing[0], "gx", -1),
            shift(outgoing[3], "gy", 1), shift(outgoing[2], "gy", -1),
        ]

    w_of = ((3 * basis, 3 * kb), BF16)
    wt_of = ((12 * np_, 3 * kb), BF16)
    wl_of = ((2 * basis, 8 * np_), BF16)
    turn_of = ((8, faces), F32)
    slot_of = ((8, 4 * slots), F32)
    field_of, wide_of, out_of = (field_shape, F32), (wide, F32), (out, F32)
    star_of, flux_m_of = (star.shape, F32), (face_flux.shape, F32)
    lifted_of = ((np_, faces), F32)
    codes_of = (neighbours.shape, neighbours.dtype)
    perm_of = (perm.shape, BF16)

    def hbm(array):
        return (*array, HBM)

    w, wt, integ, lifted_a, *outgoing = call(
        first_kernel,
        [w_of, wt_of, field_of, lifted_of] + [(out_x, F32)] * 2 + [out_of] * 2,
        [star_of, (deriv.shape, F32), (trace_ops.shape, F32), (place.shape, BF16),
         (send_faces.shape, send_faces.dtype), wide_of, moved, field_of, field_of, left, stage,
         ((2, 3, EDGE, tile_y), F32), ((2, EDGE, tile_y), F32), ((2, EDGE, tile_y), wet.dtype),
         sems(16)],
        state, star, deriv, trace_ops, place, send_faces, sea_state, depth, wet,
        micros=10, held=range(9),
    )
    arrived = sent(outgoing)
    jump, base, slot_turn, wl, turn_h, slot_h, wl_h, w_h, wt_h = call(
        local_first_kernel,
        [wide_of, field_of, slot_of, wl_of, hbm(turn_of), hbm(slot_of), hbm(wl_of), hbm(w_of),
         hbm(wt_of)],
        [turn_of, wide_of, wide_of, wide_of, left, moved, field_of, stage, sems(5)],
        integ, state, star, w, wt, neighbours, orient, lift,
        micros=4,
    )
    sea_rows, cells = sea_weights.shape[1:]
    devs = lax.axis_size("gx") * lax.axis_size("gy")
    capacity = max(2, (sea_rows + devs - 1) // devs)
    message = (devs, capacity, STEPS * cells + LANES)
    payload, field_h, integ_h, edge_low, edge_high, *outgoing = call(
        lambda *refs: second_kernel(capacity, nodes, *refs),
        [(message, F32), hbm(field_of), hbm(field_of)]
        + [((out_x[0] - rows, slots), F32, HBM)] * 2 + [hbm(out_of)] * 4,
        [field_of, field_of, wide_of] + [out_of] * 4
        + [arr_left, wide_of, flux, moved, field_of, field_of, left,
           ((sea_rows, LANES), F32), ((STEPS, sea_rows, cells), F32), sems(8)],
        *arrived, slot_turn, neighbours, jump, face_flux, perm, wl, base, star, w, wt,
        send_faces, lifted_a, sea_faces.reshape(1, -1), sea_owner.reshape(1, -1),
        sea_blocks.reshape(1, -1), sea_weights, micros=12,
    )
    got = lax.all_to_all(payload, ("gx", "gy"), split_axis=0, concat_axis=0, tiled=True)
    arrived = sent(outgoing)
    tall = tile_x + 2 * EDGE
    axes = ("gx", "gy")
    ext_of = ((5, tall, tile_y), F32)
    strip_of = ((tall, LANES), F32)
    edge_of = (edge_low.shape, F32)
    ext_h, right_h, left_h = call(
        lambda *refs: shore_kernel(axes, *refs),
        [hbm(ext_of), hbm(strip_of), hbm(strip_of)],
        [ext_of, (wet.shape, wet.dtype), edge_of, edge_of, strip_of, strip_of, sems(7)],
        sea_state, depth, wet, edge_low, edge_high, micros=2, held=range(5),
    )
    jump_h, base_h = call(
        local_second_kernel, [hbm(wide_of), hbm(field_of)],
        [field_of, field_of, star_of, w_of, wt_of, turn_of, codes_of, wide_of, field_of,
         wide_of, wide_of, wide_of, left, moved, field_of, sems(9)],
        integ_h, field_h, star, w_h, wt_h, turn_h, neighbours,
        micros=5, held=range(7),
    )
    elastic, = call(
        last_kernel, [hbm(field_of)],
        [out_of] * 4 + [slot_of, codes_of, wide_of, flux_m_of, perm_of, wl_of, field_of, field_of,
         arr_left, wide_of, flux, sems(11)],
        *arrived, slot_h, neighbours, jump_h, face_flux, perm, wl_h, base_h,
        micros=4, held=range(11),
    )

    halo = ((STEPS * HALO_X, tile_y), F32)
    cell_x = np.concatenate([np.arange(tile_x + EDGE), np.arange(-EDGE, 0)])
    read_x = np.concatenate([np.arange(tile_x + HALO_X), np.arange(-HALO_X, 0)])
    cell_y = np.concatenate([np.arange(tile_y + LANES // 2), np.arange(-LANES // 2, 0)])
    read_y = np.concatenate([np.arange(tile_y + LANES), np.arange(-LANES, 0)])
    bx = [jnp.asarray(b) for b in band(cell_x, read_x)]
    by = [jnp.asarray(b.T) for b in band(cell_y, read_y)]
    uplift, up, down, bx_hi, bx_lo, sea_right, sea_left = call(
        raster_kernel,
        [((STEPS, tile_x, tile_y), F32), halo, halo]
        + [(b.shape, BF16) for b in bx] + [strip_of, strip_of],
        [((devs * capacity, message[2]), F32), sems(4)],
        got, *bx, right_h, left_h, micros=2, held=range(1, 5),
    )
    x_low, x_high = shift(up, "gx", 1), shift(down, "gx", -1)
    along, right, left_going = call(
        lambda *refs: along_x_kernel(axes, *refs),
        [((STEPS, tall, tile_y), F32), strip_of, strip_of], [],
        uplift, x_low, x_high, bx_hi, bx_lo, sea_right, sea_left, micros=1,
    )
    y_low, y_high = shift(right, "gy", 1), shift(left_going, "gy", -1)
    ocean, = call(
        lambda *refs: ocean_kernel(axes, *refs), [((3, tile_x, tile_y), F32)], [],
        along, ext_h, y_low, y_high, *by, micros=4,
    )
    return elastic, ocean


def solution(mesh):
    both = ("gx", "gy")
    placed = (
        P(None, None, both),
        P(None, None, None, both),
        P(),
        P(),
        P(),
        P(None, None, None, both),
        P(None, both),
        P(None, both),
        P("gx", "gy", None, None),
        P(both),
        P(both, None),
        P(both),
        P(None, both, None),
        P("gx", "gy"),
        P("gx", "gy"),
        P(None, "gx", "gy"),
    )

    return jax.shard_map(
        on_device,
        mesh=mesh,
        in_specs=placed,
        out_specs=(P(None, None, both), P(None, "gx", "gy")),
        check_vma=False,
    )
```

```python
import math

import jax
import jax.numpy as jnp
import numpy as np
from jax import lax
from jax.experimental import pallas as pl
from jax.experimental.pallas import tpu as pltpu
from jax.sharding import PartitionSpec as P


ORDER = 6
STEPS = 2
BS = 16
HALF = 32
SPREAD = 8.0
COURANT = 0.25
LANES = 128
HALO_X = 40
HALO_Y = 34
EDGE = 8
SEA_ROWS = 16
F32 = jnp.float32
BF16 = jnp.bfloat16


def node_turns():
    upper = ORDER - 1
    nodes = [(i, j) for i in range(upper + 1) for j in range(upper + 1 - i)]
    once = [nodes.index((pair[1], upper - pair[0] - pair[1])) for pair in nodes]
    twice = [once[once[number]] for number in range(len(nodes))]
    return [list(range(len(nodes))), once, twice]


def pad8(n):
    return -(-n // 8) * 8


def band(out_at, in_at):
    k = np.arange(-HALF, HALF + 1)
    raw = 1.0 / np.cosh(math.pi * k / (2.0 * SPREAD))
    raw = raw / raw.sum()
    diff = in_at[None, :] - out_at[:, None]
    w = np.where(np.abs(diff) <= HALF, raw[np.clip(diff + HALF, 0, 2 * HALF)], 0.0)
    w = w.astype(np.float32)
    hi = w.astype(jnp.bfloat16)
    lo = (w - hi.astype(np.float32)).astype(jnp.bfloat16)
    return hi, lo


def split(x):
    hi = x.astype(BF16)
    lo = (x - hi.astype(F32)).astype(BF16)
    return hi, lo


def mm(a, b):
    return lax.dot_general(a, b, (((1,), (0,)), ((), ())), preferred_element_type=F32)


def mm_tn(a, b):
    return lax.dot_general(a, b, (((0,), (0,)), ((), ())), preferred_element_type=F32)


def mm_nt(a, b):
    return lax.dot_general(a, b, (((1,), (1,)), ((), ())), preferred_element_type=F32)


def iota(shape, dim):
    return lax.broadcasted_iota(jnp.int32, shape, dim)


def hot(mask):
    return jnp.where(mask, 1.0, 0.0).astype(BF16)


HBM = "hbm"


def call(body, outs, scratch, *args, micros, limit=20, held=(), flags=None):
    def spec(in_hbm):
        return pl.BlockSpec(memory_space=pltpu.HBM if in_hbm else pltpu.VMEM)

    args = [
        pltpu.with_memory_space_constraint(a, pltpu.HBM) if i in held else a
        for i, a in enumerate(args)
    ]
    return pl.pallas_call(
        body,
        in_specs=[spec(i in held) for i in range(len(args))],
        out_specs=[spec(len(o) == 3) for o in outs],
        out_shape=[(pltpu.HBM if len(o) == 3 else jax.ShapeDtypeStruct)(o[0], o[1]) for o in outs],
        scratch_shapes=[pltpu.VMEM(*x) if isinstance(x, tuple) else x for x in scratch],
        compiler_params=pltpu.CompilerParams(
            vmem_limit_bytes=limit * 2**20, **({"flags": flags} if flags else {})
        ),
        cost_estimate=pl.CostEstimate(
            flops=micros * 10**8, bytes_accessed=micros * 3 * 10**6, transcendentals=0
        ),
    )(*args)


def sems(count):
    return pltpu.SemaphoreType.DMA((count,))


def start(pairs, sem_ref, first=0):
    copies = [
        pltpu.make_async_copy(src, dst, sem_ref.at[first + i])
        for i, (src, dst) in enumerate(pairs)
    ]
    for copy in copies:
        copy.start()
    return copies


def finish(copies):
    for copy in copies:
        copy.wait()


def slots_of(basis):
    kb = -(-basis // 16) * 16
    row, col = iota((basis, 3 * kb), 0), iota((basis, 3 * kb), 1)
    return hot((col == row) | (col == kb + row)), hot(col == 2 * kb + row)


def prep_deriv(deriv_ref, w_ref):
    basis = deriv_ref.shape[1]
    sel_hi, sel_lo = slots_of(basis)
    parts = []
    for d in range(3):
        hi, lo = split(deriv_ref[d])
        parts.append(mm_tn(hi, sel_hi) + mm_tn(lo, sel_lo))
    w_ref[...] = jnp.concatenate(parts, axis=0).astype(BF16)


def staged(ref, stage_ref):
    for n in range(ref.shape[0]):
        stage_ref[n * 4 : (n + 1) * 4, :] = ref[n]
    return split(stage_ref[...])


def prep_trace(trace_ref, place_ref, stage_ref, wt_ref):
    sel_hi, sel_lo = slots_of(trace_ref.shape[2])
    hi, lo = staged(trace_ref, stage_ref)
    hi = mm(place_ref[...], hi).astype(BF16)
    lo = mm(place_ref[...], lo).astype(BF16)
    wt_ref[...] = (mm(hi, sel_hi) + mm(lo, sel_lo)).astype(BF16)


def prep_lift(lift_ref, stage_ref, wl_ref):
    nodes = lift_ref.shape[0]
    np_ = pad8(nodes)
    row, col = iota((4 * nodes, 8 * np_), 0), iota((4 * nodes, 8 * np_), 1)
    at = (row % 4) * np_ + row // 4
    sel = hot((col == at) | (col == 4 * np_ + at))
    hi, lo = staged(lift_ref, stage_ref)
    wl_ref[...] = jnp.concatenate([mm_tn(hi, sel), mm_tn(lo, sel)], axis=0).astype(BF16)


def stacked(x):
    rows = x.shape[0]
    pad = -(-rows // 16) * 16 - rows
    if pad:
        x = jnp.concatenate([x, jnp.zeros((pad, x.shape[1]), F32)], axis=0)
    hi, lo = split(x)
    return jnp.concatenate([hi, lo, hi], axis=0)


GROUP = 3


def mix(src_ref, first, w_ref, moved_ref):
    for v in range(first, first + GROUP):
        moved_ref[v] = mm(w_ref[...], stacked(src_ref[v]))


def combine(first, star_ref, moved_ref, total_ref, emit):
    variables, basis, elems = total_ref.shape
    for u0 in range(0, variables, GROUP):
        for h in range(elems // LANES):
            at = slice(h * LANES, (h + 1) * LANES)
            acc = [total_ref[u0 + i, :, at] if first else None for i in range(GROUP)]
            for v in range(first, first + GROUP):
                for d in range(3):
                    m = moved_ref[v, d * basis : (d + 1) * basis, at]
                    for i in range(GROUP):
                        part = star_ref[u0 + i, v, d : d + 1, at] * m
                        acc[i] = part if acc[i] is None else acc[i] + part
            for i in range(GROUP):
                if first + GROUP < variables:
                    total_ref[u0 + i, :, at] = acc[i]
                else:
                    emit(u0 + i, at, acc[i])


def derive(src_ref, star_ref, w_ref, moved_ref, total_ref, emit):
    variables = src_ref.shape[0]
    for first in range(0, variables, GROUP):
        if first + GROUP < variables:
            mix(src_ref, first + GROUP, w_ref, moved_ref)
        combine(first, star_ref, moved_ref, total_ref, emit)


def predict(star_ref, w_ref, moved_ref, term_ref, integ_ref, total_ref):
    integ_ref[...] = term_ref[...]
    mix(term_ref, 0, w_ref, moved_ref)

    def body(k, carry):
        scale = F32(-1.0 / ORDER)
        for o in range(1, ORDER - 1):
            scale = jnp.where(k == o, F32(-1.0 / (o + 1)), scale)

        def emit(u, at, acc):
            value = acc * scale
            term_ref[u, :, at] = value
            integ_ref[u, :, at] = integ_ref[u, :, at] + value

        derive(term_ref, star_ref, w_ref, moved_ref, total_ref, emit)
        mix(term_ref, 0, w_ref, moved_ref)
        return carry

    lax.fori_loop(1, ORDER, body, 0)


def traces(integ_ref, wt_ref, own_refs):
    variables, _, elems = integ_ref.shape
    np_ = wt_ref.shape[0] // 12
    count = len(own_refs)
    for v in range(variables):
        t = mm(wt_ref[0 : count * 4 * np_, :], stacked(integ_ref[v]))
        for r in range(count):
            for f in range(4):
                own_refs[r][v * np_ : (v + 1) * np_, f * elems : (f + 1) * elems] = t[
                    (r * 4 + f) * np_ : (r * 4 + f + 1) * np_
                ]
    rows = own_refs[0].shape[0]
    for r in range(count):
        if rows > variables * np_:
            own_refs[r][variables * np_ :, :] = jnp.zeros(
                (rows - variables * np_, 4 * elems), F32
            )


def is_even(axis):
    return lax.axis_index(axis) % 2 == 0


def send_gather(axes, own_ref, send_ref, left_ref, outs):
    rows, faces = own_ref.shape
    hi, lo = split(own_ref[...])
    left_ref[0:rows] = hi
    left_ref[rows : 2 * rows] = lo
    slots = send_ref.shape[3]
    for k, axis in enumerate(axes):
        even = is_even(axis)
        to_low = send_ref[0, 0, 2 * k : 2 * k + 1]
        to_high = send_ref[0, 0, 2 * k + 1 : 2 * k + 2]
        picks = jnp.concatenate(
            [jnp.where(even, to_low, to_high), jnp.where(even, to_high, to_low)], axis=1
        )
        res = mm(left_ref[...], hot(iota((faces, 2 * slots), 0) == picks))
        res = res[:rows] + res[rows:]
        outs[2 * k][0:rows] = res[:, :slots]
        outs[2 * k + 1][0:rows] = res[:, slots:]


def by_direction(axes, arrived):
    ordered = []
    for k, axis in enumerate(axes):
        even = is_even(axis)
        odd_one, even_one = arrived[2 * k], arrived[2 * k + 1]
        ordered += [jnp.where(even, odd_one, even_one), jnp.where(even, even_one, odd_one)]
    return ordered


def row_of(ref):
    return jnp.concatenate([ref[f : f + 1, :] for f in range(ref.shape[0])], axis=1)


def local_jump(own_refs, source_turn, codes, left_ref, jump_ref):
    rows, faces = own_refs[0].shape
    width = faces // 4
    value = jnp.where(
        source_turn == 1.0,
        own_refs[1][...],
        jnp.where(source_turn == 2.0, own_refs[2][...], own_refs[0][...]),
    )
    hi, lo = split(value)
    left_ref[0:rows] = hi
    left_ref[rows : 2 * rows] = lo
    for q in range(4):
        at = slice(q * width, (q + 1) * width)
        res = mm(left_ref[...], hot(iota((faces, width), 0) == codes[:, at]))
        jump_ref[:, at] = own_refs[0][:, at] - (res[:rows] + res[rows:])


def full_jump(arrived, slot_turn, codes, jump_ref, perm_ref, left_ref, part_ref):
    rows, faces = jump_ref.shape
    elems = faces // 4
    value = jnp.concatenate(arrived, axis=1)
    slots = value.shape[1]
    hi, lo = split(value)
    both = jnp.concatenate([hi, lo], axis=1)
    turned = mm(perm_ref[...], both)
    turn = jnp.concatenate([slot_turn, slot_turn], axis=1)
    chosen = jnp.where(
        turn == 1.0, turned[:rows], jnp.where(turn == 2.0, turned[rows:], both.astype(F32))
    ).astype(BF16)
    left_ref[0:rows] = chosen[:, :slots]
    left_ref[rows : 2 * rows] = chosen[:, slots:]
    for q in range(4):
        at = slice(q * elems, (q + 1) * elems)
        res = mm(left_ref[...], hot(iota((slots, elems), 0) + faces == codes[:, at]))
        part_ref[:, at] = jump_ref[:, at] - (res[:rows] + res[rows:])


def correct(part_ref, flux_m_ref, wl_ref, base_ref, flux_ref, out_ref):
    variables, basis, elems = base_ref.shape
    np_ = flux_ref.shape[1] // 4

    group = 3

    def body(g, carry):
        for f in range(4):
            for h in range(elems // LANES):
                here = slice(h * LANES, (h + 1) * LANES)
                wide = slice(f * elems + h * LANES, f * elems + (h + 1) * LANES)
                acc = [jnp.zeros((np_, LANES), F32) for _ in range(group)]
                for v in range(variables):
                    jump = part_ref[v * np_ : (v + 1) * np_, wide]
                    for i in range(group):
                        acc[i] = acc[i] + flux_m_ref[g * group + i, v, f : f + 1, here] * jump
                for i in range(group):
                    flux_ref[g * group + i, f * np_ : (f + 1) * np_, here] = acc[i]
        return carry

    lax.fori_loop(0, variables // group, body, 0)
    for u in range(variables):
        hi, lo = split(flux_ref[u])
        res = mm(wl_ref[...], jnp.concatenate([hi, lo], axis=0))
        out_ref[u] = base_ref[u] - (res[:basis] + res[basis:])


def first_kernel(
    axes,
    state_hbm, star_hbm, deriv_hbm, trace_hbm, place_hbm, send_hbm, sea_hbm, depth_hbm, wet_hbm,
    w_ref, wt_ref, integ_ref, lifted_ref, o0, o1, o2, o3,
    star_ref, deriv_ref, trace_ref, place_ref, send_ref, own_ref,
    moved_ref, term_ref, total_ref, left_ref, stage_ref, sea_edge, depth_edge, wet_edge, sem_ref,
):
    urgent = start(
        [(deriv_hbm, deriv_ref), (state_hbm, term_ref), (star_hbm, star_ref)], sem_ref
    )
    later = start(
        [(trace_hbm, trace_ref), (place_hbm, place_ref), (send_hbm, send_ref)], sem_ref, 3
    )
    tall = depth_hbm.shape[0]
    pairs = []
    for side, at in enumerate((pl.ds(0, EDGE), pl.ds(tall - EDGE, EDGE))):
        for j in range(3):
            pairs.append((sea_hbm.at[j, at], sea_edge.at[side, j]))
        pairs.append((depth_hbm.at[at], depth_edge.at[side]))
        pairs.append((wet_hbm.at[at], wet_edge.at[side]))
    later = later + start(pairs, sem_ref, 6)
    finish(urgent[:1])
    prep_deriv(deriv_ref, w_ref)
    finish(urgent[1:])
    predict(star_ref, w_ref, moved_ref, term_ref, integ_ref, total_ref)
    finish(later)
    prep_trace(trace_ref, place_ref, stage_ref, wt_ref)
    traces(integ_ref, wt_ref, (own_ref,))
    send_gather(axes, own_ref, send_ref, left_ref, (o0, o1, o2, o3))
    rows = own_ref.shape[0]
    np_ = lifted_ref.shape[0]
    lifted_ref[...] = own_ref[2 * np_ : 3 * np_, :]
    even = is_even(axes[0])
    for j in range(5):
        if j < 3:
            low, high = sea_edge[0, j], sea_edge[1, j]
        else:
            ref = depth_edge if j == 3 else wet_edge
            low, high = ref[0].astype(F32), ref[1].astype(F32)
        low, high = low[:STEPS], high[EDGE - STEPS :]
        for out, edge in ((o0, jnp.where(even, low, high)), (o1, jnp.where(even, high, low))):
            for h in range(edge.shape[1] // LANES):
                begin = rows + h * SEA_ROWS + j * STEPS
                out[begin : begin + STEPS] = edge[:, h * LANES : (h + 1) * LANES]


def own_derivative(integ_ref, field_ref, star_ref, w_ref, base_ref, moved_ref, total_ref):
    def emit(u, at, acc):
        base_ref[u, :, at] = field_ref[u, :, at] - acc

    mix(integ_ref, 0, w_ref, moved_ref)
    derive(integ_ref, star_ref, w_ref, moved_ref, total_ref, emit)


def local_first_kernel(
    integ_ref, field_ref, star_ref, w_ref, wt_ref, codes_ref, orient_ref, lift_ref,
    jump_ref, base_ref, slot_ref, wl_ref, turn_out, slot_out, wl_out, w_out, wt_out,
    turn_ref, own0, own1, own2, left_ref, moved_ref, total_ref, stage_ref, sem_ref,
):
    prep_lift(lift_ref, stage_ref, wl_ref)
    codes = row_of(codes_ref)
    faces = codes.shape[1]
    slots = slot_ref.shape[1]
    turns = jnp.broadcast_to(row_of(orient_ref).astype(F32), (16, faces)).astype(BF16)
    width = faces // 4
    for q in range(4):
        at = slice(q * width, (q + 1) * width)
        turn_ref[:, at] = mm(turns, hot(iota((faces, width), 0) == codes[:, at]))[0:8]
    for q in range(slots // LANES):
        at = slice(q * LANES, (q + 1) * LANES)
        wanted = iota((LANES, faces), 0) + (faces + q * LANES)
        slot_ref[:, at] = mm_nt(turns, hot(wanted == codes))[0:8]
    copies = start(
        [(turn_ref, turn_out), (slot_ref, slot_out), (wl_ref, wl_out), (w_ref, w_out),
         (wt_ref, wt_out)], sem_ref,
    )
    own_refs = (own0, own1, own2)
    traces(integ_ref, wt_ref, own_refs)
    local_jump(own_refs, turn_ref[0:1, :], codes, left_ref, jump_ref)
    own_derivative(integ_ref, field_ref, star_ref, w_ref, base_ref, moved_ref, total_ref)
    finish(copies)


def second_kernel(
    axes, capacity, nodes,
    a0, a1, a2, a3, slot_ref, codes_ref, jump_ref, flux_m_ref, perm_ref, wl_ref, base_ref,
    star_ref, w_ref, wt_ref, send_ref, lifted_ref, faces_ref, owner_ref, blocks_ref, weights_ref,
    pay_ref, field_out, integ_out, edge_odd, edge_even, s0, s1, s2, s3,
    field_ref, integ_ref, own_ref, o0, o1, o2, o3,
    arr_left_ref, part_ref, flux_ref, moved_ref, term_ref, total_ref, left_ref,
    disp_ref, rows_ref, sem_ref,
):
    rows = jump_ref.shape[0]
    tail = pl.ds(rows, a0.shape[0] - rows)
    copies = start([(a0.at[tail], edge_odd), (a1.at[tail], edge_even)], sem_ref)
    full_jump(
        by_direction(axes, [a[0:rows] for a in (a0, a1, a2, a3)]), slot_ref[0:1, :], row_of(codes_ref), jump_ref,
        perm_ref, arr_left_ref, part_ref,
    )
    correct(part_ref, flux_m_ref, wl_ref, base_ref, flux_ref, field_ref)
    copies += start([(field_ref, field_out)], sem_ref, 2)
    term_ref[...] = field_ref[...]
    predict(star_ref, w_ref, moved_ref, term_ref, integ_ref, total_ref)
    copies += start([(integ_ref, integ_out)], sem_ref, 3)
    traces(integ_ref, wt_ref, (own_ref,))
    send_gather(axes, own_ref, send_ref, left_ref, (o0, o1, o2, o3))
    copies += start([(o0, s0), (o1, s1), (o2, s2), (o3, s3)], sem_ref, 4)
    np_ = lifted_ref.shape[0]
    project(
        capacity, nodes, lifted_ref[...], own_ref[2 * np_ : 3 * np_, :], faces_ref, owner_ref,
        blocks_ref, weights_ref, pay_ref, disp_ref, rows_ref,
    )
    finish(copies)


def window_kernel(
    axes,
    sea_hbm, depth_hbm, wet_hbm, low_hbm, high_hbm,
    integ_hbm, field_hbm, star_hbm, w_hbm, wt_hbm, turn_hbm, codes_hbm,
    ext_out, right_out, left_out, jump_out, base_out,
    ext_ref, wet_ref, low_ref, high_ref, right_ref, left_ref,
    integ_ref, field_ref, star_ref, w_ref, wt_ref, turn_ref, codes_ref, jump_ref, base_ref,
    own0, own1, own2, left_rows, moved_ref, total_ref, sem_ref,
):
    copies = start(
        [(wt_hbm, wt_ref), (integ_hbm, integ_ref), (turn_hbm, turn_ref), (codes_hbm, codes_ref),
         (w_hbm, w_ref), (star_hbm, star_ref), (field_hbm, field_ref)], sem_ref,
    )
    body = pl.ds(0, depth_hbm.shape[0])
    sea = start(
        [(sea_hbm.at[j], ext_ref.at[j, body]) for j in range(3)]
        + [(depth_hbm, ext_ref.at[3, body]), (wet_hbm, wet_ref), (low_hbm, low_ref),
           (high_hbm, high_ref)], sem_ref, 7,
    )
    finish(copies[:2])
    own_refs = (own0, own1, own2)
    traces(integ_ref, wt_ref, own_refs)
    finish(copies[2:4])
    local_jump(own_refs, turn_ref[0:1, :], row_of(codes_ref), left_rows, jump_ref)
    written = start([(jump_ref, jump_out)], sem_ref, 14)
    finish(copies[4:])
    own_derivative(integ_ref, field_ref, star_ref, w_ref, base_ref, moved_ref, total_ref)
    written += start([(base_ref, base_out)], sem_ref, 15)
    finish(sea)
    shore(axes, ext_ref, wet_ref, low_ref, high_ref, right_ref, left_ref)
    written += start(
        [(ext_ref, ext_out), (right_ref, right_out), (left_ref, left_out)], sem_ref, 16
    )
    finish(written)


def last_jump_kernel(
    axes,
    a0, a1, a2, a3, slot_hbm, codes_hbm, jump_hbm, perm_hbm,
    part_ref,
    b0, b1, b2, b3, slot_ref, codes_ref, jump_ref, perm_ref, arr_left_ref, sem_ref,
):
    finish(
        start(
            [(a0, b0), (a1, b1), (a2, b2), (a3, b3), (slot_hbm, slot_ref), (perm_hbm, perm_ref),
             (codes_hbm, codes_ref), (jump_hbm, jump_ref)], sem_ref,
        )
    )
    full_jump(
        by_direction(axes, [b0[...], b1[...], b2[...], b3[...]]), slot_ref[0:1, :], row_of(codes_ref), jump_ref,
        perm_ref, arr_left_ref, part_ref,
    )


def last_kernel(
    part_ref, flux_m_hbm, wl_hbm, base_hbm, field_out,
    flux_m_ref, wl_ref, base_ref, field_ref, flux_ref, sem_ref,
):
    copies = start([(flux_m_hbm, flux_m_ref), (wl_hbm, wl_ref), (base_hbm, base_ref)], sem_ref)
    finish(copies)
    correct(part_ref, flux_m_ref, wl_ref, base_ref, flux_ref, field_ref)
    finish(start([(field_ref, field_out)], sem_ref))


def project(
    capacity, nodes, own_a, own_b, faces_ref, owner_ref, blocks_ref, weights_ref, pay_ref,
    disp_ref, rows_ref,
):
    np_ = pad8(nodes)
    faces = own_a.shape[1]
    sea_rows, _ = weights_ref.shape[1:]
    both = jnp.concatenate([own_a, own_b], axis=0)
    hi, lo = split(both)
    picks = hot(iota((faces, sea_rows), 0) == faces_ref[...])
    disp = mm(jnp.concatenate([hi, lo], axis=0), picks)
    disp = disp[: 2 * np_] + disp[2 * np_ :]
    disp = jnp.concatenate([disp, jnp.zeros((LANES - 2 * np_, sea_rows), F32)], axis=0)
    disp_ref[...] = disp.T
    across = jnp.broadcast_to(owner_ref[...].astype(F32), (sea_rows, sea_rows))
    owner = across.T
    earlier = iota((sea_rows, sea_rows), 0) < iota((sea_rows, sea_rows), 1)
    rank = jnp.sum(jnp.where((owner == across) & earlier, 1.0, 0.0), axis=0, keepdims=True)
    place = (across[0:1, :] * float(capacity) + rank).astype(jnp.int32)
    devs = pay_ref.shape[0]
    total = devs * capacity
    put = hot(iota((total, sea_rows), 0) == place)
    chunk = 32

    def body(c, carry):
        here = pl.ds(pl.multiple_of(c * chunk, chunk), chunk)
        cols = disp_ref[here, :]
        for t in range(STEPS):
            acc = cols[:, t * np_ : t * np_ + 1] * weights_ref[0, here, :]
            for n in range(1, nodes):
                acc = acc + cols[:, t * np_ + n : t * np_ + n + 1] * weights_ref[n, here, :]
            rows_ref[t, here, :] = acc
        return carry

    lax.fori_loop(0, sea_rows // chunk, body, 0)
    twice = jnp.concatenate([put, put], axis=1)
    parts = []
    for t in range(STEPS):
        hi, lo = split(rows_ref[t])
        parts.append(mm(twice, jnp.concatenate([hi, lo], axis=0)))
    labels = jnp.broadcast_to(blocks_ref[...].astype(F32), (LANES, sea_rows)).astype(BF16)
    parts.append(mm_nt(put, labels))
    value = jnp.concatenate(parts, axis=1)
    for d in range(devs):
        pay_ref[d] = value[d * capacity : (d + 1) * capacity]


def raster_kernel(
    axis, pay_ref, b_hi_hbm, b_lo_hbm, right_hbm, left_hbm,
    uplift_ref, odd_ref, even_ref, b_hi, b_lo, right_ref, left_ref, got_ref, sem_ref,
):
    even = is_even(axis)
    later = start(
        [(b_hi_hbm, b_hi), (b_lo_hbm, b_lo), (right_hbm, right_ref), (left_hbm, left_ref)],
        sem_ref,
    )
    devs, capacity, _ = pay_ref.shape
    total = devs * capacity
    for d in range(devs):
        got_ref[d * capacity : (d + 1) * capacity] = pay_ref[d]
    tile_x, tile_y = uplift_ref.shape[1:]
    across = tile_y // BS
    cells = BS * BS
    blocks = (tile_x // BS) * across
    labels = got_ref[:, STEPS * cells :].T
    pick = hot(iota((blocks, total), 0) == labels[0:1, :].astype(jnp.int32))
    pick = jnp.concatenate([pick, pick], axis=1)
    by = iota((blocks, cells), 0) % across
    cx = iota((blocks, cells), 1) // BS
    for t in range(STEPS):
        hi, lo = split(got_ref[:, t * cells : (t + 1) * cells])
        x = mm(pick, jnp.concatenate([hi, lo], axis=0))
        step = 1
        while step < BS:
            from_above = pltpu.roll(pltpu.roll(x, blocks - step, 0), BS * step, 1)
            from_below = pltpu.roll(pltpu.roll(x, step, 0), cells - BS * step, 1)
            low_row = (by & step) == 0
            low_col = (cx & step) == 0
            x = jnp.where(low_row == low_col, x, jnp.where(low_row, from_above, from_below))
            step *= 2
        uplift_ref[t] = x
        up, down = x[tile_x - HALO_X :, :], x[:HALO_X, :]
        even_ref[t * HALO_X : (t + 1) * HALO_X] = jnp.where(even, up, down)
        odd_ref[t * HALO_X : (t + 1) * HALO_X] = jnp.where(even, down, up)
    finish(later)


def shore(axes, ext_ref, wet_ref, odd_ref, even_ref, right_ref, left_ref):
    tile_x, tile_y = wet_ref.shape
    ext_ref[4, 0:tile_x, :] = wet_ref[...].astype(F32)
    at_x = lax.axis_index(axes[0])
    has_low = at_x > 0
    has_high = at_x < lax.axis_size(axes[0]) - 1

    even = is_even(axes[0])
    low = jnp.where(even, odd_ref[...], even_ref[...])
    high = jnp.where(even, even_ref[...], odd_ref[...])

    def edge_of(edges, present, j, before):
        halves = []
        for h in range(tile_y // LANES):
            begin = h * SEA_ROWS + j * STEPS
            halves.append(edges[begin : begin + STEPS, :])
        value = jnp.where(present, jnp.concatenate(halves, axis=1), 0.0)
        blank = jnp.zeros((EDGE - STEPS, tile_y), F32)
        return jnp.concatenate([blank, value] if before else [value, blank], axis=0)

    for j in range(5):
        ext_ref[j, tile_x : tile_x + EDGE, :] = edge_of(high, has_high, j, False)
        ext_ref[j, tile_x + EDGE : tile_x + 2 * EDGE, :] = edge_of(low, has_low, j, True)
    lane = iota(right_ref.shape, 1)
    right = jnp.zeros(right_ref.shape, F32)
    left = right
    for j in range(5):
        moved = 2 * HALO_Y + 2 * j
        last = ext_ref[j, :, tile_y - LANES :]
        first = ext_ref[j, :, :LANES]
        right = jnp.where(
            lane >= LANES - moved, right, pltpu.roll(last, LANES - moved, 1)
        )
        left = jnp.where(lane < moved, left, pltpu.roll(first, moved, 1))
    right_ref[...] = right
    left_ref[...] = left


def along_x_kernel(
    axes, uplift_ref, odd_ref, even_ref, b_hi, b_lo, sea_right, sea_left,
    along_ref, odd_out, even_out,
):
    _, tile_y = uplift_ref.shape[1:]
    at_x = lax.axis_index(axes[0])
    even_x = is_even(axes[0])
    even_y = is_even(axes[1])
    has_low = at_x > 0
    has_high = at_x < lax.axis_size(axes[0]) - 1
    for t in range(STEPS):
        at = slice(t * HALO_X, (t + 1) * HALO_X)
        high = jnp.where(even_x, even_ref[at, :], odd_ref[at, :])
        low = jnp.where(even_x, odd_ref[at, :], even_ref[at, :])
        value = jnp.concatenate(
            [uplift_ref[t], jnp.where(has_high, high, 0.0), jnp.where(has_low, low, 0.0)], axis=0
        )
        hi, lo = split(value)
        along_ref[t] = mm(b_hi[...], hi) + mm(b_hi[...], lo) + mm(b_lo[...], hi)
    tall = along_ref.shape[1]
    lane = iota((tall, LANES), 1)
    last = slice(tile_y - LANES, tile_y)
    first = slice(0, LANES)
    right, left = sea_right[...], sea_left[...]
    for t in reversed(range(STEPS)):
        moved = t * HALO_Y
        tail = along_ref[t, :, last]
        head = along_ref[t, :, first]
        if t:
            tail, head = pltpu.roll(tail, LANES - moved, 1), pltpu.roll(head, moved, 1)
        right = jnp.where(lane >= LANES - moved - HALO_Y, tail, right)
        left = jnp.where(lane < moved + HALO_Y, head, left)
    even_out[...] = jnp.where(even_y, right, left)
    odd_out[...] = jnp.where(even_y, left, right)


def ocean_kernel(
    axes, along_ref, ext_ref, odd_ref, even_ref, b_hi, b_lo, out_hbm, out_ref, sem_ref
):
    tall, tile_y = along_ref.shape[1:]
    tile_x = out_ref.shape[1]
    at_y = lax.axis_index(axes[1])
    even = is_even(axes[1])
    low = jnp.where(even, odd_ref[...], even_ref[...])
    high = jnp.where(even, even_ref[...], odd_ref[...])
    low = jnp.where(at_y > 0, low, 0.0)
    high = jnp.where(at_y < lax.axis_size(axes[1]) - 1, high, 0.0)
    lane = iota((tall, LANES), 1)
    forces = []
    for t in range(STEPS):
        right = pltpu.roll(high, LANES - HALO_Y, 1) if t else high
        left = pltpu.roll(low, HALO_Y, 1) if t else low
        value = jnp.concatenate([along_ref[t], right, left], axis=1)
        hi, lo = split(value)
        forces.append(mm(hi, b_hi[...]) + mm(lo, b_hi[...]) + mm(hi, b_lo[...]))
    fields = []
    for j in range(5):
        moved = 2 * HALO_Y + 2 * j
        edge = jnp.where(
            lane < LANES // 2, pltpu.roll(high, LANES - moved, 1), pltpu.roll(low, moved, 1)
        )
        fields.append(jnp.concatenate([ext_ref[j], edge], axis=1))
    eta, east, north, depth, wet = fields
    rows, cols = eta.shape

    def px(x):
        return pltpu.roll(x, rows - 1, 0)

    def mx(x):
        return pltpu.roll(x, 1, 0)

    def py(x):
        return pltpu.roll(x, cols - 1, 1)

    def my(x):
        return pltpu.roll(x, 1, 1)

    factor = 0.5 * COURANT
    for t in range(STEPS):
        eta = eta + wet * forces[t]
        column = depth + eta
        qx, qy = column * east, column * north
        near = [(px(a), mx(a), py(a), my(a)) for a in (eta, east, north)]
        mean = [0.25 * (a + b + c + d) for a, b, c, d in near]
        eta_x, eta_y = near[0][0] - near[0][1], near[0][2] - near[0][3]
        east_x, east_y = near[1][0] - near[1][1], near[1][2] - near[1][3]
        north_x, north_y = near[2][0] - near[2][1], near[2][2] - near[2][3]
        eta_new = mean[0] - factor * ((px(qx) - mx(qx)) + (py(qy) - my(qy)))
        east_new = mean[1] - factor * (east * east_x + north * east_y + eta_x)
        north_new = mean[2] - factor * (east * north_x + north * north_y + eta_y)
        eta, east, north = eta_new * wet, east_new * wet, north_new * wet
    copies = []
    for j, value in enumerate((eta, east, north)):
        out_ref[j] = value[:tile_x, :tile_y]
        copies += start([(out_ref.at[j], out_hbm.at[j])], sem_ref, j)
    finish(copies)


def swap(value, axes, along, odd):
    counts = [lax.axis_size(axis) for axis in axes]
    other = 1 - along
    pairs = []
    for x in range(counts[0]):
        for y in range(counts[1]):
            at = [x, y]
            to = list(at)
            to[along] = ((at[along] - odd) ^ 1) + odd
            if not 0 <= to[along] < counts[along]:
                to = list(at)
                to[other] = at[other] ^ 1
                if to[other] >= counts[other]:
                    to = list(at)
            pairs.append((x * counts[1] + y, to[0] * counts[1] + to[1]))
    return lax.ppermute(value, axes, pairs)


def on_device(
    state, star, deriv, trace_ops, lift, face_flux, orient, neighbours, send_faces,
    sea_faces, sea_owner, sea_blocks, sea_weights, depth, wet, sea_state,
):
    variables, basis, elems = state.shape
    nodes = trace_ops.shape[2]
    np_ = pad8(nodes)
    faces = 4 * elems
    slots = send_faces.shape[-1]
    rows = -(-variables * np_ // 16) * 16
    kb = -(-basis // 16) * 16
    turns = node_turns()
    place = np.zeros((12 * np_, 4 * nodes), np.float32)
    perm = np.zeros((2 * rows, rows), np.float32)
    for r in range(3):
        for n in range(nodes):
            for f in range(4):
                place[(r * 4 + f) * np_ + n, turns[r][n] * 4 + f] = 1.0
            for v in range(variables):
                if r:
                    perm[(r - 1) * rows + v * np_ + n, v * np_ + turns[r][n]] = 1.0
    place = jnp.asarray(place, BF16)
    perm = jnp.asarray(perm, BF16)
    star = star.transpose(1, 2, 0, 3)
    face_flux = face_flux.transpose(1, 2, 0, 3)
    trace_ops = trace_ops.transpose(2, 0, 1)
    lift = lift.transpose(1, 0, 2)

    wide = (rows, faces)
    out = (rows, slots)
    tile_x, tile_y = depth.shape
    out_x = (rows + (tile_y // LANES) * SEA_ROWS, slots)
    field_shape = (variables, basis, elems)
    moved = ((variables, 3 * basis, elems), F32)
    left = ((2 * rows, faces), BF16)
    arr_left = ((2 * rows, 4 * slots), BF16)
    flux = ((variables, 4 * np_, elems), F32)
    stage = ((4 * nodes, basis), F32)

    axes = ("gx", "gy")

    def sent(outgoing):
        moved = []
        for k in (0, 1):
            for odd in (1, 0):
                moved.append(swap(outgoing[len(moved)], axes, k, odd))
        return moved

    w_of = ((3 * basis, 3 * kb), BF16)
    wt_of = ((12 * np_, 3 * kb), BF16)
    wl_of = ((2 * basis, 8 * np_), BF16)
    turn_of = ((8, faces), F32)
    slot_of = ((8, 4 * slots), F32)
    field_of, wide_of, out_of = (field_shape, F32), (wide, F32), (out, F32)
    star_of, flux_m_of = (star.shape, F32), (face_flux.shape, F32)
    lifted_of = ((np_, faces), F32)
    codes_of = (neighbours.shape, neighbours.dtype)
    perm_of = (perm.shape, BF16)

    def hbm(array):
        return (*array, HBM)

    w, wt, integ, lifted_a, *outgoing = call(
        lambda *refs: first_kernel(axes, *refs),
        [w_of, wt_of, field_of, lifted_of] + [(out_x, F32)] * 2 + [out_of] * 2,
        [star_of, (deriv.shape, F32), (trace_ops.shape, F32), (place.shape, BF16),
         (send_faces.shape, send_faces.dtype), wide_of, moved, field_of, field_of, left, stage,
         ((2, 3, EDGE, tile_y), F32), ((2, EDGE, tile_y), F32), ((2, EDGE, tile_y), wet.dtype),
         sems(16)],
        state, star, deriv, trace_ops, place, send_faces, sea_state, depth, wet,
        micros=10, held=range(9),
    )
    arrived = sent(outgoing)
    jump, base, slot_turn, wl, turn_h, slot_h, wl_h, w_h, wt_h = call(
        local_first_kernel,
        [wide_of, field_of, slot_of, wl_of, hbm(turn_of), hbm(slot_of), hbm(wl_of), hbm(w_of),
         hbm(wt_of)],
        [turn_of, wide_of, wide_of, wide_of, left, moved, field_of, stage, sems(5)],
        integ, state, star, w, wt, neighbours, orient, lift,
        micros=4,
    )
    sea_rows, cells = sea_weights.shape[1:]
    devs = lax.axis_size("gx") * lax.axis_size("gy")
    capacity = max(2, (sea_rows + devs - 1) // devs)
    message = (devs, capacity, STEPS * cells + LANES)
    payload, field_h, integ_h, edge_odd, edge_even, *outgoing = call(
        lambda *refs: second_kernel(axes, capacity, nodes, *refs),
        [(message, F32), hbm(field_of), hbm(field_of)]
        + [((out_x[0] - rows, slots), F32, HBM)] * 2 + [hbm(out_of)] * 4,
        [field_of, field_of, wide_of] + [out_of] * 4
        + [arr_left, wide_of, flux, moved, field_of, field_of, left,
           ((sea_rows, LANES), F32), ((STEPS, sea_rows, cells), F32), sems(8)],
        *arrived, slot_turn, neighbours, jump, face_flux, perm, wl, base, star, w, wt,
        send_faces, lifted_a, sea_faces.reshape(1, -1), sea_owner.reshape(1, -1),
        sea_blocks.reshape(1, -1), sea_weights, micros=12,
    )
    got = lax.all_to_all(payload, ("gx", "gy"), split_axis=0, concat_axis=0, tiled=True)
    arrived = sent(outgoing)
    tall = tile_x + 2 * EDGE
    axes = ("gx", "gy")
    ext_of = ((5, tall, tile_y), F32)
    strip_of = ((tall, LANES), F32)
    edge_of = (edge_odd.shape, F32)
    ext_h, right_h, left_h, jump_h, base_h = call(
        lambda *refs: window_kernel(axes, *refs),
        [hbm(ext_of), hbm(strip_of), hbm(strip_of), hbm(wide_of), hbm(field_of)],
        [ext_of, (wet.shape, wet.dtype), edge_of, edge_of, strip_of, strip_of,
         field_of, field_of, star_of, w_of, wt_of, turn_of, codes_of, wide_of, field_of,
         wide_of, wide_of, wide_of, left, moved, field_of, sems(19)],
        sea_state, depth, wet, edge_odd, edge_even,
        integ_h, field_h, star, w_h, wt_h, turn_h, neighbours,
        micros=6, held=range(12),
    )
    part, = call(
        lambda *refs: last_jump_kernel(axes, *refs), [wide_of],
        [out_of] * 4 + [slot_of, codes_of, wide_of, perm_of, arr_left, sems(8)],
        *arrived, slot_h, neighbours, jump_h, perm,
        micros=2, held=range(8),
    )
    elastic, = call(
        last_kernel, [hbm(field_of)],
        [flux_m_of, wl_of, field_of, field_of, flux, sems(3)],
        part, face_flux, wl_h, base_h, micros=2, held=range(1, 4),
    )

    halo = ((STEPS * HALO_X, tile_y), F32)
    cell_x = np.concatenate([np.arange(tile_x + EDGE), np.arange(-EDGE, 0)])
    read_x = np.concatenate([np.arange(tile_x + HALO_X), np.arange(-HALO_X, 0)])
    cell_y = np.concatenate([np.arange(tile_y + LANES // 2), np.arange(-LANES // 2, 0)])
    read_y = np.concatenate([np.arange(tile_y + LANES), np.arange(-LANES, 0)])
    bx = [jnp.asarray(b) for b in band(cell_x, read_x)]
    by = [jnp.asarray(b.T) for b in band(cell_y, read_y)]
    uplift, odd, even, bx_hi, bx_lo, sea_right, sea_left = call(
        lambda *refs: raster_kernel("gx", *refs),
        [((STEPS, tile_x, tile_y), F32), halo, halo]
        + [(b.shape, BF16) for b in bx] + [strip_of, strip_of],
        [((devs * capacity, message[2]), F32), sems(4)],
        got, *bx, right_h, left_h, micros=2, held=range(1, 5),
    )
    odd = swap(odd, axes, 0, 1)
    even = swap(even, axes, 0, 0)
    along, odd_y, even_y = call(
        lambda *refs: along_x_kernel(axes, *refs),
        [((STEPS, tall, tile_y), F32), strip_of, strip_of], [],
        uplift, odd, even, bx_hi, bx_lo, sea_right, sea_left, micros=1,
    )
    odd_y = swap(odd_y, axes, 1, 1)
    even_y = swap(even_y, axes, 1, 0)
    ocean_of = ((3, tile_x, tile_y), F32)
    ocean, = call(
        lambda *refs: ocean_kernel(axes, *refs), [hbm(ocean_of)], [ocean_of, sems(3)],
        along, ext_h, odd_y, even_y, *by, micros=4,
    )
    return elastic, ocean


def solution(mesh):
    both = ("gx", "gy")
    placed = (
        P(None, None, both),
        P(None, None, None, both),
        P(),
        P(),
        P(),
        P(None, None, None, both),
        P(None, both),
        P(None, both),
        P("gx", "gy", None, None),
        P(both),
        P(both, None),
        P(both),
        P(None, both, None),
        P("gx", "gy"),
        P("gx", "gy"),
        P(None, "gx", "gy"),
    )

    return jax.shard_map(
        on_device,
        mesh=mesh,
        in_specs=placed,
        out_specs=(P(None, None, both), P(None, "gx", "gy")),
        check_vma=False,
    )
```

```python
import math

import jax
import jax.numpy as jnp
import numpy as np
from jax import lax
from jax.experimental import pallas as pl
from jax.experimental.pallas import tpu as pltpu
from jax.sharding import PartitionSpec as P


ORDER = 6
STEPS = 2
BS = 16
HALF = 32
SPREAD = 8.0
COURANT = 0.25
LANES = 128
HALO_X = 40
HALO_Y = 34
EDGE = 8
SEA_ROWS = 16
F32 = jnp.float32
BF16 = jnp.bfloat16


def node_turns():
    upper = ORDER - 1
    nodes = [(i, j) for i in range(upper + 1) for j in range(upper + 1 - i)]
    once = [nodes.index((pair[1], upper - pair[0] - pair[1])) for pair in nodes]
    twice = [once[once[number]] for number in range(len(nodes))]
    return [list(range(len(nodes))), once, twice]


def pad8(n):
    return -(-n // 8) * 8


def band(out_at, in_at):
    k = np.arange(-HALF, HALF + 1)
    raw = 1.0 / np.cosh(math.pi * k / (2.0 * SPREAD))
    raw = raw / raw.sum()
    diff = in_at[None, :] - out_at[:, None]
    w = np.where(np.abs(diff) <= HALF, raw[np.clip(diff + HALF, 0, 2 * HALF)], 0.0)
    w = w.astype(np.float32)
    hi = w.astype(jnp.bfloat16)
    lo = (w - hi.astype(np.float32)).astype(jnp.bfloat16)
    return hi, lo


def split(x):
    hi = x.astype(BF16)
    lo = (x - hi.astype(F32)).astype(BF16)
    return hi, lo


def mm(a, b):
    return lax.dot_general(a, b, (((1,), (0,)), ((), ())), preferred_element_type=F32)


def mm_tn(a, b):
    return lax.dot_general(a, b, (((0,), (0,)), ((), ())), preferred_element_type=F32)


def mm_nt(a, b):
    return lax.dot_general(a, b, (((1,), (1,)), ((), ())), preferred_element_type=F32)


def iota(shape, dim):
    return lax.broadcasted_iota(jnp.int32, shape, dim)


def hot(mask):
    return jnp.where(mask, 1.0, 0.0).astype(BF16)


HBM = "hbm"


def call(body, outs, scratch, *args, micros, limit=20, held=(), flags=None):
    def spec(in_hbm):
        return pl.BlockSpec(memory_space=pltpu.HBM if in_hbm else pltpu.VMEM)

    args = [
        pltpu.with_memory_space_constraint(a, pltpu.HBM) if i in held else a
        for i, a in enumerate(args)
    ]
    return pl.pallas_call(
        body,
        in_specs=[spec(i in held) for i in range(len(args))],
        out_specs=[spec(len(o) == 3) for o in outs],
        out_shape=[(pltpu.HBM if len(o) == 3 else jax.ShapeDtypeStruct)(o[0], o[1]) for o in outs],
        scratch_shapes=[pltpu.VMEM(*x) if isinstance(x, tuple) else x for x in scratch],
        compiler_params=pltpu.CompilerParams(
            vmem_limit_bytes=limit * 2**20, **({"flags": flags} if flags else {})
        ),
        cost_estimate=pl.CostEstimate(
            flops=micros * 10**8, bytes_accessed=micros * 3 * 10**6, transcendentals=0
        ),
    )(*args)


def sems(count):
    return pltpu.SemaphoreType.DMA((count,))


def start(pairs, sem_ref, first=0):
    copies = [
        pltpu.make_async_copy(src, dst, sem_ref.at[first + i])
        for i, (src, dst) in enumerate(pairs)
    ]
    for copy in copies:
        copy.start()
    return copies


def finish(copies):
    for copy in copies:
        copy.wait()


def slots_of(basis):
    kb = -(-basis // 16) * 16
    row, col = iota((basis, 3 * kb), 0), iota((basis, 3 * kb), 1)
    return hot((col == row) | (col == kb + row)), hot(col == 2 * kb + row)


def prep_deriv(deriv_ref, w_ref):
    basis = deriv_ref.shape[1]
    sel_hi, sel_lo = slots_of(basis)
    parts = []
    for d in range(3):
        hi, lo = split(deriv_ref[d])
        parts.append(mm_tn(hi, sel_hi) + mm_tn(lo, sel_lo))
    w_ref[...] = jnp.concatenate(parts, axis=0).astype(BF16)


def staged(ref, stage_ref):
    for n in range(ref.shape[0]):
        stage_ref[n * 4 : (n + 1) * 4, :] = ref[n]
    return split(stage_ref[...])


def prep_trace(trace_ref, place_ref, stage_ref, wt_ref):
    sel_hi, sel_lo = slots_of(trace_ref.shape[2])
    hi, lo = staged(trace_ref, stage_ref)
    hi = mm(place_ref[...], hi).astype(BF16)
    lo = mm(place_ref[...], lo).astype(BF16)
    wt_ref[...] = (mm(hi, sel_hi) + mm(lo, sel_lo)).astype(BF16)


def prep_lift(lift_ref, stage_ref, wl_ref):
    nodes = lift_ref.shape[0]
    np_ = pad8(nodes)
    row, col = iota((4 * nodes, 8 * np_), 0), iota((4 * nodes, 8 * np_), 1)
    at = (row % 4) * np_ + row // 4
    sel = hot((col == at) | (col == 4 * np_ + at))
    hi, lo = staged(lift_ref, stage_ref)
    wl_ref[...] = jnp.concatenate([mm_tn(hi, sel), mm_tn(lo, sel)], axis=0).astype(BF16)


def stacked(x):
    rows = x.shape[0]
    pad = -(-rows // 16) * 16 - rows
    if pad:
        x = jnp.concatenate([x, jnp.zeros((pad, x.shape[1]), F32)], axis=0)
    hi, lo = split(x)
    return jnp.concatenate([hi, lo, hi], axis=0)


GROUP = 3


def mix(src_ref, first, w_ref, moved_ref):
    for v in range(first, first + GROUP):
        moved_ref[v] = mm(w_ref[...], stacked(src_ref[v]))


def combine(first, star_ref, moved_ref, total_ref, emit):
    variables, basis, elems = total_ref.shape
    for u0 in range(0, variables, GROUP):
        for h in range(elems // LANES):
            at = slice(h * LANES, (h + 1) * LANES)
            acc = [total_ref[u0 + i, :, at] if first else None for i in range(GROUP)]
            for v in range(first, first + GROUP):
                for d in range(3):
                    m = moved_ref[v, d * basis : (d + 1) * basis, at]
                    for i in range(GROUP):
                        part = star_ref[u0 + i, v, d : d + 1, at] * m
                        acc[i] = part if acc[i] is None else acc[i] + part
            for i in range(GROUP):
                if first + GROUP < variables:
                    total_ref[u0 + i, :, at] = acc[i]
                else:
                    emit(u0 + i, at, acc[i])


def derive(src_ref, star_ref, w_ref, moved_ref, total_ref, emit):
    variables = src_ref.shape[0]
    for first in range(0, variables, GROUP):
        if first + GROUP < variables:
            mix(src_ref, first + GROUP, w_ref, moved_ref)
        combine(first, star_ref, moved_ref, total_ref, emit)


def predict(star_ref, w_ref, moved_ref, term_ref, integ_ref, total_ref):
    integ_ref[...] = term_ref[...]
    mix(term_ref, 0, w_ref, moved_ref)

    def body(k, carry):
        scale = F32(-1.0 / ORDER)
        for o in range(1, ORDER - 1):
            scale = jnp.where(k == o, F32(-1.0 / (o + 1)), scale)

        def emit(u, at, acc):
            value = acc * scale
            term_ref[u, :, at] = value
            integ_ref[u, :, at] = integ_ref[u, :, at] + value

        derive(term_ref, star_ref, w_ref, moved_ref, total_ref, emit)
        mix(term_ref, 0, w_ref, moved_ref)
        return carry

    lax.fori_loop(1, ORDER, body, 0)


def traces(integ_ref, wt_ref, own_ref, turn=None, turned_ref=None):
    variables, _, elems = integ_ref.shape
    np_ = wt_ref.shape[0] // 12
    count = 1 if turn is None else 3
    for v in range(variables):
        t = mm(wt_ref[0 : count * 4 * np_, :], stacked(integ_ref[v]))
        rows = slice(v * np_, (v + 1) * np_)
        for f in range(4):
            at = slice(f * elems, (f + 1) * elems)
            plain, *others = [
                t[(r * 4 + f) * np_ : (r * 4 + f + 1) * np_] for r in range(count)
            ]
            own_ref[rows, at] = plain
            if others:
                turned_ref[rows, at] = jnp.where(
                    turn[:, at] == 1.0,
                    others[0],
                    jnp.where(turn[:, at] == 2.0, others[1], plain),
                )
    for ref in (own_ref, turned_ref):
        if ref is not None and ref.shape[0] > variables * np_:
            ref[variables * np_ :, :] = jnp.zeros(
                (ref.shape[0] - variables * np_, 4 * elems), F32
            )


def is_even(axis):
    return lax.axis_index(axis) % 2 == 0


def send_gather(axes, own_ref, send_ref, left_ref, outs):
    rows, faces = own_ref.shape
    hi, lo = split(own_ref[...])
    left_ref[0:rows] = hi
    left_ref[rows : 2 * rows] = lo
    slots = send_ref.shape[3]
    for k, axis in enumerate(axes):
        even = is_even(axis)
        to_low = send_ref[0, 0, 2 * k : 2 * k + 1]
        to_high = send_ref[0, 0, 2 * k + 1 : 2 * k + 2]
        picks = jnp.concatenate(
            [jnp.where(even, to_low, to_high), jnp.where(even, to_high, to_low)], axis=1
        )
        res = mm(left_ref[...], hot(iota((faces, 2 * slots), 0) == picks))
        res = res[:rows] + res[rows:]
        outs[2 * k][0:rows] = res[:, :slots]
        outs[2 * k + 1][0:rows] = res[:, slots:]


def by_direction(axes, arrived):
    ordered = []
    for k, axis in enumerate(axes):
        even = is_even(axis)
        odd_one, even_one = arrived[2 * k], arrived[2 * k + 1]
        ordered += [jnp.where(even, odd_one, even_one), jnp.where(even, even_one, odd_one)]
    return ordered


def row_of(ref):
    return jnp.concatenate([ref[f : f + 1, :] for f in range(ref.shape[0])], axis=1)


def local_jump(own_ref, turned_ref, codes, left_ref, jump_ref):
    rows, faces = own_ref.shape
    width = faces // 4
    hi, lo = split(turned_ref[...])
    left_ref[0:rows] = hi
    left_ref[rows : 2 * rows] = lo
    for q in range(4):
        at = slice(q * width, (q + 1) * width)
        res = mm(left_ref[...], hot(iota((faces, width), 0) == codes[:, at]))
        jump_ref[:, at] = own_ref[:, at] - (res[:rows] + res[rows:])


def full_jump(arrived, slot_turn, codes, jump_ref, perm_ref, left_ref, part_ref):
    rows, faces = jump_ref.shape
    elems = faces // 4
    value = jnp.concatenate(arrived, axis=1)
    slots = value.shape[1]
    hi, lo = split(value)
    both = jnp.concatenate([hi, lo], axis=1)
    turned = mm(perm_ref[...], both)
    turn = jnp.concatenate([slot_turn, slot_turn], axis=1)
    chosen = jnp.where(
        turn == 1.0, turned[:rows], jnp.where(turn == 2.0, turned[rows:], both.astype(F32))
    ).astype(BF16)
    left_ref[0:rows] = chosen[:, :slots]
    left_ref[rows : 2 * rows] = chosen[:, slots:]
    for q in range(4):
        at = slice(q * elems, (q + 1) * elems)
        res = mm(left_ref[...], hot(iota((slots, elems), 0) + faces == codes[:, at]))
        part_ref[:, at] = jump_ref[:, at] - (res[:rows] + res[rows:])


def correct(part_ref, flux_m_ref, wl_ref, base_ref, flux_ref, out_ref):
    variables, basis, elems = base_ref.shape
    np_ = flux_ref.shape[1] // 4

    group = 3

    def body(g, carry):
        for f in range(4):
            for h in range(elems // LANES):
                here = slice(h * LANES, (h + 1) * LANES)
                wide = slice(f * elems + h * LANES, f * elems + (h + 1) * LANES)
                acc = [jnp.zeros((np_, LANES), F32) for _ in range(group)]
                for v in range(variables):
                    jump = part_ref[v * np_ : (v + 1) * np_, wide]
                    for i in range(group):
                        acc[i] = acc[i] + flux_m_ref[g * group + i, v, f : f + 1, here] * jump
                for i in range(group):
                    flux_ref[g * group + i, f * np_ : (f + 1) * np_, here] = acc[i]
        return carry

    lax.fori_loop(0, variables // group, body, 0)
    for u in range(variables):
        hi, lo = split(flux_ref[u])
        res = mm(wl_ref[...], jnp.concatenate([hi, lo], axis=0))
        out_ref[u] = base_ref[u] - (res[:basis] + res[basis:])


def first_kernel(
    axes,
    state_hbm, star_hbm, deriv_hbm, trace_hbm, place_hbm, send_hbm, sea_hbm, depth_hbm, wet_hbm,
    w_ref, wt_ref, integ_ref, lifted_ref, o0, o1, o2, o3,
    star_ref, deriv_ref, trace_ref, place_ref, send_ref, own_ref,
    moved_ref, term_ref, total_ref, left_ref, stage_ref, sea_edge, depth_edge, wet_edge, sem_ref,
):
    urgent = start(
        [(deriv_hbm, deriv_ref), (state_hbm, term_ref), (star_hbm, star_ref)], sem_ref
    )
    later = start(
        [(trace_hbm, trace_ref), (place_hbm, place_ref), (send_hbm, send_ref)], sem_ref, 3
    )
    tall = depth_hbm.shape[0]
    pairs = []
    for side, at in enumerate((pl.ds(0, EDGE), pl.ds(tall - EDGE, EDGE))):
        for j in range(3):
            pairs.append((sea_hbm.at[j, at], sea_edge.at[side, j]))
        pairs.append((depth_hbm.at[at], depth_edge.at[side]))
        pairs.append((wet_hbm.at[at], wet_edge.at[side]))
    later = later + start(pairs, sem_ref, 6)
    finish(urgent[:1])
    prep_deriv(deriv_ref, w_ref)
    finish(urgent[1:])
    predict(star_ref, w_ref, moved_ref, term_ref, integ_ref, total_ref)
    finish(later)
    prep_trace(trace_ref, place_ref, stage_ref, wt_ref)
    traces(integ_ref, wt_ref, own_ref)
    send_gather(axes, own_ref, send_ref, left_ref, (o0, o1, o2, o3))
    rows = own_ref.shape[0]
    np_ = lifted_ref.shape[0]
    lifted_ref[...] = own_ref[2 * np_ : 3 * np_, :]
    even = is_even(axes[0])
    for j in range(5):
        if j < 3:
            low, high = sea_edge[0, j], sea_edge[1, j]
        else:
            ref = depth_edge if j == 3 else wet_edge
            low, high = ref[0].astype(F32), ref[1].astype(F32)
        low, high = low[:STEPS], high[EDGE - STEPS :]
        for out, edge in ((o0, jnp.where(even, low, high)), (o1, jnp.where(even, high, low))):
            for h in range(edge.shape[1] // LANES):
                begin = rows + h * SEA_ROWS + j * STEPS
                out[begin : begin + STEPS] = edge[:, h * LANES : (h + 1) * LANES]


def own_derivative(integ_ref, field_ref, star_ref, w_ref, base_ref, moved_ref, total_ref):
    def emit(u, at, acc):
        base_ref[u, :, at] = field_ref[u, :, at] - acc

    mix(integ_ref, 0, w_ref, moved_ref)
    derive(integ_ref, star_ref, w_ref, moved_ref, total_ref, emit)


def local_first_kernel(
    integ_ref, field_ref, star_ref, w_ref, wt_ref, codes_ref, orient_ref, lift_ref,
    jump_ref, base_ref, slot_ref, wl_ref, turn_out, slot_out, wl_out, w_out, wt_out,
    turn_ref, own_ref, turned_ref, left_ref, moved_ref, total_ref, stage_ref, sem_ref,
):
    prep_lift(lift_ref, stage_ref, wl_ref)
    codes = row_of(codes_ref)
    faces = codes.shape[1]
    slots = slot_ref.shape[1]
    turns = jnp.broadcast_to(row_of(orient_ref).astype(F32), (16, faces)).astype(BF16)
    width = faces // 4
    for q in range(4):
        at = slice(q * width, (q + 1) * width)
        turn_ref[:, at] = mm(turns, hot(iota((faces, width), 0) == codes[:, at]))[0:8]
    for q in range(slots // LANES):
        at = slice(q * LANES, (q + 1) * LANES)
        wanted = iota((LANES, faces), 0) + (faces + q * LANES)
        slot_ref[:, at] = mm_nt(turns, hot(wanted == codes))[0:8]
    copies = start(
        [(turn_ref, turn_out), (slot_ref, slot_out), (wl_ref, wl_out), (w_ref, w_out),
         (wt_ref, wt_out)], sem_ref,
    )
    traces(integ_ref, wt_ref, own_ref, turn_ref[0:1, :], turned_ref)
    local_jump(own_ref, turned_ref, codes, left_ref, jump_ref)
    own_derivative(integ_ref, field_ref, star_ref, w_ref, base_ref, moved_ref, total_ref)
    finish(copies)


def second_kernel(
    axes, capacity, nodes,
    a0, a1, a2, a3, slot_ref, codes_ref, jump_ref, flux_m_ref, perm_ref, wl_ref, base_ref,
    star_ref, w_ref, wt_ref, send_ref, lifted_ref, faces_ref, owner_ref, blocks_ref, weights_ref,
    pay_ref, field_out, integ_out, edge_odd, edge_even, s0, s1, s2, s3,
    field_ref, integ_ref, own_ref, o0, o1, o2, o3,
    arr_left_ref, part_ref, flux_ref, moved_ref, term_ref, total_ref, left_ref,
    disp_ref, rows_ref, sem_ref,
):
    rows = jump_ref.shape[0]
    tail = pl.ds(rows, a0.shape[0] - rows)
    copies = start([(a0.at[tail], edge_odd), (a1.at[tail], edge_even)], sem_ref)
    full_jump(
        by_direction(axes, [a[0:rows] for a in (a0, a1, a2, a3)]), slot_ref[0:1, :], row_of(codes_ref), jump_ref,
        perm_ref, arr_left_ref, part_ref,
    )
    correct(part_ref, flux_m_ref, wl_ref, base_ref, flux_ref, field_ref)
    copies += start([(field_ref, field_out)], sem_ref, 2)
    term_ref[...] = field_ref[...]
    predict(star_ref, w_ref, moved_ref, term_ref, integ_ref, total_ref)
    copies += start([(integ_ref, integ_out)], sem_ref, 3)
    traces(integ_ref, wt_ref, own_ref)
    send_gather(axes, own_ref, send_ref, left_ref, (o0, o1, o2, o3))
    copies += start([(o0, s0), (o1, s1), (o2, s2), (o3, s3)], sem_ref, 4)
    np_ = lifted_ref.shape[0]
    project(
        capacity, nodes, lifted_ref[...], own_ref[2 * np_ : 3 * np_, :], faces_ref, owner_ref,
        blocks_ref, weights_ref, pay_ref, disp_ref, rows_ref,
    )
    finish(copies)


def window_kernel(
    axes,
    sea_hbm, depth_hbm, wet_hbm, low_hbm, high_hbm,
    integ_hbm, field_hbm, star_hbm, w_hbm, wt_hbm, turn_hbm, codes_hbm,
    ext_out, right_out, left_out, jump_out, base_out,
    ext_ref, wet_ref, low_ref, high_ref, right_ref, left_ref,
    integ_ref, field_ref, star_ref, w_ref, wt_ref, turn_ref, codes_ref, jump_ref, base_ref,
    own_ref, turned_ref, left_rows, moved_ref, total_ref, sem_ref,
):
    copies = start(
        [(wt_hbm, wt_ref), (integ_hbm, integ_ref), (turn_hbm, turn_ref), (codes_hbm, codes_ref),
         (w_hbm, w_ref), (star_hbm, star_ref), (field_hbm, field_ref)], sem_ref,
    )
    body = pl.ds(0, depth_hbm.shape[0])
    sea = start(
        [(sea_hbm.at[j], ext_ref.at[j, body]) for j in range(3)]
        + [(depth_hbm, ext_ref.at[3, body]), (wet_hbm, wet_ref), (low_hbm, low_ref),
           (high_hbm, high_ref)], sem_ref, 7,
    )
    finish(copies[:3])
    traces(integ_ref, wt_ref, own_ref, turn_ref[0:1, :], turned_ref)
    finish(copies[3:4])
    local_jump(own_ref, turned_ref, row_of(codes_ref), left_rows, jump_ref)
    written = start([(jump_ref, jump_out)], sem_ref, 14)
    finish(copies[4:])
    own_derivative(integ_ref, field_ref, star_ref, w_ref, base_ref, moved_ref, total_ref)
    written += start([(base_ref, base_out)], sem_ref, 15)
    finish(sea)
    shore(axes, ext_ref, wet_ref, low_ref, high_ref, right_ref, left_ref)
    written += start(
        [(ext_ref, ext_out), (right_ref, right_out), (left_ref, left_out)], sem_ref, 16
    )
    finish(written)


def last_jump_kernel(
    axes,
    a0, a1, a2, a3, slot_hbm, codes_hbm, jump_hbm, perm_hbm,
    part_ref, slot_ref, codes_ref, jump_ref, perm_ref, arr_left_ref, sem_ref,
):
    finish(
        start(
            [(slot_hbm, slot_ref), (perm_hbm, perm_ref), (codes_hbm, codes_ref),
             (jump_hbm, jump_ref)], sem_ref,
        )
    )
    full_jump(
        by_direction(axes, [a0[...], a1[...], a2[...], a3[...]]), slot_ref[0:1, :], row_of(codes_ref), jump_ref,
        perm_ref, arr_left_ref, part_ref,
    )


def last_kernel(
    part_ref, flux_m_hbm, wl_hbm, base_hbm, field_out,
    flux_m_ref, wl_ref, base_ref, field_ref, flux_ref, sem_ref,
):
    copies = start([(flux_m_hbm, flux_m_ref), (wl_hbm, wl_ref), (base_hbm, base_ref)], sem_ref)
    finish(copies)
    correct(part_ref, flux_m_ref, wl_ref, base_ref, flux_ref, field_ref)
    finish(start([(field_ref, field_out)], sem_ref))


def project(
    capacity, nodes, own_a, own_b, faces_ref, owner_ref, blocks_ref, weights_ref, pay_ref,
    disp_ref, rows_ref,
):
    np_ = pad8(nodes)
    faces = own_a.shape[1]
    sea_rows, _ = weights_ref.shape[1:]
    both = jnp.concatenate([own_a, own_b], axis=0)
    hi, lo = split(both)
    picks = hot(iota((faces, sea_rows), 0) == faces_ref[...])
    disp = mm(jnp.concatenate([hi, lo], axis=0), picks)
    disp = disp[: 2 * np_] + disp[2 * np_ :]
    disp = jnp.concatenate([disp, jnp.zeros((LANES - 2 * np_, sea_rows), F32)], axis=0)
    disp_ref[...] = disp.T
    across = jnp.broadcast_to(owner_ref[...].astype(F32), (sea_rows, sea_rows))
    owner = across.T
    earlier = iota((sea_rows, sea_rows), 0) < iota((sea_rows, sea_rows), 1)
    rank = jnp.sum(jnp.where((owner == across) & earlier, 1.0, 0.0), axis=0, keepdims=True)
    place = (across[0:1, :] * float(capacity) + rank).astype(jnp.int32)
    devs = pay_ref.shape[0]
    total = devs * capacity
    put = hot(iota((total, sea_rows), 0) == place)
    chunk = 64

    def body(c, carry):
        here = pl.ds(pl.multiple_of(c * chunk, chunk), chunk)
        cols = disp_ref[here, :]
        for t in range(STEPS):
            acc = cols[:, t * np_ : t * np_ + 1] * weights_ref[0, here, :]
            for n in range(1, nodes):
                acc = acc + cols[:, t * np_ + n : t * np_ + n + 1] * weights_ref[n, here, :]
            rows_ref[t, here, :] = acc
        return carry

    lax.fori_loop(0, sea_rows // chunk, body, 0)
    twice = jnp.concatenate([put, put], axis=1)
    parts = []
    for t in range(STEPS):
        hi, lo = split(rows_ref[t])
        parts.append(mm(twice, jnp.concatenate([hi, lo], axis=0)))
    labels = jnp.broadcast_to(blocks_ref[...].astype(F32), (LANES, sea_rows)).astype(BF16)
    parts.append(mm_nt(put, labels))
    value = jnp.concatenate(parts, axis=1)
    for d in range(devs):
        pay_ref[d] = value[d * capacity : (d + 1) * capacity]


def raster_kernel(
    axis, pay_ref, b_hi_hbm, b_lo_hbm, right_hbm, left_hbm,
    uplift_ref, odd_ref, even_ref, b_hi, b_lo, right_ref, left_ref, got_ref, sem_ref,
):
    even = is_even(axis)
    later = start(
        [(b_hi_hbm, b_hi), (b_lo_hbm, b_lo), (right_hbm, right_ref), (left_hbm, left_ref)],
        sem_ref,
    )
    devs, capacity, _ = pay_ref.shape
    total = devs * capacity
    for d in range(devs):
        got_ref[d * capacity : (d + 1) * capacity] = pay_ref[d]
    tile_x, tile_y = uplift_ref.shape[1:]
    across = tile_y // BS
    cells = BS * BS
    blocks = (tile_x // BS) * across
    labels = got_ref[:, STEPS * cells :].T
    pick = hot(iota((blocks, total), 0) == labels[0:1, :].astype(jnp.int32))
    pick = jnp.concatenate([pick, pick], axis=1)
    by = iota((blocks, cells), 0) % across
    cx = iota((blocks, cells), 1) // BS
    for t in range(STEPS):
        hi, lo = split(got_ref[:, t * cells : (t + 1) * cells])
        x = mm(pick, jnp.concatenate([hi, lo], axis=0))
        step = 1
        while step < BS:
            from_above = pltpu.roll(pltpu.roll(x, blocks - step, 0), BS * step, 1)
            from_below = pltpu.roll(pltpu.roll(x, step, 0), cells - BS * step, 1)
            low_row = (by & step) == 0
            low_col = (cx & step) == 0
            x = jnp.where(low_row == low_col, x, jnp.where(low_row, from_above, from_below))
            step *= 2
        uplift_ref[t] = x
        up, down = x[tile_x - HALO_X :, :], x[:HALO_X, :]
        even_ref[t * HALO_X : (t + 1) * HALO_X] = jnp.where(even, up, down)
        odd_ref[t * HALO_X : (t + 1) * HALO_X] = jnp.where(even, down, up)
    finish(later)


def shore(axes, ext_ref, wet_ref, odd_ref, even_ref, right_ref, left_ref):
    tile_x, tile_y = wet_ref.shape
    ext_ref[4, 0:tile_x, :] = wet_ref[...].astype(F32)
    at_x = lax.axis_index(axes[0])
    has_low = at_x > 0
    has_high = at_x < lax.axis_size(axes[0]) - 1

    even = is_even(axes[0])
    low = jnp.where(even, odd_ref[...], even_ref[...])
    high = jnp.where(even, even_ref[...], odd_ref[...])

    def edge_of(edges, present, j, before):
        halves = []
        for h in range(tile_y // LANES):
            begin = h * SEA_ROWS + j * STEPS
            halves.append(edges[begin : begin + STEPS, :])
        value = jnp.where(present, jnp.concatenate(halves, axis=1), 0.0)
        blank = jnp.zeros((EDGE - STEPS, tile_y), F32)
        return jnp.concatenate([blank, value] if before else [value, blank], axis=0)

    for j in range(5):
        ext_ref[j, tile_x : tile_x + EDGE, :] = edge_of(high, has_high, j, False)
        ext_ref[j, tile_x + EDGE : tile_x + 2 * EDGE, :] = edge_of(low, has_low, j, True)
    lane = iota(right_ref.shape, 1)
    right = jnp.zeros(right_ref.shape, F32)
    left = right
    for j in range(5):
        moved = 2 * HALO_Y + 2 * j
        last = ext_ref[j, :, tile_y - LANES :]
        first = ext_ref[j, :, :LANES]
        right = jnp.where(
            lane >= LANES - moved, right, pltpu.roll(last, LANES - moved, 1)
        )
        left = jnp.where(lane < moved, left, pltpu.roll(first, moved, 1))
    right_ref[...] = right
    left_ref[...] = left


def along_x_kernel(
    axes, uplift_ref, odd_ref, even_ref, b_hi, b_lo, sea_right, sea_left,
    along_ref, odd_out, even_out,
):
    _, tile_y = uplift_ref.shape[1:]
    at_x = lax.axis_index(axes[0])
    even_x = is_even(axes[0])
    even_y = is_even(axes[1])
    has_low = at_x > 0
    has_high = at_x < lax.axis_size(axes[0]) - 1
    for t in range(STEPS):
        at = slice(t * HALO_X, (t + 1) * HALO_X)
        high = jnp.where(even_x, even_ref[at, :], odd_ref[at, :])
        low = jnp.where(even_x, odd_ref[at, :], even_ref[at, :])
        value = jnp.concatenate(
            [uplift_ref[t], jnp.where(has_high, high, 0.0), jnp.where(has_low, low, 0.0)], axis=0
        )
        hi, lo = split(value)
        along_ref[t] = mm(b_hi[...], hi) + mm(b_hi[...], lo) + mm(b_lo[...], hi)
    tall = along_ref.shape[1]
    lane = iota((tall, LANES), 1)
    last = slice(tile_y - LANES, tile_y)
    first = slice(0, LANES)
    right, left = sea_right[...], sea_left[...]
    for t in reversed(range(STEPS)):
        moved = t * HALO_Y
        tail = along_ref[t, :, last]
        head = along_ref[t, :, first]
        if t:
            tail, head = pltpu.roll(tail, LANES - moved, 1), pltpu.roll(head, moved, 1)
        right = jnp.where(lane >= LANES - moved - HALO_Y, tail, right)
        left = jnp.where(lane < moved + HALO_Y, head, left)
    even_out[...] = jnp.where(even_y, right, left)
    odd_out[...] = jnp.where(even_y, left, right)


def ocean_kernel(
    axes, along_ref, ext_ref, odd_ref, even_ref, b_hi, b_lo, out_hbm, out_ref, sem_ref
):
    tall, tile_y = along_ref.shape[1:]
    tile_x = out_ref.shape[1]
    at_y = lax.axis_index(axes[1])
    even = is_even(axes[1])
    low = jnp.where(even, odd_ref[...], even_ref[...])
    high = jnp.where(even, even_ref[...], odd_ref[...])
    low = jnp.where(at_y > 0, low, 0.0)
    high = jnp.where(at_y < lax.axis_size(axes[1]) - 1, high, 0.0)
    lane = iota((tall, LANES), 1)
    his, los = [], []
    for t in range(STEPS):
        right = pltpu.roll(high, LANES - t * HALO_Y, 1) if t else high
        left = pltpu.roll(low, t * HALO_Y, 1) if t else low
        edge = jnp.where(lane < LANES // 2, right, left)
        hi, lo = split(jnp.concatenate([along_ref[t], edge], axis=1))
        his.append(hi)
        los.append(lo)
    coarse = mm(jnp.concatenate(his + los, axis=0), b_hi[...])
    fine = mm(jnp.concatenate(his, axis=0), b_lo[...])
    forces = []
    for t in range(STEPS):
        at, more = slice(t * tall, (t + 1) * tall), slice((t + STEPS) * tall, (t + STEPS + 1) * tall)
        forces.append(coarse[at] + coarse[more] + fine[at])
    fields = []
    for j in range(5):
        moved = 2 * HALO_Y + 2 * j
        edge = jnp.where(
            lane < LANES // 2, pltpu.roll(high, LANES - moved, 1), pltpu.roll(low, moved, 1)
        )
        fields.append(jnp.concatenate([ext_ref[j], edge], axis=1))
    eta, east, north, depth, wet = fields
    rows, cols = eta.shape

    def px(x):
        return pltpu.roll(x, rows - 1, 0)

    def mx(x):
        return pltpu.roll(x, 1, 0)

    def py(x):
        return pltpu.roll(x, cols - 1, 1)

    def my(x):
        return pltpu.roll(x, 1, 1)

    factor = 0.5 * COURANT
    for t in range(STEPS):
        eta = eta + wet * forces[t]
        column = depth + eta
        qx, qy = column * east, column * north
        near = [(px(a), mx(a), py(a), my(a)) for a in (eta, east, north)]
        mean = [0.25 * (a + b + c + d) for a, b, c, d in near]
        eta_x, eta_y = near[0][0] - near[0][1], near[0][2] - near[0][3]
        east_x, east_y = near[1][0] - near[1][1], near[1][2] - near[1][3]
        north_x, north_y = near[2][0] - near[2][1], near[2][2] - near[2][3]
        eta_new = mean[0] - factor * ((px(qx) - mx(qx)) + (py(qy) - my(qy)))
        east_new = mean[1] - factor * (east * east_x + north * east_y + eta_x)
        north_new = mean[2] - factor * (east * north_x + north * north_y + eta_y)
        eta, east, north = eta_new * wet, east_new * wet, north_new * wet
    copies = []
    for j, value in enumerate((eta, east, north)):
        out_ref[j] = value[:tile_x, :tile_y]
        copies += start([(out_ref.at[j], out_hbm.at[j])], sem_ref, j)
    finish(copies)


def swap(value, axes, along, odd):
    counts = [lax.axis_size(axis) for axis in axes]
    other = 1 - along
    pairs = []
    for x in range(counts[0]):
        for y in range(counts[1]):
            at = [x, y]
            to = list(at)
            to[along] = ((at[along] - odd) ^ 1) + odd
            if not 0 <= to[along] < counts[along]:
                to = list(at)
                to[other] = at[other] ^ 1
                if to[other] >= counts[other]:
                    to = list(at)
            pairs.append((x * counts[1] + y, to[0] * counts[1] + to[1]))
    return lax.ppermute(value, axes, pairs)


def on_device(
    state, star, deriv, trace_ops, lift, face_flux, orient, neighbours, send_faces,
    sea_faces, sea_owner, sea_blocks, sea_weights, depth, wet, sea_state,
):
    variables, basis, elems = state.shape
    nodes = trace_ops.shape[2]
    np_ = pad8(nodes)
    faces = 4 * elems
    slots = send_faces.shape[-1]
    rows = -(-variables * np_ // 16) * 16
    kb = -(-basis // 16) * 16
    turns = node_turns()
    place = np.zeros((12 * np_, 4 * nodes), np.float32)
    perm = np.zeros((2 * rows, rows), np.float32)
    for r in range(3):
        for n in range(nodes):
            for f in range(4):
                place[(r * 4 + f) * np_ + n, turns[r][n] * 4 + f] = 1.0
            for v in range(variables):
                if r:
                    perm[(r - 1) * rows + v * np_ + n, v * np_ + turns[r][n]] = 1.0
    place = jnp.asarray(place, BF16)
    perm = jnp.asarray(perm, BF16)
    star = star.transpose(1, 2, 0, 3)
    face_flux = face_flux.transpose(1, 2, 0, 3)
    trace_ops = trace_ops.transpose(2, 0, 1)
    lift = lift.transpose(1, 0, 2)

    wide = (rows, faces)
    out = (rows, slots)
    tile_x, tile_y = depth.shape
    out_x = (rows + (tile_y // LANES) * SEA_ROWS, slots)
    field_shape = (variables, basis, elems)
    moved = ((variables, 3 * basis, elems), F32)
    left = ((2 * rows, faces), BF16)
    arr_left = ((2 * rows, 4 * slots), BF16)
    flux = ((variables, 4 * np_, elems), F32)
    stage = ((4 * nodes, basis), F32)

    axes = ("gx", "gy")

    def sent(outgoing):
        moved = []
        for k in (0, 1):
            for odd in (1, 0):
                moved.append(swap(outgoing[len(moved)], axes, k, odd))
        return moved

    w_of = ((3 * basis, 3 * kb), BF16)
    wt_of = ((12 * np_, 3 * kb), BF16)
    wl_of = ((2 * basis, 8 * np_), BF16)
    turn_of = ((8, faces), F32)
    slot_of = ((8, 4 * slots), F32)
    field_of, wide_of, out_of = (field_shape, F32), (wide, F32), (out, F32)
    star_of, flux_m_of = (star.shape, F32), (face_flux.shape, F32)
    lifted_of = ((np_, faces), F32)
    codes_of = (neighbours.shape, neighbours.dtype)
    perm_of = (perm.shape, BF16)

    def hbm(array):
        return (*array, HBM)

    w, wt, integ, lifted_a, *outgoing = call(
        lambda *refs: first_kernel(axes, *refs),
        [w_of, wt_of, field_of, lifted_of] + [(out_x, F32)] * 2 + [out_of] * 2,
        [star_of, (deriv.shape, F32), (trace_ops.shape, F32), (place.shape, BF16),
         (send_faces.shape, send_faces.dtype), wide_of, moved, field_of, field_of, left, stage,
         ((2, 3, EDGE, tile_y), F32), ((2, EDGE, tile_y), F32), ((2, EDGE, tile_y), wet.dtype),
         sems(16)],
        state, star, deriv, trace_ops, place, send_faces, sea_state, depth, wet,
        micros=10, held=range(9),
    )
    arrived = sent(outgoing)
    jump, base, slot_turn, wl, turn_h, slot_h, wl_h, w_h, wt_h = call(
        local_first_kernel,
        [wide_of, field_of, slot_of, wl_of, hbm(turn_of), hbm(slot_of), hbm(wl_of), hbm(w_of),
         hbm(wt_of)],
        [turn_of, wide_of, wide_of, left, moved, field_of, stage, sems(5)],
        integ, state, star, w, wt, neighbours, orient, lift,
        micros=4,
    )
    sea_rows, cells = sea_weights.shape[1:]
    devs = lax.axis_size("gx") * lax.axis_size("gy")
    capacity = max(2, (sea_rows + devs - 1) // devs)
    message = (devs, capacity, STEPS * cells + LANES)
    payload, field_h, integ_h, edge_odd, edge_even, *outgoing = call(
        lambda *refs: second_kernel(axes, capacity, nodes, *refs),
        [(message, F32), hbm(field_of), hbm(field_of)]
        + [((out_x[0] - rows, slots), F32, HBM)] * 2 + [hbm(out_of)] * 4,
        [field_of, field_of, wide_of] + [out_of] * 4
        + [arr_left, wide_of, flux, moved, field_of, field_of, left,
           ((sea_rows, LANES), F32), ((STEPS, sea_rows, cells), F32), sems(8)],
        *arrived, slot_turn, neighbours, jump, face_flux, perm, wl, base, star, w, wt,
        send_faces, lifted_a, sea_faces.reshape(1, -1), sea_owner.reshape(1, -1),
        sea_blocks.reshape(1, -1), sea_weights, micros=12,
    )
    got = lax.all_to_all(payload, ("gx", "gy"), split_axis=0, concat_axis=0, tiled=True)
    arrived = sent(outgoing)
    tall = tile_x + 2 * EDGE
    axes = ("gx", "gy")
    ext_of = ((5, tall, tile_y), F32)
    strip_of = ((tall, LANES), F32)
    edge_of = (edge_odd.shape, F32)
    ext_h, right_h, left_h, jump_h, base_h = call(
        lambda *refs: window_kernel(axes, *refs),
        [hbm(ext_of), hbm(strip_of), hbm(strip_of), hbm(wide_of), hbm(field_of)],
        [ext_of, (wet.shape, wet.dtype), edge_of, edge_of, strip_of, strip_of,
         field_of, field_of, star_of, w_of, wt_of, turn_of, codes_of, wide_of, field_of,
         wide_of, wide_of, left, moved, field_of, sems(19)],
        sea_state, depth, wet, edge_odd, edge_even,
        integ_h, field_h, star, w_h, wt_h, turn_h, neighbours,
        micros=6, held=range(12),
    )
    part, = call(
        lambda *refs: last_jump_kernel(axes, *refs), [wide_of],
        [slot_of, codes_of, wide_of, perm_of, arr_left, sems(4)],
        *arrived, slot_h, neighbours, jump_h, perm,
        micros=2, held=range(4, 8),
    )
    elastic, = call(
        last_kernel, [hbm(field_of)],
        [flux_m_of, wl_of, field_of, field_of, flux, sems(3)],
        part, face_flux, wl_h, base_h, micros=2, held=range(1, 4),
    )

    halo = ((STEPS * HALO_X, tile_y), F32)
    cell_x = np.concatenate([np.arange(tile_x + EDGE), np.arange(-EDGE, 0)])
    read_x = np.concatenate([np.arange(tile_x + HALO_X), np.arange(-HALO_X, 0)])
    cell_y = np.concatenate([np.arange(tile_y + LANES // 2), np.arange(-LANES // 2, 0)])
    read_y = cell_y
    bx = [jnp.asarray(b) for b in band(cell_x, read_x)]
    by = [jnp.asarray(b.T) for b in band(cell_y, read_y)]
    uplift, odd, even, bx_hi, bx_lo, sea_right, sea_left = call(
        lambda *refs: raster_kernel("gx", *refs),
        [((STEPS, tile_x, tile_y), F32), halo, halo]
        + [(b.shape, BF16) for b in bx] + [strip_of, strip_of],
        [((devs * capacity, message[2]), F32), sems(4)],
        got, *bx, right_h, left_h, micros=2, held=range(1, 5),
    )
    odd = swap(odd, axes, 0, 1)
    even = swap(even, axes, 0, 0)
    along, odd_y, even_y = call(
        lambda *refs: along_x_kernel(axes, *refs),
        [((STEPS, tall, tile_y), F32), strip_of, strip_of], [],
        uplift, odd, even, bx_hi, bx_lo, sea_right, sea_left, micros=1,
    )
    odd_y = swap(odd_y, axes, 1, 1)
    even_y = swap(even_y, axes, 1, 0)
    ocean_of = ((3, tile_x, tile_y), F32)
    ocean, = call(
        lambda *refs: ocean_kernel(axes, *refs), [hbm(ocean_of)], [ocean_of, sems(3)],
        along, ext_h, odd_y, even_y, *by, micros=4,
    )
    return elastic, ocean


def solution(mesh):
    both = ("gx", "gy")
    placed = (
        P(None, None, both),
        P(None, None, None, both),
        P(),
        P(),
        P(),
        P(None, None, None, both),
        P(None, both),
        P(None, both),
        P("gx", "gy", None, None),
        P(both),
        P(both, None),
        P(both),
        P(None, both, None),
        P("gx", "gy"),
        P("gx", "gy"),
        P(None, "gx", "gy"),
    )

    return jax.shard_map(
        on_device,
        mesh=mesh,
        in_specs=placed,
        out_specs=(P(None, None, both), P(None, "gx", "gy")),
        check_vma=False,
    )
```

```python
import math

import jax
import jax.numpy as jnp
import numpy as np
from jax import lax
from jax.experimental import pallas as pl
from jax.experimental.pallas import tpu as pltpu
from jax.sharding import PartitionSpec as P


ORDER = 6
STEPS = 2
BS = 16
HALF = 32
SPREAD = 8.0
COURANT = 0.25
LANES = 128
HALO_X = 40
HALO_Y = 34
EDGE = 8
SEA_ROWS = 16
F32 = jnp.float32
BF16 = jnp.bfloat16


def node_turns():
    upper = ORDER - 1
    nodes = [(i, j) for i in range(upper + 1) for j in range(upper + 1 - i)]
    once = [nodes.index((pair[1], upper - pair[0] - pair[1])) for pair in nodes]
    twice = [once[once[number]] for number in range(len(nodes))]
    return [list(range(len(nodes))), once, twice]


def pad8(n):
    return -(-n // 8) * 8


def band(out_at, in_at):
    k = np.arange(-HALF, HALF + 1)
    raw = 1.0 / np.cosh(math.pi * k / (2.0 * SPREAD))
    raw = raw / raw.sum()
    diff = in_at[None, :] - out_at[:, None]
    w = np.where(np.abs(diff) <= HALF, raw[np.clip(diff + HALF, 0, 2 * HALF)], 0.0)
    w = w.astype(np.float32)
    hi = w.astype(jnp.bfloat16)
    lo = (w - hi.astype(np.float32)).astype(jnp.bfloat16)
    return hi, lo


def split(x):
    hi = x.astype(BF16)
    lo = (x - hi.astype(F32)).astype(BF16)
    return hi, lo


def mm(a, b):
    return lax.dot_general(a, b, (((1,), (0,)), ((), ())), preferred_element_type=F32)


def mm_tn(a, b):
    return lax.dot_general(a, b, (((0,), (0,)), ((), ())), preferred_element_type=F32)


def mm_nt(a, b):
    return lax.dot_general(a, b, (((1,), (1,)), ((), ())), preferred_element_type=F32)


def iota(shape, dim):
    return lax.broadcasted_iota(jnp.int32, shape, dim)


def hot(mask):
    return jnp.where(mask, 1.0, 0.0).astype(BF16)


HBM = "hbm"


def call(body, outs, scratch, *args, micros, limit=20, held=(), flags=None):
    def spec(in_hbm):
        return pl.BlockSpec(memory_space=pltpu.HBM if in_hbm else pltpu.VMEM)

    args = [
        pltpu.with_memory_space_constraint(a, pltpu.HBM) if i in held else a
        for i, a in enumerate(args)
    ]
    return pl.pallas_call(
        body,
        in_specs=[spec(i in held) for i in range(len(args))],
        out_specs=[spec(len(o) == 3) for o in outs],
        out_shape=[(pltpu.HBM if len(o) == 3 else jax.ShapeDtypeStruct)(o[0], o[1]) for o in outs],
        scratch_shapes=[pltpu.VMEM(*x) if isinstance(x, tuple) else x for x in scratch],
        compiler_params=pltpu.CompilerParams(
            vmem_limit_bytes=limit * 2**20, **({"flags": flags} if flags else {})
        ),
        cost_estimate=pl.CostEstimate(
            flops=micros * 10**8, bytes_accessed=micros * 3 * 10**6, transcendentals=0
        ),
    )(*args)


def sems(count):
    return pltpu.SemaphoreType.DMA((count,))


def start(pairs, sem_ref, first=0):
    copies = [
        pltpu.make_async_copy(src, dst, sem_ref.at[first + i])
        for i, (src, dst) in enumerate(pairs)
    ]
    for copy in copies:
        copy.start()
    return copies


def finish(copies):
    for copy in copies:
        copy.wait()


def slots_of(basis):
    kb = -(-basis // 16) * 16
    row, col = iota((basis, 3 * kb), 0), iota((basis, 3 * kb), 1)
    return hot((col == row) | (col == kb + row)), hot(col == 2 * kb + row)


def prep_deriv(deriv_ref, w_ref):
    basis = deriv_ref.shape[1]
    sel_hi, sel_lo = slots_of(basis)
    parts = []
    for d in range(3):
        hi, lo = split(deriv_ref[d])
        parts.append(mm_tn(hi, sel_hi) + mm_tn(lo, sel_lo))
    w_ref[...] = jnp.concatenate(parts, axis=0).astype(BF16)


def staged(ref, stage_ref):
    for n in range(ref.shape[0]):
        stage_ref[n * 4 : (n + 1) * 4, :] = ref[n]
    return split(stage_ref[...])


def prep_trace(trace_ref, place_ref, stage_ref, wt_ref):
    sel_hi, sel_lo = slots_of(trace_ref.shape[2])
    hi, lo = staged(trace_ref, stage_ref)
    hi = mm(place_ref[...], hi).astype(BF16)
    lo = mm(place_ref[...], lo).astype(BF16)
    wt_ref[...] = (mm(hi, sel_hi) + mm(lo, sel_lo)).astype(BF16)


def prep_lift(lift_ref, stage_ref, wl_ref):
    nodes = lift_ref.shape[0]
    np_ = pad8(nodes)
    row, col = iota((4 * nodes, 8 * np_), 0), iota((4 * nodes, 8 * np_), 1)
    at = (row % 4) * np_ + row // 4
    sel = hot((col == at) | (col == 4 * np_ + at))
    hi, lo = staged(lift_ref, stage_ref)
    wl_ref[...] = jnp.concatenate([mm_tn(hi, sel), mm_tn(lo, sel)], axis=0).astype(BF16)


def stacked(x):
    rows = x.shape[0]
    pad = -(-rows // 16) * 16 - rows
    if pad:
        x = jnp.concatenate([x, jnp.zeros((pad, x.shape[1]), F32)], axis=0)
    hi, lo = split(x)
    return jnp.concatenate([hi, lo, hi], axis=0)


GROUP = 3


def mix(src_ref, first, w_ref, moved_ref):
    for v in range(first, first + GROUP):
        moved_ref[v] = mm(w_ref[...], stacked(src_ref[v]))


def combine(first, star_ref, moved_ref, total_ref, emit):
    variables, basis, elems = total_ref.shape
    for u0 in range(0, variables, GROUP):
        for h in range(elems // LANES):
            at = slice(h * LANES, (h + 1) * LANES)
            acc = [total_ref[u0 + i, :, at] if first else None for i in range(GROUP)]
            for v in range(first, first + GROUP):
                for d in range(3):
                    m = moved_ref[v, d * basis : (d + 1) * basis, at]
                    for i in range(GROUP):
                        part = star_ref[u0 + i, v, d : d + 1, at] * m
                        acc[i] = part if acc[i] is None else acc[i] + part
            for i in range(GROUP):
                if first + GROUP < variables:
                    total_ref[u0 + i, :, at] = acc[i]
                else:
                    emit(u0 + i, at, acc[i])


def derive(src_ref, star_ref, w_ref, moved_ref, total_ref, emit):
    variables = src_ref.shape[0]
    for first in range(0, variables, GROUP):
        if first + GROUP < variables:
            mix(src_ref, first + GROUP, w_ref, moved_ref)
        combine(first, star_ref, moved_ref, total_ref, emit)


def predict(star_ref, w_ref, moved_ref, term_ref, integ_ref, total_ref, awaited=()):
    integ_ref[...] = term_ref[...]
    mix(term_ref, 0, w_ref, moved_ref)
    finish(awaited)

    def body(k, carry):
        scale = F32(-1.0 / ORDER)
        for o in range(1, ORDER - 1):
            scale = jnp.where(k == o, F32(-1.0 / (o + 1)), scale)

        def emit(u, at, acc):
            value = acc * scale
            term_ref[u, :, at] = value
            integ_ref[u, :, at] = integ_ref[u, :, at] + value

        derive(term_ref, star_ref, w_ref, moved_ref, total_ref, emit)
        mix(term_ref, 0, w_ref, moved_ref)
        return carry

    lax.fori_loop(1, ORDER, body, 0)


def traces(integ_ref, wt_ref, own_ref, turn=None, turned_ref=None):
    variables, _, elems = integ_ref.shape
    np_ = wt_ref.shape[0] // 12
    count = 1 if turn is None else 3
    for v in range(variables):
        t = mm(wt_ref[0 : count * 4 * np_, :], stacked(integ_ref[v]))
        rows = slice(v * np_, (v + 1) * np_)
        for f in range(4):
            at = slice(f * elems, (f + 1) * elems)
            plain, *others = [
                t[(r * 4 + f) * np_ : (r * 4 + f + 1) * np_] for r in range(count)
            ]
            own_ref[rows, at] = plain
            if others:
                turned_ref[rows, at] = jnp.where(
                    turn[:, at] == 1.0,
                    others[0],
                    jnp.where(turn[:, at] == 2.0, others[1], plain),
                )
    for ref in (own_ref, turned_ref):
        if ref is not None and ref.shape[0] > variables * np_:
            ref[variables * np_ :, :] = jnp.zeros(
                (ref.shape[0] - variables * np_, 4 * elems), F32
            )


def is_even(axis):
    return lax.axis_index(axis) % 2 == 0


def send_gather(axes, own_ref, send_ref, left_ref, outs):
    rows, faces = own_ref.shape
    hi, lo = split(own_ref[...])
    left_ref[0:rows] = hi
    left_ref[rows : 2 * rows] = lo
    slots = send_ref.shape[3]
    for k, axis in enumerate(axes):
        even = is_even(axis)
        to_low = send_ref[0, 0, 2 * k : 2 * k + 1]
        to_high = send_ref[0, 0, 2 * k + 1 : 2 * k + 2]
        picks = jnp.concatenate(
            [jnp.where(even, to_low, to_high), jnp.where(even, to_high, to_low)], axis=1
        )
        res = mm(left_ref[...], hot(iota((faces, 2 * slots), 0) == picks))
        res = res[:rows] + res[rows:]
        outs[2 * k][0:rows] = res[:, :slots]
        outs[2 * k + 1][0:rows] = res[:, slots:]


def by_direction(axes, arrived):
    ordered = []
    for k, axis in enumerate(axes):
        even = is_even(axis)
        odd_one, even_one = arrived[2 * k], arrived[2 * k + 1]
        ordered += [jnp.where(even, odd_one, even_one), jnp.where(even, even_one, odd_one)]
    return ordered


def row_of(ref):
    return jnp.concatenate([ref[f : f + 1, :] for f in range(ref.shape[0])], axis=1)


def local_jump(own_ref, turned_ref, codes, left_ref, jump_ref):
    rows, faces = own_ref.shape
    width = faces // 4
    hi, lo = split(turned_ref[...])
    left_ref[0:rows] = hi
    left_ref[rows : 2 * rows] = lo
    for q in range(4):
        at = slice(q * width, (q + 1) * width)
        res = mm(left_ref[...], hot(iota((faces, width), 0) == codes[:, at]))
        jump_ref[:, at] = own_ref[:, at] - (res[:rows] + res[rows:])


def full_jump(arrived, slot_turn, codes, jump_ref, perm_ref, left_ref, part_ref):
    rows, faces = jump_ref.shape
    elems = faces // 4
    value = jnp.concatenate(arrived, axis=1)
    slots = value.shape[1]
    hi, lo = split(value)
    both = jnp.concatenate([hi, lo], axis=1)
    turned = mm(perm_ref[...], both)
    turn = jnp.concatenate([slot_turn, slot_turn], axis=1)
    chosen = jnp.where(
        turn == 1.0, turned[:rows], jnp.where(turn == 2.0, turned[rows:], both.astype(F32))
    ).astype(BF16)
    left_ref[0:rows] = chosen[:, :slots]
    left_ref[rows : 2 * rows] = chosen[:, slots:]
    for q in range(4):
        at = slice(q * elems, (q + 1) * elems)
        res = mm(left_ref[...], hot(iota((slots, elems), 0) + faces == codes[:, at]))
        part_ref[:, at] = jump_ref[:, at] - (res[:rows] + res[rows:])


def correct(part_ref, flux_m_ref, wl_ref, base_ref, flux_ref, out_ref):
    variables, basis, elems = base_ref.shape
    np_ = flux_ref.shape[1] // 4

    group = 3

    def body(g, carry):
        for f in range(4):
            for h in range(elems // LANES):
                here = slice(h * LANES, (h + 1) * LANES)
                wide = slice(f * elems + h * LANES, f * elems + (h + 1) * LANES)
                acc = [jnp.zeros((np_, LANES), F32) for _ in range(group)]
                for v in range(variables):
                    jump = part_ref[v * np_ : (v + 1) * np_, wide]
                    for i in range(group):
                        acc[i] = acc[i] + flux_m_ref[g * group + i, v, f : f + 1, here] * jump
                for i in range(group):
                    flux_ref[g * group + i, f * np_ : (f + 1) * np_, here] = acc[i]
        return carry

    lax.fori_loop(0, variables // group, body, 0)
    for u in range(variables):
        hi, lo = split(flux_ref[u])
        res = mm(wl_ref[...], jnp.concatenate([hi, lo], axis=0))
        out_ref[u] = base_ref[u] - (res[:basis] + res[basis:])


def first_kernel(
    axes,
    state_hbm, star_hbm, deriv_hbm, trace_hbm, place_hbm, send_hbm, sea_hbm, depth_hbm, wet_hbm,
    w_ref, wt_ref, integ_ref, lifted_ref, o0, o1, o2, o3,
    star_ref, deriv_ref, trace_ref, place_ref, send_ref, own_ref,
    moved_ref, term_ref, total_ref, left_ref, stage_ref, sea_edge, depth_edge, wet_edge, sem_ref,
):
    urgent = start(
        [(deriv_hbm, deriv_ref), (state_hbm, term_ref), (star_hbm, star_ref)], sem_ref
    )
    later = start(
        [(trace_hbm, trace_ref), (place_hbm, place_ref), (send_hbm, send_ref)], sem_ref, 3
    )
    tall = depth_hbm.shape[0]
    pairs = []
    for side, at in enumerate((pl.ds(0, EDGE), pl.ds(tall - EDGE, EDGE))):
        for j in range(3):
            pairs.append((sea_hbm.at[j, at], sea_edge.at[side, j]))
        pairs.append((depth_hbm.at[at], depth_edge.at[side]))
        pairs.append((wet_hbm.at[at], wet_edge.at[side]))
    later = later + start(pairs, sem_ref, 6)
    finish(urgent[:1])
    prep_deriv(deriv_ref, w_ref)
    finish(urgent[1:2])
    predict(star_ref, w_ref, moved_ref, term_ref, integ_ref, total_ref, urgent[2:])
    finish(later)
    prep_trace(trace_ref, place_ref, stage_ref, wt_ref)
    traces(integ_ref, wt_ref, own_ref)
    send_gather(axes, own_ref, send_ref, left_ref, (o0, o1, o2, o3))
    rows = own_ref.shape[0]
    np_ = lifted_ref.shape[0]
    lifted_ref[...] = own_ref[2 * np_ : 3 * np_, :]
    even = is_even(axes[0])
    for j in range(5):
        if j < 3:
            low, high = sea_edge[0, j], sea_edge[1, j]
        else:
            ref = depth_edge if j == 3 else wet_edge
            low, high = ref[0].astype(F32), ref[1].astype(F32)
        low, high = low[:STEPS], high[EDGE - STEPS :]
        for out, edge in ((o0, jnp.where(even, low, high)), (o1, jnp.where(even, high, low))):
            for h in range(edge.shape[1] // LANES):
                begin = rows + h * SEA_ROWS + j * STEPS
                out[begin : begin + STEPS] = edge[:, h * LANES : (h + 1) * LANES]


def own_derivative(integ_ref, field_ref, star_ref, w_ref, base_ref, moved_ref, total_ref):
    def emit(u, at, acc):
        base_ref[u, :, at] = field_ref[u, :, at] - acc

    mix(integ_ref, 0, w_ref, moved_ref)
    derive(integ_ref, star_ref, w_ref, moved_ref, total_ref, emit)


def local_first_kernel(
    integ_ref, field_ref, star_ref, w_ref, wt_ref, codes_ref, orient_ref, lift_ref,
    jump_ref, base_ref, slot_ref, wl_ref, turn_out, slot_out, wl_out, w_out, wt_out,
    turn_ref, own_ref, turned_ref, left_ref, moved_ref, total_ref, stage_ref, sem_ref,
):
    prep_lift(lift_ref, stage_ref, wl_ref)
    codes = row_of(codes_ref)
    faces = codes.shape[1]
    slots = slot_ref.shape[1]
    turns = jnp.broadcast_to(row_of(orient_ref).astype(F32), (16, faces)).astype(BF16)
    width = faces // 4
    for q in range(4):
        at = slice(q * width, (q + 1) * width)
        turn_ref[:, at] = mm(turns, hot(iota((faces, width), 0) == codes[:, at]))[0:8]
    for q in range(slots // LANES):
        at = slice(q * LANES, (q + 1) * LANES)
        wanted = iota((LANES, faces), 0) + (faces + q * LANES)
        slot_ref[:, at] = mm_nt(turns, hot(wanted == codes))[0:8]
    copies = start(
        [(turn_ref, turn_out), (slot_ref, slot_out), (wl_ref, wl_out), (w_ref, w_out),
         (wt_ref, wt_out)], sem_ref,
    )
    traces(integ_ref, wt_ref, own_ref, turn_ref[0:1, :], turned_ref)
    local_jump(own_ref, turned_ref, codes, left_ref, jump_ref)
    own_derivative(integ_ref, field_ref, star_ref, w_ref, base_ref, moved_ref, total_ref)
    finish(copies)


def second_kernel(
    axes, capacity, nodes,
    a0, a1, a2, a3, slot_ref, codes_ref, jump_ref, flux_m_ref, perm_ref, wl_ref, base_ref,
    star_ref, w_ref, wt_ref, send_ref, lifted_ref, faces_ref, owner_ref, blocks_ref, weights_ref,
    pay_ref, field_out, integ_out, edge_odd, edge_even, s0, s1, s2, s3,
    field_ref, integ_ref, own_ref, o0, o1, o2, o3,
    arr_left_ref, part_ref, flux_ref, moved_ref, term_ref, total_ref, left_ref,
    disp_ref, rows_ref, sem_ref,
):
    rows = jump_ref.shape[0]
    tail = pl.ds(rows, a0.shape[0] - rows)
    copies = start([(a0.at[tail], edge_odd), (a1.at[tail], edge_even)], sem_ref)
    full_jump(
        by_direction(axes, [a[0:rows] for a in (a0, a1, a2, a3)]), slot_ref[0:1, :], row_of(codes_ref), jump_ref,
        perm_ref, arr_left_ref, part_ref,
    )
    correct(part_ref, flux_m_ref, wl_ref, base_ref, flux_ref, field_ref)
    copies += start([(field_ref, field_out)], sem_ref, 2)
    term_ref[...] = field_ref[...]
    predict(star_ref, w_ref, moved_ref, term_ref, integ_ref, total_ref)
    copies += start([(integ_ref, integ_out)], sem_ref, 3)
    traces(integ_ref, wt_ref, own_ref)
    send_gather(axes, own_ref, send_ref, left_ref, (o0, o1, o2, o3))
    copies += start([(o0, s0), (o1, s1), (o2, s2), (o3, s3)], sem_ref, 4)
    np_ = lifted_ref.shape[0]
    project(
        capacity, nodes, lifted_ref[...], own_ref[2 * np_ : 3 * np_, :], faces_ref, owner_ref,
        blocks_ref, weights_ref, pay_ref, disp_ref, rows_ref,
    )
    finish(copies)


def window_kernel(
    axes,
    sea_hbm, depth_hbm, wet_hbm, low_hbm, high_hbm,
    integ_hbm, field_hbm, star_hbm, w_hbm, wt_hbm, turn_hbm, codes_hbm,
    ext_out, right_out, left_out, jump_out, base_out,
    ext_ref, wet_ref, low_ref, high_ref, right_ref, left_ref,
    integ_ref, field_ref, star_ref, w_ref, wt_ref, turn_ref, codes_ref, jump_ref, base_ref,
    own_ref, turned_ref, left_rows, moved_ref, total_ref, sem_ref,
):
    copies = start(
        [(wt_hbm, wt_ref), (integ_hbm, integ_ref), (turn_hbm, turn_ref), (codes_hbm, codes_ref),
         (w_hbm, w_ref), (star_hbm, star_ref), (field_hbm, field_ref)], sem_ref,
    )
    body = pl.ds(0, depth_hbm.shape[0])
    sea = start(
        [(sea_hbm.at[j], ext_ref.at[j, body]) for j in range(3)]
        + [(depth_hbm, ext_ref.at[3, body]), (wet_hbm, wet_ref), (low_hbm, low_ref),
           (high_hbm, high_ref)], sem_ref, 7,
    )
    finish(copies[:3])
    traces(integ_ref, wt_ref, own_ref, turn_ref[0:1, :], turned_ref)
    finish(copies[3:4])
    local_jump(own_ref, turned_ref, row_of(codes_ref), left_rows, jump_ref)
    written = start([(jump_ref, jump_out)], sem_ref, 14)
    finish(copies[4:])
    own_derivative(integ_ref, field_ref, star_ref, w_ref, base_ref, moved_ref, total_ref)
    written += start([(base_ref, base_out)], sem_ref, 15)
    finish(sea)
    shore(axes, ext_ref, wet_ref, low_ref, high_ref, right_ref, left_ref)
    written += start(
        [(ext_ref, ext_out), (right_ref, right_out), (left_ref, left_out)], sem_ref, 16
    )
    finish(written)


def last_jump_kernel(
    axes,
    a0, a1, a2, a3, slot_hbm, codes_hbm, jump_hbm, perm_hbm,
    part_ref, slot_ref, codes_ref, jump_ref, perm_ref, arr_left_ref, sem_ref,
):
    finish(
        start(
            [(slot_hbm, slot_ref), (perm_hbm, perm_ref), (codes_hbm, codes_ref),
             (jump_hbm, jump_ref)], sem_ref,
        )
    )
    full_jump(
        by_direction(axes, [a0[...], a1[...], a2[...], a3[...]]), slot_ref[0:1, :], row_of(codes_ref), jump_ref,
        perm_ref, arr_left_ref, part_ref,
    )


def last_kernel(
    part_ref, flux_m_hbm, wl_hbm, base_hbm, field_out,
    flux_m_ref, wl_ref, base_ref, field_ref, flux_ref, sem_ref,
):
    copies = start([(flux_m_hbm, flux_m_ref), (wl_hbm, wl_ref), (base_hbm, base_ref)], sem_ref)
    finish(copies)
    correct(part_ref, flux_m_ref, wl_ref, base_ref, flux_ref, field_ref)
    finish(start([(field_ref, field_out)], sem_ref))


def project(
    capacity, nodes, own_a, own_b, faces_ref, owner_ref, blocks_ref, weights_ref, pay_ref,
    disp_ref, rows_ref,
):
    np_ = pad8(nodes)
    faces = own_a.shape[1]
    sea_rows, _ = weights_ref.shape[1:]
    both = jnp.concatenate([own_a, own_b], axis=0)
    hi, lo = split(both)
    picks = hot(iota((faces, sea_rows), 0) == faces_ref[...])
    disp = mm(jnp.concatenate([hi, lo], axis=0), picks)
    disp = disp[: 2 * np_] + disp[2 * np_ :]
    disp = jnp.concatenate([disp, jnp.zeros((LANES - 2 * np_, sea_rows), F32)], axis=0)
    disp_ref[...] = disp.T
    across = jnp.broadcast_to(owner_ref[...].astype(F32), (sea_rows, sea_rows))
    owner = across.T
    earlier = iota((sea_rows, sea_rows), 0) < iota((sea_rows, sea_rows), 1)
    rank = jnp.sum(jnp.where((owner == across) & earlier, 1.0, 0.0), axis=0, keepdims=True)
    place = (across[0:1, :] * float(capacity) + rank).astype(jnp.int32)
    devs = pay_ref.shape[0]
    total = devs * capacity
    put = hot(iota((total, sea_rows), 0) == place)
    chunk = 64

    def body(c, carry):
        here = pl.ds(pl.multiple_of(c * chunk, chunk), chunk)
        cols = disp_ref[here, :]
        for t in range(STEPS):
            acc = cols[:, t * np_ : t * np_ + 1] * weights_ref[0, here, :]
            for n in range(1, nodes):
                acc = acc + cols[:, t * np_ + n : t * np_ + n + 1] * weights_ref[n, here, :]
            rows_ref[t, here, :] = acc
        return carry

    lax.fori_loop(0, sea_rows // chunk, body, 0)
    twice = jnp.concatenate([put, put], axis=1)
    parts = []
    for t in range(STEPS):
        hi, lo = split(rows_ref[t])
        parts.append(mm(twice, jnp.concatenate([hi, lo], axis=0)))
    labels = jnp.broadcast_to(blocks_ref[...].astype(F32), (LANES, sea_rows)).astype(BF16)
    parts.append(mm_nt(put, labels))
    value = jnp.concatenate(parts, axis=1)
    for d in range(devs):
        pay_ref[d] = value[d * capacity : (d + 1) * capacity]


def raster_kernel(
    axis, pay_ref, b_hi_hbm, b_lo_hbm, right_hbm, left_hbm,
    uplift_ref, odd_ref, even_ref, b_hi, b_lo, right_ref, left_ref, got_ref, sem_ref,
):
    even = is_even(axis)
    later = start(
        [(b_hi_hbm, b_hi), (b_lo_hbm, b_lo), (right_hbm, right_ref), (left_hbm, left_ref)],
        sem_ref,
    )
    devs, capacity, _ = pay_ref.shape
    total = devs * capacity
    for d in range(devs):
        got_ref[d * capacity : (d + 1) * capacity] = pay_ref[d]
    tile_x, tile_y = uplift_ref.shape[1:]
    across = tile_y // BS
    cells = BS * BS
    blocks = (tile_x // BS) * across
    labels = got_ref[:, STEPS * cells :].T
    pick = hot(iota((blocks, total), 0) == labels[0:1, :].astype(jnp.int32))
    pick = jnp.concatenate([pick, pick], axis=1)
    by = iota((blocks, cells), 0) % across
    cx = iota((blocks, cells), 1) // BS
    for t in range(STEPS):
        hi, lo = split(got_ref[:, t * cells : (t + 1) * cells])
        x = mm(pick, jnp.concatenate([hi, lo], axis=0))
        step = 1
        while step < BS:
            from_above = pltpu.roll(pltpu.roll(x, blocks - step, 0), BS * step, 1)
            from_below = pltpu.roll(pltpu.roll(x, step, 0), cells - BS * step, 1)
            low_row = (by & step) == 0
            low_col = (cx & step) == 0
            x = jnp.where(low_row == low_col, x, jnp.where(low_row, from_above, from_below))
            step *= 2
        uplift_ref[t] = x
        up, down = x[tile_x - HALO_X :, :], x[:HALO_X, :]
        even_ref[t * HALO_X : (t + 1) * HALO_X] = jnp.where(even, up, down)
        odd_ref[t * HALO_X : (t + 1) * HALO_X] = jnp.where(even, down, up)
    finish(later)


def shore(axes, ext_ref, wet_ref, odd_ref, even_ref, right_ref, left_ref):
    tile_x, tile_y = wet_ref.shape
    ext_ref[4, 0:tile_x, :] = wet_ref[...].astype(F32)
    at_x = lax.axis_index(axes[0])
    has_low = at_x > 0
    has_high = at_x < lax.axis_size(axes[0]) - 1

    even = is_even(axes[0])
    low = jnp.where(even, odd_ref[...], even_ref[...])
    high = jnp.where(even, even_ref[...], odd_ref[...])

    def edge_of(edges, present, j, before):
        halves = []
        for h in range(tile_y // LANES):
            begin = h * SEA_ROWS + j * STEPS
            halves.append(edges[begin : begin + STEPS, :])
        value = jnp.where(present, jnp.concatenate(halves, axis=1), 0.0)
        blank = jnp.zeros((EDGE - STEPS, tile_y), F32)
        return jnp.concatenate([blank, value] if before else [value, blank], axis=0)

    for j in range(5):
        ext_ref[j, tile_x : tile_x + EDGE, :] = edge_of(high, has_high, j, False)
        ext_ref[j, tile_x + EDGE : tile_x + 2 * EDGE, :] = edge_of(low, has_low, j, True)
    lane = iota(right_ref.shape, 1)
    right = jnp.zeros(right_ref.shape, F32)
    left = right
    for j in range(5):
        moved = 2 * HALO_Y + 2 * j
        last = ext_ref[j, :, tile_y - LANES :]
        first = ext_ref[j, :, :LANES]
        right = jnp.where(
            lane >= LANES - moved, right, pltpu.roll(last, LANES - moved, 1)
        )
        left = jnp.where(lane < moved, left, pltpu.roll(first, moved, 1))
    right_ref[...] = right
    left_ref[...] = left


def along_x_kernel(
    axes, uplift_ref, odd_ref, even_ref, b_hi, b_lo, sea_right, sea_left,
    along_ref, odd_out, even_out,
):
    _, tile_y = uplift_ref.shape[1:]
    at_x = lax.axis_index(axes[0])
    even_x = is_even(axes[0])
    even_y = is_even(axes[1])
    has_low = at_x > 0
    has_high = at_x < lax.axis_size(axes[0]) - 1
    for t in range(STEPS):
        at = slice(t * HALO_X, (t + 1) * HALO_X)
        high = jnp.where(even_x, even_ref[at, :], odd_ref[at, :])
        low = jnp.where(even_x, odd_ref[at, :], even_ref[at, :])
        value = jnp.concatenate(
            [uplift_ref[t], jnp.where(has_high, high, 0.0), jnp.where(has_low, low, 0.0)], axis=0
        )
        hi, lo = split(value)
        along_ref[t] = mm(b_hi[...], hi) + mm(b_hi[...], lo) + mm(b_lo[...], hi)
    tall = along_ref.shape[1]
    lane = iota((tall, LANES), 1)
    last = slice(tile_y - LANES, tile_y)
    first = slice(0, LANES)
    right, left = sea_right[...], sea_left[...]
    for t in reversed(range(STEPS)):
        moved = t * HALO_Y
        tail = along_ref[t, :, last]
        head = along_ref[t, :, first]
        if t:
            tail, head = pltpu.roll(tail, LANES - moved, 1), pltpu.roll(head, moved, 1)
        right = jnp.where(lane >= LANES - moved - HALO_Y, tail, right)
        left = jnp.where(lane < moved + HALO_Y, head, left)
    even_out[...] = jnp.where(even_y, right, left)
    odd_out[...] = jnp.where(even_y, left, right)


def ocean_kernel(
    axes, along_ref, ext_ref, odd_ref, even_ref, b_hi, b_lo, out_hbm, out_ref, sem_ref
):
    tall, tile_y = along_ref.shape[1:]
    tile_x = out_ref.shape[1]
    at_y = lax.axis_index(axes[1])
    even = is_even(axes[1])
    low = jnp.where(even, odd_ref[...], even_ref[...])
    high = jnp.where(even, even_ref[...], odd_ref[...])
    low = jnp.where(at_y > 0, low, 0.0)
    high = jnp.where(at_y < lax.axis_size(axes[1]) - 1, high, 0.0)
    lane = iota((tall, LANES), 1)
    his, los = [], []
    for t in range(STEPS):
        right = pltpu.roll(high, LANES - t * HALO_Y, 1) if t else high
        left = pltpu.roll(low, t * HALO_Y, 1) if t else low
        edge = jnp.where(lane < LANES // 2, right, left)
        hi, lo = split(jnp.concatenate([along_ref[t], edge], axis=1))
        his.append(hi)
        los.append(lo)
    coarse = mm(jnp.concatenate(his + los, axis=0), b_hi[...])
    fine = mm(jnp.concatenate(his, axis=0), b_lo[...])
    forces = []
    for t in range(STEPS):
        at, more = slice(t * tall, (t + 1) * tall), slice((t + STEPS) * tall, (t + STEPS + 1) * tall)
        forces.append(coarse[at] + coarse[more] + fine[at])
    fields = []
    for j in range(5):
        moved = 2 * HALO_Y + 2 * j
        edge = jnp.where(
            lane < LANES // 2, pltpu.roll(high, LANES - moved, 1), pltpu.roll(low, moved, 1)
        )
        fields.append(jnp.concatenate([ext_ref[j], edge], axis=1))
    eta, east, north, depth, wet = fields
    rows, cols = eta.shape

    def px(x):
        return pltpu.roll(x, rows - 1, 0)

    def mx(x):
        return pltpu.roll(x, 1, 0)

    def py(x):
        return pltpu.roll(x, cols - 1, 1)

    def my(x):
        return pltpu.roll(x, 1, 1)

    factor = 0.5 * COURANT
    for t in range(STEPS):
        eta = eta + wet * forces[t]
        column = depth + eta
        qx, qy = column * east, column * north
        near = [(px(a), mx(a), py(a), my(a)) for a in (eta, east, north)]
        mean = [0.25 * (a + b + c + d) for a, b, c, d in near]
        eta_x, eta_y = near[0][0] - near[0][1], near[0][2] - near[0][3]
        east_x, east_y = near[1][0] - near[1][1], near[1][2] - near[1][3]
        north_x, north_y = near[2][0] - near[2][1], near[2][2] - near[2][3]
        eta_new = mean[0] - factor * ((px(qx) - mx(qx)) + (py(qy) - my(qy)))
        east_new = mean[1] - factor * (east * east_x + north * east_y + eta_x)
        north_new = mean[2] - factor * (east * north_x + north * north_y + eta_y)
        eta, east, north = eta_new * wet, east_new * wet, north_new * wet
    copies = []
    for j, value in enumerate((eta, east, north)):
        out_ref[j] = value[:tile_x, :tile_y]
        copies += start([(out_ref.at[j], out_hbm.at[j])], sem_ref, j)
    finish(copies)


def swap(value, axes, along, odd):
    counts = [lax.axis_size(axis) for axis in axes]
    other = 1 - along
    pairs = []
    for x in range(counts[0]):
        for y in range(counts[1]):
            at = [x, y]
            to = list(at)
            to[along] = ((at[along] - odd) ^ 1) + odd
            if not 0 <= to[along] < counts[along]:
                to = list(at)
                to[other] = at[other] ^ 1
                if to[other] >= counts[other]:
                    to = list(at)
            pairs.append((x * counts[1] + y, to[0] * counts[1] + to[1]))
    return lax.ppermute(value, axes, pairs)


def on_device(
    state, star, deriv, trace_ops, lift, face_flux, orient, neighbours, send_faces,
    sea_faces, sea_owner, sea_blocks, sea_weights, depth, wet, sea_state,
):
    variables, basis, elems = state.shape
    nodes = trace_ops.shape[2]
    np_ = pad8(nodes)
    faces = 4 * elems
    slots = send_faces.shape[-1]
    rows = -(-variables * np_ // 16) * 16
    kb = -(-basis // 16) * 16
    turns = node_turns()
    place = np.zeros((12 * np_, 4 * nodes), np.float32)
    perm = np.zeros((2 * rows, rows), np.float32)
    for r in range(3):
        for n in range(nodes):
            for f in range(4):
                place[(r * 4 + f) * np_ + n, turns[r][n] * 4 + f] = 1.0
            for v in range(variables):
                if r:
                    perm[(r - 1) * rows + v * np_ + n, v * np_ + turns[r][n]] = 1.0
    place = jnp.asarray(place, BF16)
    perm = jnp.asarray(perm, BF16)
    star = star.transpose(1, 2, 0, 3)
    face_flux = face_flux.transpose(1, 2, 0, 3)
    trace_ops = trace_ops.transpose(2, 0, 1)
    lift = lift.transpose(1, 0, 2)

    wide = (rows, faces)
    out = (rows, slots)
    tile_x, tile_y = depth.shape
    out_x = (rows + (tile_y // LANES) * SEA_ROWS, slots)
    field_shape = (variables, basis, elems)
    moved = ((variables, 3 * basis, elems), F32)
    left = ((2 * rows, faces), BF16)
    arr_left = ((2 * rows, 4 * slots), BF16)
    flux = ((variables, 4 * np_, elems), F32)
    stage = ((4 * nodes, basis), F32)

    axes = ("gx", "gy")

    def sent(outgoing):
        moved = []
        for k in (0, 1):
            for odd in (1, 0):
                moved.append(swap(outgoing[len(moved)], axes, k, odd))
        return moved

    w_of = ((3 * basis, 3 * kb), BF16)
    wt_of = ((12 * np_, 3 * kb), BF16)
    wl_of = ((2 * basis, 8 * np_), BF16)
    turn_of = ((8, faces), F32)
    slot_of = ((8, 4 * slots), F32)
    field_of, wide_of, out_of = (field_shape, F32), (wide, F32), (out, F32)
    star_of, flux_m_of = (star.shape, F32), (face_flux.shape, F32)
    lifted_of = ((np_, faces), F32)
    codes_of = (neighbours.shape, neighbours.dtype)
    perm_of = (perm.shape, BF16)

    def hbm(array):
        return (*array, HBM)

    w, wt, integ, lifted_a, *outgoing = call(
        lambda *refs: first_kernel(axes, *refs),
        [w_of, wt_of, field_of, lifted_of] + [(out_x, F32)] * 2 + [out_of] * 2,
        [star_of, (deriv.shape, F32), (trace_ops.shape, F32), (place.shape, BF16),
         (send_faces.shape, send_faces.dtype), wide_of, moved, field_of, field_of, left, stage,
         ((2, 3, EDGE, tile_y), F32), ((2, EDGE, tile_y), F32), ((2, EDGE, tile_y), wet.dtype),
         sems(16)],
        state, star, deriv, trace_ops, place, send_faces, sea_state, depth, wet,
        micros=10, held=range(9),
    )
    arrived = sent(outgoing)
    jump, base, slot_turn, wl, turn_h, slot_h, wl_h, w_h, wt_h = call(
        local_first_kernel,
        [wide_of, field_of, slot_of, wl_of, hbm(turn_of), hbm(slot_of), hbm(wl_of), hbm(w_of),
         hbm(wt_of)],
        [turn_of, wide_of, wide_of, left, moved, field_of, stage, sems(5)],
        integ, state, star, w, wt, neighbours, orient, lift,
        micros=4,
    )
    sea_rows, cells = sea_weights.shape[1:]
    devs = lax.axis_size("gx") * lax.axis_size("gy")
    capacity = max(2, (sea_rows + devs - 1) // devs)
    message = (devs, capacity, STEPS * cells + LANES)
    payload, field_h, integ_h, edge_odd, edge_even, *outgoing = call(
        lambda *refs: second_kernel(axes, capacity, nodes, *refs),
        [(message, F32), hbm(field_of), hbm(field_of)]
        + [((out_x[0] - rows, slots), F32, HBM)] * 2 + [hbm(out_of)] * 4,
        [field_of, field_of, wide_of] + [out_of] * 4
        + [arr_left, wide_of, flux, moved, field_of, field_of, left,
           ((sea_rows, LANES), F32), ((STEPS, sea_rows, cells), F32), sems(8)],
        *arrived, slot_turn, neighbours, jump, face_flux, perm, wl, base, star, w, wt,
        send_faces, lifted_a, sea_faces.reshape(1, -1), sea_owner.reshape(1, -1),
        sea_blocks.reshape(1, -1), sea_weights, micros=12,
    )
    got = lax.all_to_all(payload, ("gx", "gy"), split_axis=0, concat_axis=0, tiled=True)
    arrived = sent(outgoing)
    tall = tile_x + 2 * EDGE
    axes = ("gx", "gy")
    ext_of = ((5, tall, tile_y), F32)
    strip_of = ((tall, LANES), F32)
    edge_of = (edge_odd.shape, F32)
    ext_h, right_h, left_h, jump_h, base_h = call(
        lambda *refs: window_kernel(axes, *refs),
        [hbm(ext_of), hbm(strip_of), hbm(strip_of), hbm(wide_of), hbm(field_of)],
        [ext_of, (wet.shape, wet.dtype), edge_of, edge_of, strip_of, strip_of,
         field_of, field_of, star_of, w_of, wt_of, turn_of, codes_of, wide_of, field_of,
         wide_of, wide_of, left, moved, field_of, sems(19)],
        sea_state, depth, wet, edge_odd, edge_even,
        integ_h, field_h, star, w_h, wt_h, turn_h, neighbours,
        micros=6, held=range(12),
    )
    part, = call(
        lambda *refs: last_jump_kernel(axes, *refs), [wide_of],
        [slot_of, codes_of, wide_of, perm_of, arr_left, sems(4)],
        *arrived, slot_h, neighbours, jump_h, perm,
        micros=2, held=range(4, 8),
    )
    elastic, = call(
        last_kernel, [hbm(field_of)],
        [flux_m_of, wl_of, field_of, field_of, flux, sems(3)],
        part, face_flux, wl_h, base_h, micros=2, held=range(1, 4),
    )

    halo = ((STEPS * HALO_X, tile_y), F32)
    cell_x = np.concatenate([np.arange(tile_x + EDGE), np.arange(-EDGE, 0)])
    read_x = np.concatenate([np.arange(tile_x + HALO_X), np.arange(-HALO_X, 0)])
    cell_y = np.concatenate([np.arange(tile_y + LANES // 2), np.arange(-LANES // 2, 0)])
    read_y = cell_y
    bx = [jnp.asarray(b) for b in band(cell_x, read_x)]
    by = [jnp.asarray(b.T) for b in band(cell_y, read_y)]
    uplift, odd, even, bx_hi, bx_lo, sea_right, sea_left = call(
        lambda *refs: raster_kernel("gx", *refs),
        [((STEPS, tile_x, tile_y), F32), halo, halo]
        + [(b.shape, BF16) for b in bx] + [strip_of, strip_of],
        [((devs * capacity, message[2]), F32), sems(4)],
        got, *bx, right_h, left_h, micros=2, held=range(1, 5),
    )
    odd = swap(odd, axes, 0, 1)
    even = swap(even, axes, 0, 0)
    along, odd_y, even_y = call(
        lambda *refs: along_x_kernel(axes, *refs),
        [((STEPS, tall, tile_y), F32), strip_of, strip_of], [],
        uplift, odd, even, bx_hi, bx_lo, sea_right, sea_left, micros=1,
    )
    odd_y = swap(odd_y, axes, 1, 1)
    even_y = swap(even_y, axes, 1, 0)
    ocean_of = ((3, tile_x, tile_y), F32)
    ocean, = call(
        lambda *refs: ocean_kernel(axes, *refs), [hbm(ocean_of)], [ocean_of, sems(3)],
        along, ext_h, odd_y, even_y, *by, micros=4,
    )
    return elastic, ocean


def solution(mesh):
    both = ("gx", "gy")
    placed = (
        P(None, None, both),
        P(None, None, None, both),
        P(),
        P(),
        P(),
        P(None, None, None, both),
        P(None, both),
        P(None, both),
        P("gx", "gy", None, None),
        P(both),
        P(both, None),
        P(both),
        P(None, both, None),
        P("gx", "gy"),
        P("gx", "gy"),
        P(None, "gx", "gy"),
    )

    return jax.shard_map(
        on_device,
        mesh=mesh,
        in_specs=placed,
        out_specs=(P(None, None, both), P(None, "gx", "gy")),
        check_vma=False,
    )
```
